32 devices in a mesh: dp: 16 (over z, y, x), head: 2 (over core).
Axes of the slice: x: 2, y: 2, z: 4, core: 2. Of those that a mesh axis runs over, the one named last changes fastest.
Arguments:
- rows_in: bfloat16 [32, 1024, 128], P(('dp', 'head')), may hold values from -6 to 6
- feat_mask: int32 [32, 128], P(('dp', 'head')), may hold values 0 or 1
- counts: int32 [32], replicated, may hold values from 64 to 768, as said below
- ctx_vals: float32 [32, 768], P(('dp', 'head')), may hold values from -6 to 6
- targets: int32 [32, 256], P(('dp', 'head')), may hold values from 0 to 511
- query_mask: int32 [32, 256], P(('dp', 'head')), may hold values from 0 to 1, as said below
- w_emb: float32 [128, 768], replicated, may hold values from -0.5 to 0.5
- m_emb: float32 [128, 768], replicated, may hold values from -1.5258789e-05 to 1.5258789e-05
- a_emb: float32 [128, 768], replicated, may hold values from -0.5 to 0.5
- vectors: float32 [16, 768], replicated
- m_vec: float32 [16, 768], replicated, may hold values from -1.5258789e-05 to 1.5258789e-05
- a_vec: float32 [16, 768], replicated
- w_qkv: float32 [2, 768, 3, 2, 384], P(None, 'dp', None, 'head'), may hold values from -0.21875 to 0.21875
- m_qkv: float32 [2, 768, 3, 2, 384], P(None, 'dp', None, 'head'), may hold values from -1.5258789e-05 to 1.5258789e-05
- a_qkv: float32 [2, 768, 3, 2, 384], P(None, 'dp', None, 'head'), may hold values from -0.21875 to 0.21875
- w_out: float32 [2, 2, 384, 768], P(None, 'head', 'dp'), may hold values from -0.875 to 0.875
- m_out: float32 [2, 2, 384, 768], P(None, 'head', 'dp'), may hold values from -1.5258789e-05 to 1.5258789e-05
- a_out: float32 [2, 2, 384, 768], P(None, 'head', 'dp'), may hold values from -0.875 to 0.875
- w_up: float32 [2, 768, 3072], P(None, ('dp', 'head')), may hold values from -0.21875 to 0.21875
- m_up: float32 [2, 768, 3072], P(None, ('dp', 'head')), may hold values from -1.5258789e-05 to 1.5258789e-05
- a_up: float32 [2, 768, 3072], P(None, ('dp', 'head')), may hold values from -0.21875 to 0.21875
- w_down: float32 [2, 3072, 768], P(None, ('dp', 'head')), may hold values from -0.109375 to 0.109375
- m_down: float32 [2, 3072, 768], P(None, ('dp', 'head')), may hold values from -1.5258789e-05 to 1.5258789e-05
- a_down: float32 [2, 3072, 768], P(None, ('dp', 'head')), may hold values from -0.109375 to 0.109375
- w_head: float32 [768, 512], replicated, may hold values from -0.4375 to 0.4375
- m_head: float32 [768, 512], replicated, may hold values from -1.5258789e-05 to 1.5258789e-05
- a_head: float32 [768, 512], replicated, may hold values from -0.4375 to 0.4375
Outputs:
- loss: float32 [], replicated
- grad_norm: float32 [], replicated
- new_w_emb: float32 [128, 768], replicated
- new_m_emb: float32 [128, 768], replicated
- new_a_emb: float32 [128, 768], replicated
- new_vectors: float32 [16, 768], replicated
- new_m_vec: float32 [16, 768], replicated
- new_a_vec: float32 [16, 768], replicated
- new_w_qkv: float32 [2, 768, 3, 2, 384], P(None, 'dp', None, 'head')
- new_m_qkv: float32 [2, 768, 3, 2, 384], P(None, 'dp', None, 'head')
- new_a_qkv: float32 [2, 768, 3, 2, 384], P(None, 'dp', None, 'head')
- new_w_out: float32 [2, 2, 384, 768], P(None, 'head', 'dp')
- new_m_out: float32 [2, 2, 384, 768], P(None, 'head', 'dp')
- new_a_out: float32 [2, 2, 384, 768], P(None, 'head', 'dp')
- new_w_up: float32 [2, 768, 3072], P(None, ('dp', 'head'))
- new_m_up: float32 [2, 768, 3072], P(None, ('dp', 'head'))
- new_a_up: float32 [2, 768, 3072], P(None, ('dp', 'head'))
- new_w_down: float32 [2, 3072, 768], P(None, ('dp', 'head'))
- new_m_down: float32 [2, 3072, 768], P(None, ('dp', 'head'))
- new_a_down: float32 [2, 3072, 768], P(None, ('dp', 'head'))
- new_w_head: float32 [768, 512], replicated
- new_m_head: float32 [768, 512], replicated
- new_a_head: float32 [768, 512], replicated
The draws below stay inside these ranges and needn't reach their ends.
Inputs may be any that keep to these rules, and one draw needn't show every extreme that they name: Slots 0 to counts[t] - 1 of table t hold context; table 0 fills all 768, table 1 holds the least, 64. `query_mask`: the first query row of every table is true.
All inputs are finite; a program needn't handle non-finite values. No bound on the sum of `feat_mask` on one device may be relied on, other than what follows from the above.
Results may differ from the reference program's by a relative error of at most 0.012.
Values may be sent and summed in bfloat16 or wider, within the bound.
A program may use at most 256 MiB of HBM per device.

```python
import jax
import jax.numpy as jnp
from jax import lax

D = 768
HEADS = 12
HD = 64
FF = 3072
F = 128
BINS = 512
L = 2
CTX = 768
QRY = 256
ROWS = 1024
NV = 16
TABLES = 32
N_HEAD = 2


def draw_counts(key, part):
    least_count = CTX // 12
    values = jax.random.randint(jax.random.fold_in(key, 3), (TABLES,), least_count, CTX + 1)
    return values.at[0].set(CTX).at[1].set(least_count).astype(jnp.int32)


def draw_query_mask(key, part):
    threshold_row = 300 + 700 * jnp.arange(TABLES)[:, None] // max(TABLES - 1, 1)
    dice_rolls = jax.random.randint(jax.random.fold_in(key, 4), (TABLES, QRY), 0, 1000)
    marked = jnp.where(dice_rolls < threshold_row, 1, 0).astype(jnp.int32)
    return marked.at[:, 0].set(1)


def vector_rows(key):
    noise_rows = jax.random.normal(key, (NV, D), jnp.float32)
    row_at = jnp.arange(NV)[:, None]
    slot_in_layer = (row_at - 2) % 6
    gain_row = (row_at >= 2) & (row_at < NV - 2) & ((slot_in_layer == 0) | (slot_in_layer == 2)) | (row_at == NV - 2)
    shaped = jnp.where(gain_row, 1.0 + 0.2 * noise_rows, 0.1 * noise_rows)
    return jnp.where(row_at == 0, noise_rows, shaped)


def draw_vectors(key, part):
    return vector_rows(jax.random.fold_in(key, 1))


def draw_a_vec(key, part):
    return vector_rows(jax.random.fold_in(key, 2))


def touch_ends(array, stream_key, least, high):
    longest = array.shape.index(max(array.shape))
    spots = []
    for shift in (0, 1):
        where = [jax.random.randint(jax.random.fold_in(stream_key, axis), (), 0, length) for axis, length in enumerate(array.shape)]
        where[longest] = (where[longest] + shift) % array.shape[longest]
        spots.append(tuple(where))
    return array.at[spots[0]].set(least).at[spots[1]].set(high)


def steps_of(stream_key, dims, pieces, least, high):
    def one(axis_at, parts):
        draws = jax.random.uniform(jax.random.fold_in(jax.random.fold_in(stream_key, 6), axis_at), (parts,), jnp.float32, least / len(pieces), high / len(pieces))
        return jnp.repeat(jnp.exp(draws), dims[axis_at] // parts).reshape((-1,) + (1,) * (len(dims) - axis_at - 1))

    factor_of = one(*pieces[0])
    for cut in pieces[1:]:
        factor_of = factor_of * one(*cut)
    return factor_of


def noise(own_key, shape, deviation, most, split=(), held_as=jnp.bfloat16):
    factor_of = steps_of(own_key, shape, split, -0.22, 0.18) if split else 1.0
    result = jax.random.normal(own_key, shape, jnp.float32) * deviation * factor_of
    return jnp.minimum(jnp.maximum(result, -most), most).astype(held_as)


def setup_inputs(seed: int = 0) -> dict:
    arg_keys = jax.random.split(jax.random.key(seed), 28)
    return {
        "rows_in": noise(arg_keys[0], (TABLES, ROWS, F), 1.0, 6.0, ((0, 32),)),
        "feat_mask": touch_ends((jax.random.randint(arg_keys[1], (TABLES, F), 0, 8) < 7).astype(jnp.int32), jax.random.fold_in(arg_keys[1], 1), 0, 1),
        "counts": draw_counts(jax.random.fold_in(arg_keys[27], 71), 0),
        "ctx_vals": noise(arg_keys[3], (TABLES, CTX), 1.0, 6.0, ((0, 32),), jnp.float32),
        "targets": touch_ends(jax.random.randint(arg_keys[4], (TABLES, QRY), 0, BINS), jax.random.fold_in(arg_keys[4], 1), 0, BINS - 1).astype(jnp.int32),
        "query_mask": draw_query_mask(jax.random.fold_in(arg_keys[27], 71), 0),
        "w_emb": noise(arg_keys[6], (F, D), F ** -0.5, 0.5, (), jnp.float32),
        "m_emb": noise(arg_keys[7], (F, D), (0.01 * (L * (4 * D * D + 2 * D * FF) + F * D + D * BINS + NV * D) ** -0.5), 1.52587890625e-05, (), jnp.float32),
        "a_emb": noise(arg_keys[8], (F, D), F ** -0.5, 0.5, (), jnp.float32),
        "vectors": draw_vectors(jax.random.fold_in(arg_keys[27], 71), 0),
        "m_vec": noise(arg_keys[10], (NV, D), (0.01 * (L * (4 * D * D + 2 * D * FF) + F * D + D * BINS + NV * D) ** -0.5), 1.52587890625e-05, (), jnp.float32),
        "a_vec": draw_a_vec(jax.random.fold_in(arg_keys[27], 71), 0),
        "w_qkv": noise(arg_keys[12], (L, D, 3, N_HEAD, D // N_HEAD), D ** -0.5, 0.21875, ((1, 16), (3, 2)), jnp.float32),
        "m_qkv": noise(arg_keys[13], (L, D, 3, N_HEAD, D // N_HEAD), (0.01 * (L * (4 * D * D + 2 * D * FF) + F * D + D * BINS + NV * D) ** -0.5), 1.52587890625e-05, ((1, 16), (3, 2)), jnp.float32),
        "a_qkv": noise(arg_keys[14], (L, D, 3, N_HEAD, D // N_HEAD), D ** -0.5, 0.21875, ((1, 16), (3, 2)), jnp.float32),
        "w_out": noise(arg_keys[15], (L, N_HEAD, D // N_HEAD, D), (D // 16) ** -0.5, 0.875, ((1, 2), (2, 16)), jnp.float32),
        "m_out": noise(arg_keys[16], (L, N_HEAD, D // N_HEAD, D), (0.01 * (L * (4 * D * D + 2 * D * FF) + F * D + D * BINS + NV * D) ** -0.5), 1.52587890625e-05, ((1, 2), (2, 16)), jnp.float32),
        "a_out": noise(arg_keys[17], (L, N_HEAD, D // N_HEAD, D), (D // 16) ** -0.5, 0.875, ((1, 2), (2, 16)), jnp.float32),
        "w_up": noise(arg_keys[18], (L, D, FF), D ** -0.5, 0.21875, ((1, 32),), jnp.float32),
        "m_up": noise(arg_keys[19], (L, D, FF), (0.01 * (L * (4 * D * D + 2 * D * FF) + F * D + D * BINS + NV * D) ** -0.5), 1.52587890625e-05, ((1, 32),), jnp.float32),
        "a_up": noise(arg_keys[20], (L, D, FF), D ** -0.5, 0.21875, ((1, 32),), jnp.float32),
        "w_down": noise(arg_keys[21], (L, FF, D), FF ** -0.5, 0.109375, ((1, 32),), jnp.float32),
        "m_down": noise(arg_keys[22], (L, FF, D), (0.01 * (L * (4 * D * D + 2 * D * FF) + F * D + D * BINS + NV * D) ** -0.5), 1.52587890625e-05, ((1, 32),), jnp.float32),
        "a_down": noise(arg_keys[23], (L, FF, D), FF ** -0.5, 0.109375, ((1, 32),), jnp.float32),
        "w_head": noise(arg_keys[24], (D, BINS), (D // 4) ** -0.5, 0.4375, (), jnp.float32),
        "m_head": noise(arg_keys[25], (D, BINS), (0.01 * (L * (4 * D * D + 2 * D * FF) + F * D + D * BINS + NV * D) ** -0.5), 1.52587890625e-05, (), jnp.float32),
        "a_head": noise(arg_keys[26], (D, BINS), (D // 4) ** -0.5, 0.4375, (), jnp.float32),
    }


@jax.custom_vjp
def low(v):
    return lax.optimization_barrier(v.astype(jnp.bfloat16)).astype(jnp.float32)

@jax.custom_vjp
def low_back(v):
    return v

def low_keep(v):
    return (low(v), None)

def low_pass(kept, grad):
    return (grad,)

def back_keep(v):
    return (v, None)

def back_low(kept, grad):
    return (low(grad),)
low.defvjp(low_keep, low_pass)
low_back.defvjp(back_keep, back_low)
eps_norm = 1e-05
clip_at = 0.01
rate = 3000.0
moment = 0.9
keep_avg = 0.9
decay_wd = 1e-05

def layer_norm(values, gain_row, shift_row):
    center = values - lax.optimization_barrier(jnp.mean(values, -1, keepdims=True))
    spread = lax.optimization_barrier(jnp.mean(center * center, -1, keepdims=True))
    return center * lax.rsqrt(spread + eps_norm) * gain_row + shift_row

def product(first_op, second_op):
    return jnp.dot(first_op, second_op, precision=lax.Precision.HIGHEST, preferred_element_type=jnp.float32)

def table_loss(params, rows_in, feat_mask, ctx_vals, ctx_count, target_bins, query_mask, pooled):
    w_emb, vectors, w_qkv, w_out, w_up, w_down, w_head = params
    width = HEADS * HD
    masked = low(rows_in * feat_mask[None, :])
    leading = jnp.concatenate([ctx_vals, jnp.zeros((QRY,), jnp.float32)])
    residual = low_back(product(masked, low(w_emb))) + vectors[1] + leading[:, None] * vectors[0]
    key_valid = jnp.arange(CTX) < ctx_count
    for layer_at in range(L):
        vec_base = 2 + 6 * layer_at
        normed = low(layer_norm(residual, vectors[vec_base], vectors[vec_base + 1]))
        joined = low_back(low(product(normed, low(w_qkv[layer_at].reshape(width, 3 * width)))))
        queries = joined[:, :width].reshape(ROWS, HEADS, HD)
        key_rows = joined[:CTX, width:2 * width].reshape(CTX, HEADS, HD)
        value_rows = joined[:CTX, 2 * width:].reshape(CTX, HEADS, HD)
        raw_score = jnp.einsum('rhe,che->hrc', queries, key_rows, precision=lax.Precision.HIGHEST)
        raw_score = low_back(raw_score * HD ** (-0.5))
        raw_score = jnp.where(key_valid[None, None, :], raw_score, -1e+30)
        weights_low = low(jax.nn.softmax(raw_score, axis=-1))
        mixed_rows = jnp.einsum('hrc,che->rhe', weights_low, value_rows, precision=lax.Precision.HIGHEST)
        mixed_rows = low_back(low(mixed_rows.reshape(ROWS, width)))
        attn_part = low_back(product(mixed_rows, low(w_out[layer_at].reshape(width, width))))
        residual = residual + attn_part + vectors[vec_base + 4]
        normed_mlp = low(layer_norm(residual, vectors[vec_base + 2], vectors[vec_base + 3]))
        hidden = low_back(product(normed_mlp, low(w_up[layer_at])))
        active = low(jax.nn.gelu(hidden))
        residual = residual + low_back(product(active, low(w_down[layer_at]))) + vectors[vec_base + 5]
    final_rows = low(layer_norm(residual[CTX:], vectors[NV - 2], vectors[NV - 1]))
    logits = low_back(product(final_rows, low(w_head)))
    row_peak = lax.optimization_barrier(jnp.max(logits, -1, keepdims=True))
    log_total = row_peak[:, 0] + jnp.log(lax.optimization_barrier(jnp.sum(jnp.exp(logits - row_peak), -1)))
    target_hit = jnp.arange(BINS)[None, :] == target_bins[:, None]
    picked = lax.optimization_barrier(jnp.sum(jnp.where(target_hit, logits, 0.0), -1))
    return jnp.sum((log_total - picked) * query_mask) / pooled

def update(weight, moment_old, average, grad_in, scale):
    applied = grad_in * scale + decay_wd * weight
    moment_new = moment * moment_old + applied
    weight_new = weight - rate * (applied + moment * moment_new)
    return (weight_new, moment_new, keep_avg * average + (1.0 - keep_avg) * weight_new)

def reference(rows_in, feat_mask, counts, ctx_vals, targets, query_mask, w_emb, m_emb, a_emb, vectors, m_vec, a_vec, w_qkv, m_qkv, a_qkv, w_out, m_out, a_out, w_up, m_up, a_up, w_down, m_down, a_down, w_head, m_head, a_head):
    params = (w_emb, vectors, w_qkv, w_out, w_up, w_down, w_head)
    query_float = query_mask.astype(jnp.float32)
    pooled = jnp.sum(query_float)

    def one_table(carry, item):
        loss_sum, grad_sum = carry
        rows_t, feat_t, ctx_t, count_t, target_t, query_t = item

        def table_fn(values):
            return table_loss(values, rows_t, feat_t, ctx_t, count_t, target_t, query_t, pooled)
        value, pull = jax.vjp(table_fn, params)
        grads = pull(jnp.ones((), jnp.float32))[0]
        return ((loss_sum + value, jax.tree.map(jnp.add, grad_sum, grads)), None)
    zeros = jax.tree.map(jnp.zeros_like, params)
    items = (rows_in.astype(jnp.float32), feat_mask.astype(jnp.float32), ctx_vals, counts, targets, query_float)
    (loss, grads), _ = lax.scan(one_table, (jnp.zeros((), jnp.float32), zeros), items)
    total_sq = jnp.zeros((), jnp.float32)
    for grad_leaf in grads:
        total_sq = total_sq + jnp.sum(grad_leaf * grad_leaf)
    grad_norm = jnp.sqrt(total_sq)
    scale = jnp.minimum(1.0, clip_at / grad_norm)
    g_emb, g_vec, g_qkv, g_out, g_up, g_down, g_head = grads
    e_w, e_m, e_a = update(w_emb, m_emb, a_emb, g_emb, scale)
    v_w, v_m, v_a = update(vectors, m_vec, a_vec, g_vec, scale)
    q_w, q_m, q_a = update(w_qkv, m_qkv, a_qkv, g_qkv, scale)
    o_w, o_m, o_a = update(w_out, m_out, a_out, g_out, scale)
    u_w, u_m, u_a = update(w_up, m_up, a_up, g_up, scale)
    d_w, d_m, d_a = update(w_down, m_down, a_down, g_down, scale)
    h_w, h_m, h_a = update(w_head, m_head, a_head, g_head, scale)
    return (loss, grad_norm, e_w, e_m, e_a, v_w, v_m, v_a, q_w, q_m, q_a, o_w, o_m, o_a, u_w, u_m, u_a, d_w, d_m, d_a, h_w, h_m, h_a)
```

```python
import functools
import jax
import jax.numpy as jnp
from jax import lax
from jax.sharding import PartitionSpec as P
from jax.experimental import pallas as pl
from jax.experimental.pallas import tpu as pltpu

MESH = pl.DeviceIdType.MESH
ORDERS = ("zxy", "xzy", "yzx")
PIECES = len(ORDERS)


class Place:
    def __init__(self):
        self.chip = lax.axis_index("dp")
        self.core = lax.axis_index("head")
        self.x = self.chip % 2
        self.y = (self.chip // 2) % 2
        self.z = self.chip // 4
        z = self.z
        self.z_from = (z, 1 + z % 2, (12 - 2 * z) % 5, 3 - 3 * (z // 2))

    def peer(self, way):
        step = {
            "x": 1 - 2 * self.x,
            "y": 2 - 4 * self.y,
            "u": 4,
            "d": -4,
            "c": 0,
        }[way]
        core = 1 - self.core if way == "c" else self.core
        return (self.chip + step, core)

    def block(self, k, ax, ay):
        sx = self.x if ax == 0 else 1 - self.x
        sy = self.y if ay == 0 else 1 - self.y
        return self.z_from[k] * 4 + sy * 2 + sx


def meet(place):
    barrier = pltpu.get_barrier_semaphore()
    for way in "xyc":
        pl.semaphore_signal(barrier, inc=1, device_id=place.peer(way), device_id_type=MESH)

    @pl.when(place.z < 3)
    def _():
        pl.semaphore_signal(barrier, inc=1, device_id=place.peer("u"), device_id_type=MESH)

    @pl.when(place.z > 0)
    def _():
        pl.semaphore_signal(barrier, inc=1, device_id=place.peer("d"), device_id_type=MESH)

    ends = place.z * (3 - place.z)
    pl.semaphore_wait(barrier, 4 + ends // 2)


def at_block(ref, chip, core, piece, by_core):
    return ref.at[core, chip, piece] if by_core else ref.at[chip, core, piece]


def gather_kernel(by_core, *refs):
    n = len(by_core)
    ins, outs = refs[:n], refs[n : 2 * n]
    local_sem, recv, core_recv, send, core_send = refs[2 * n :]
    place = Place()
    me = place.chip
    meet(place)

    def slot(a, c, chip, core=None):
        return at_block(outs[a], chip, place.core if core is None else core, c, by_core[a])

    def copy(a, c, chip, way, src, sems):
        return pltpu.make_async_remote_copy(
            src_ref=src, dst_ref=slot(a, c, chip), send_sem=sems[0], recv_sem=sems[1],
            device_id=place.peer(way), device_id_type=MESH)

    ways = {"x": 0, "y": 1, "u": 2, "d": 3}

    def forward(a, c, order, k, ax, ay):
        chip = place.block(k, ax, ay)
        rel = {"x": ax, "y": ay, "z": k}
        last = max([i for i in range(3) if rel[order[i]] != 0], default=-1)
        src = ins[a].at[c] if last < 0 else slot(a, c, chip)
        for i in range(max(last, 0), 3):
            dim = order[i]
            if dim == "z":
                sz = place.z_from[k]

                @pl.when((sz <= place.z) & (place.z < 3))
                def _():
                    copy(a, c, chip, "u", src, (send.at[a, c, 2], recv.at[a, c, chip])).start()

                @pl.when((sz >= place.z) & (place.z > 0))
                def _():
                    copy(a, c, chip, "d", src, (send.at[a, c, 3], recv.at[a, c, chip])).start()
            elif rel[dim] == 0:
                w = dim
                copy(a, c, chip, w, src, (send.at[a, c, ways[w]], recv.at[a, c, chip])).start()
        copy(a, c, chip, "c", src, (core_send.at[a], core_recv.at[a])).start()

    entries = sorted(
        [(k, ax, ay) for k in range(4) for ax in range(2) for ay in range(2)],
        key=lambda e: (e[0] * 1.0 + e[1] + e[2]))
    for k, ax, ay in entries:
        for a in range(n):
            for c, order in enumerate(ORDERS):
                chip = place.block(k, ax, ay)
                if (k, ax, ay) != (0, 0, 0):
                    copy(a, c, chip, "x", slot(a, c, chip), (send.at[a, c, 0], recv.at[a, c, chip])).wait_recv()
                forward(a, c, order, k, ax, ay)
    own = []
    for a in range(n):
        for c in range(PIECES):
            cp = pltpu.make_async_copy(ins[a].at[c], slot(a, c, me), local_sem.at[a, c])
            cp.start()
            own.append(cp)
    for cp in own:
        cp.wait()
    for a in range(n):
        whole = outs[a].at[0] if by_core[a] else outs[a].at[:, 0]
        pltpu.make_async_remote_copy(
            src_ref=whole, dst_ref=whole, send_sem=core_send.at[a], recv_sem=core_recv.at[a],
            device_id=place.peer("c"), device_id_type=MESH).wait()
        for c, order in enumerate(ORDERS):
            def drain(way, count):
                part = outs[a].at[0, pl.ds(0, count), c] if by_core[a] else outs[a].at[pl.ds(0, count), 0, c]
                pltpu.make_async_remote_copy(
                    src_ref=part, dst_ref=part, send_sem=send.at[a, c, ways[way]], recv_sem=recv.at[a, c, 0],
                    device_id=place.peer("c"), device_id_type=MESH).wait_send()
            size = {"x": 2, "y": 2, "z": 4}
            before = 1
            for dim in order:
                if dim == "z":
                    for zz in range(4):
                        @pl.when(place.z == zz)
                        def _(zz=zz, before=before):
                            if zz < 3:
                                drain("u", before * (zz + 1))
                            if zz > 0:
                                drain("d", before * (4 - zz))
                else:
                    drain(dim, before)
                before *= size[dim]


def all_gather_layer(arrays, by_core, collective_id):
    n = len(arrays)
    outs = tuple(
        jax.ShapeDtypeStruct(((2, 16) if bc else (16, 2)) + a.shape, a.dtype)
        for a, bc in zip(arrays, by_core))
    sent = sum(a.size * 2 for a in arrays) * 31
    return pl.pallas_call(
        functools.partial(gather_kernel, by_core),
        out_shape=outs,
        in_specs=[pl.BlockSpec(memory_space=pltpu.VMEM)] * n,
        out_specs=[pl.BlockSpec(memory_space=pl.ANY)] * n,
        scratch_shapes=[
            pltpu.SemaphoreType.DMA((n, PIECES)),
            pltpu.SemaphoreType.DMA((n, PIECES, 16)),
            pltpu.SemaphoreType.DMA((n,)),
            pltpu.SemaphoreType.DMA((n, PIECES, 4)),
            pltpu.SemaphoreType.DMA((n,)),
        ],
        compiler_params=pltpu.CompilerParams(
            collective_id=collective_id, has_side_effects=True),
        cost_estimate=pl.CostEstimate(flops=0, bytes_accessed=2 * sent, transcendentals=0),
    )(*arrays)


def reduce_kernel(by_core, *refs):
    n = len(by_core)
    ins, outs = refs[:n], refs[n : 2 * n]
    scr = refs[2 * n :]
    mine, other = scr[:n], scr[n : 2 * n]
    got = {"x": scr[2 * n : 3 * n], "y": scr[3 * n : 4 * n], "u": scr[4 * n : 5 * n], "d": scr[5 * n : 6 * n]}
    load_sem, core_recv, core_send, recv, send = scr[6 * n :]
    ways = {"x": 0, "y": 1, "u": 2, "d": 3}
    place = Place()
    meet(place)
    f32 = jnp.float32

    def chip_of(sx, sy, sz):
        return sz * 4 + sy * 2 + sx

    def load(a):
        src = ins[a].at[place.core] if by_core[a] else ins[a].at[:, place.core]
        return pltpu.make_async_copy(src, mine[a], load_sem.at[a])

    def to_core(a, c, chip):
        src = at_block(ins[a], chip, 1 - place.core, c, by_core[a])
        return pltpu.make_async_remote_copy(
            src_ref=src, dst_ref=other[a].at[chip, c], send_sem=core_send.at[a, c], recv_sem=core_recv.at[a, c, chip],
            device_id=place.peer("c"), device_id_type=MESH)

    def hop(a, c, chip, way):
        return pltpu.make_async_remote_copy(
            src_ref=mine[a].at[chip, c], dst_ref=got[way][a].at[chip, c],
            send_sem=send.at[a, c, ways[way]], recv_sem=recv.at[a, c, ways[way], chip],
            device_id=place.peer(way), device_id_type=MESH)

    def add(a, c, chip, extra):
        mine[a][chip, c] = (mine[a][chip, c].astype(f32) + extra[a][chip, c].astype(f32)).astype(jnp.bfloat16)

    for a in range(n):
        load(a).start()
    work = [(a, c, order) for a in range(n) for c, order in enumerate(ORDERS)]

    def split(order, i):
        dim = order[2]
        far = 1 - i // 8
        j = i % 8
        sz, w = j // 2, j % 2
        if dim == "x":
            sx = place.x + far * (1 - 2 * place.x)
            return chip_of(sx, w, sz)
        sy = place.y + far * (1 - 2 * place.y)
        return chip_of(w, sy, sz)

    for half in range(2):
        for a, c, order in work:
            def start_core(i, carry):
                to_core(a, c, split(order, i)).start()
                return carry
            lax.fori_loop(8 * half, 8 * half + 8, start_core, 0)
    for a in range(n):
        load(a).wait()
    for half in range(2):
        for a, c, order in work:
            def fold(i, carry):
                chip = split(order, i)
                to_core(a, c, chip).wait_recv()
                add(a, c, chip, other)
                if half == 0:
                    hop(a, c, chip, order[2]).start()
                return carry
            lax.fori_loop(8 * half, 8 * half + 8, fold, 0)

    def firsts_of(order):
        if order[0] == "z":
            return [(place.x, place.y)]
        if order[0] == "x":
            return [(1 - place.x, place.y), (place.x, place.y)]
        return [(place.x, 1 - place.y), (place.x, place.y)]

    for a, c, order in work:
        dim, nxt = order[2], order[1]
        for far in ((1, 0) if nxt != "z" else (None,)):
            def take(i, carry):
                if far is None:
                    w, sz = i % 2, i // 2
                else:
                    sz = i
                    m = place.x if nxt == "x" else place.y
                    w = m + far * (1 - 2 * m)
                chip = chip_of(place.x, w, sz) if dim == "x" else chip_of(w, place.y, sz)
                hop(a, c, chip, dim).wait_recv()
                add(a, c, chip, got[dim])
                if far == 1:
                    hop(a, c, chip, nxt).start()
                return carry
            lax.fori_loop(0, 8 if far is None else 4, take, 0)
    for a, c, order in work:
        if order[0] == "z":
            def take(i, carry):
                chip = chip_of(place.x, place.y, i)
                hop(a, c, chip, order[1]).wait_recv()
                add(a, c, chip, got[order[1]])
                return carry
            lax.fori_loop(0, 4, take, 0)
    for j in range(3):
        for way, target, active, inner in (
            ("u", 3 - j, place.z < 3 - j, place.z > 0),
            ("d", j, place.z > j, place.z < 3),
        ):
            @pl.when(active)
            def _():
                for a, c, order in work:
                    for sx, sy in firsts_of(order):
                        chip = chip_of(sx, sy, target)

                        @pl.when(inner)
                        def _():
                            hop(a, c, chip, way).wait_recv()
                            add(a, c, chip, got[way])
                        hop(a, c, chip, way).start()
    for a, c, order in work:
        for n_first, (sx, sy) in enumerate(firsts_of(order)):
            chip = chip_of(sx, sy, place.z)

            @pl.when(place.z > 0)
            def _():
                hop(a, c, chip, "u").wait_recv()
                add(a, c, chip, got["u"])

            @pl.when(place.z < 3)
            def _():
                hop(a, c, chip, "d").wait_recv()
                add(a, c, chip, got["d"])
            if order[0] != "z" and n_first == 0:
                hop(a, c, chip, order[0]).start()
    for a, c, order in work:
        if order[0] != "z":
            hop(a, c, place.chip, order[0]).wait_recv()
            add(a, c, place.chip, got[order[0]])
        outs[a][c] = mine[a][place.chip, c].astype(f32)
    for a, c, order in work:
        def drain(sem, count):
            part = other[a].at[pl.ds(0, count), c]
            pltpu.make_async_remote_copy(
                src_ref=part, dst_ref=part, send_sem=sem, recv_sem=recv.at[a, c, 0, 0],
                device_id=place.peer("c"), device_id_type=MESH).wait_send()
        drain(core_send.at[a, c], 16)
        left = 16
        for stage in (2, 1, 0):
            dim = order[stage]
            if dim == "z":
                q = left // 4
                for zz in range(4):
                    @pl.when(place.z == zz)
                    def _(zz=zz, q=q):
                        if zz < 3:
                            drain(send.at[a, c, 2], q * (3 - zz))
                        if zz > 0:
                            drain(send.at[a, c, 3], q * zz)
                left = q
            else:
                left //= 2
                drain(send.at[a, c, ways[dim]], left)


def reduce_scatter_layer(arrays, by_core, collective_id):
    n = len(arrays)
    shapes = [a.shape[2:] for a in arrays]
    full = [pltpu.VMEM((16,) + s, jnp.bfloat16) for s in shapes]
    sent = sum(a.size for a in arrays)
    return pl.pallas_call(
        functools.partial(reduce_kernel, by_core),
        out_shape=tuple(jax.ShapeDtypeStruct(s, jnp.float32) for s in shapes),
        in_specs=[pl.BlockSpec(memory_space=pl.ANY)] * n,
        out_specs=[pl.BlockSpec(memory_space=pltpu.VMEM)] * n,
        scratch_shapes=full * 6 + [
            pltpu.SemaphoreType.DMA((n,)),
            pltpu.SemaphoreType.DMA((n, PIECES, 16)),
            pltpu.SemaphoreType.DMA((n, PIECES)),
            pltpu.SemaphoreType.DMA((n, PIECES, 4, 16)),
            pltpu.SemaphoreType.DMA((n, PIECES, 4)),
        ],
        compiler_params=pltpu.CompilerParams(
            collective_id=collective_id, has_side_effects=True, vmem_limit_bytes=64 * 1024 * 1024 - 65536),
        cost_estimate=pl.CostEstimate(flops=sent, bytes_accessed=2 * sent, transcendentals=0),
    )(*arrays)


HD = 64
CTX = 768

eps_norm = 1e-05
clip_at = 0.01
rate = 3000.0
moment = 0.9
keep_avg = 0.9
decay_wd = 1e-05
low_type = jnp.bfloat16
wide_type = jnp.float32


def layer_norm(values, gain_row, shift_row):
    center = values - jnp.mean(values, -1, keepdims=True)
    spread = jnp.mean(center * center, -1, keepdims=True)
    return center * lax.rsqrt(spread + eps_norm) * gain_row + shift_row


def norm_back(values, gain_row, shift_row, upstream):
    _, pull = jax.vjp(layer_norm, values, gain_row, shift_row)
    return pull(upstream)


def gelu_back(values, upstream):
    _, pull = jax.vjp(jax.nn.gelu, values)
    return pull(upstream)[0]


def matmul(first_op, second_op):
    return jnp.dot(first_op, second_op, preferred_element_type=wide_type)


def contract(first_op, second_op, first_dim, second_dim):
    return lax.dot_general(
        first_op, second_op, (((first_dim,), (second_dim,)), ((), ())), preferred_element_type=wide_type
    )


def matmul_tn(first_op, second_op):
    return contract(first_op, second_op, 0, 0)


def matmul_nt(first_op, second_op):
    return contract(first_op, second_op, 1, 1)


def head_lanes(shape, head):
    lane = lax.broadcasted_iota(jnp.int32, shape, 1)
    mine = (lane < HD) if head == 0 else (lane >= HD)
    return mine, lane == (HD if head == 0 else 0)


def attend_kernel(q_ref, k_ref, v_ref, bias_ref, out_ref, lse_ref):
    q_block = q_ref[0] * jnp.asarray(HD ** -0.5, low_type)
    k_block, v_block, bias = k_ref[0], v_ref[0], bias_ref[...]
    v_turned = v_block.T
    parts = []
    for head in range(2):
        q_mine, q_one = head_lanes(q_block.shape, head)
        k_mine, _ = head_lanes(k_block.shape, head)
        one = jnp.where(q_one, jnp.ones_like(q_block), jnp.zeros_like(q_block))
        score = matmul_nt(jnp.where(k_mine, k_block, bias), jnp.where(q_mine, q_block, one))
        peak = jnp.max(score, 0, keepdims=True)
        lifted = jnp.exp(score - peak)
        total = jnp.sum(lifted, 0, keepdims=True)
        mixed = matmul(v_turned[head * HD : (head + 1) * HD], lifted.astype(low_type))
        parts.append(mixed / total)
        lse_ref[0, head : head + 1, :] = peak + jnp.log(total)
    out_ref[...] = jnp.concatenate(parts, 0).T.astype(low_type)


def attend(queries, keys_values, bias):
    groups, rows, width = queries.shape
    pairs = width // 128
    block = min(256, rows)
    grid = (groups * pairs, rows // block)
    return pl.pallas_call(
        attend_kernel,
        grid=grid,
        in_specs=[
            pl.BlockSpec((1, block, 128), lambda p, i: (p // pairs, i, p % pairs)),
            pl.BlockSpec((1, CTX, 128), lambda p, i: (p // pairs, 0, p % pairs)),
            pl.BlockSpec((1, CTX, 128), lambda p, i: (p // pairs, 0, pairs + p % pairs)),
            pl.BlockSpec((CTX, 128), lambda p, i: (0, 0)),
        ],
        out_specs=[
            pl.BlockSpec((block, 128), lambda p, i: (i, p)),
            pl.BlockSpec((1, 2, block), lambda p, i: (p, 0, i)),
        ],
        out_shape=(
            jax.ShapeDtypeStruct((rows, groups * width), low_type),
            jax.ShapeDtypeStruct((groups * pairs, 2, rows), wide_type),
        ),
        cost_estimate=pl.CostEstimate(
            flops=4 * rows * CTX * groups * width, bytes_accessed=8 * rows * groups * width,
            transcendentals=rows * CTX * groups * width // HD),
    )(queries, keys_values, keys_values, bias)


def attend_back_kernel(q_ref, k_ref, v_ref, bias_ref, g_ref, o_ref, lse_ref, gq_ref, gk_ref, gv_ref, k_sum, v_sum):
    step = pl.program_id(1)

    @pl.when(step == 0)
    def _():
        k_sum[...] = jnp.zeros_like(k_sum)
        v_sum[...] = jnp.zeros_like(v_sum)

    scale = HD ** -0.5
    q_block = q_ref[0] * jnp.asarray(scale, low_type)
    k_block, v_block, bias = k_ref[0], v_ref[0], bias_ref[...]
    g_block = g_ref[...]
    k_turned = k_block.T
    both = (g_block.astype(wide_type) * o_ref[...].astype(wide_type)).T
    parts = []
    for head in range(2):
        q_mine, q_one = head_lanes(q_block.shape, head)
        k_mine, _ = head_lanes(k_block.shape, head)
        nothing = jnp.zeros_like(q_block)
        one = jnp.where(q_one, jnp.ones_like(q_block), nothing)
        score = matmul_nt(jnp.where(k_mine, k_block, bias), jnp.where(q_mine, q_block, one))
        prob = jnp.exp(score - lse_ref[0, head : head + 1, :])
        g_mine = jnp.where(q_mine, g_block, nothing)
        grad_prob = matmul_nt(v_block, g_mine)
        inner = jnp.sum(both[head * HD : (head + 1) * HD], 0, keepdims=True)
        grad_score = (prob * (grad_prob - inner)).astype(low_type)
        v_sum[...] += matmul(prob.astype(low_type), g_mine)
        k_sum[...] += matmul(grad_score, jnp.where(q_mine, q_block, nothing))
        parts.append(matmul(k_turned[head * HD : (head + 1) * HD], grad_score) * scale)
    gq_ref[0] = jnp.concatenate(parts, 0).T.astype(low_type)

    @pl.when(step == pl.num_programs(1) - 1)
    def _():
        gk_ref[0] = k_sum[...].astype(low_type)
        gv_ref[0] = v_sum[...].astype(low_type)


def attend_back(queries, keys_values, bias, grad_mixed, mixed, lse):
    groups, rows, width = queries.shape
    pairs = width // 128
    block = min(256, rows)
    grid = (groups * pairs, rows // block)
    row_spec = pl.BlockSpec((block, 128), lambda p, i: (i, p))
    key_out = pl.BlockSpec((1, CTX, 128), lambda p, i: (p // pairs, 0, p % pairs))
    return pl.pallas_call(
        attend_back_kernel,
        grid=grid,
        in_specs=[
            pl.BlockSpec((1, block, 128), lambda p, i: (p // pairs, i, p % pairs)),
            pl.BlockSpec((1, CTX, 128), lambda p, i: (p // pairs, 0, p % pairs)),
            pl.BlockSpec((1, CTX, 128), lambda p, i: (p // pairs, 0, pairs + p % pairs)),
            pl.BlockSpec((CTX, 128), lambda p, i: (0, 0)),
            row_spec,
            row_spec,
            pl.BlockSpec((1, 2, block), lambda p, i: (p, 0, i)),
        ],
        out_specs=[
            pl.BlockSpec((1, block, 128), lambda p, i: (p // pairs, i, p % pairs)),
            key_out,
            key_out,
        ],
        out_shape=(
            jax.ShapeDtypeStruct(queries.shape, low_type),
            jax.ShapeDtypeStruct((groups, CTX, width), low_type),
            jax.ShapeDtypeStruct((groups, CTX, width), low_type),
        ),
        scratch_shapes=[pltpu.VMEM((CTX, 128), wide_type)] * 2,
        cost_estimate=pl.CostEstimate(
            flops=10 * rows * CTX * groups * width, bytes_accessed=16 * rows * groups * width,
            transcendentals=rows * CTX * groups * width // HD),
    )(queries, keys_values, keys_values, bias, grad_mixed, mixed, lse)


def grouped(rows, weight):
    return jnp.einsum("rd,gdc->grc", rows, weight, preferred_element_type=wide_type)


def layer_forward(residual, first, vec_rows, weights, bias):
    w_joined, w_mix, w_grow, w_shrink = weights
    width = w_joined.shape[2] // 3
    normed = layer_norm(residual, vec_rows[0], vec_rows[1]).astype(low_type)
    queries = grouped(normed[first:], w_joined[:, :, :width]).astype(low_type)
    keys_values = grouped(normed[:CTX], w_joined[:, :, width:]).astype(low_type)
    mixed, lse = attend(queries, keys_values, bias)
    middle = residual[first:] + matmul(mixed, w_mix) + vec_rows[4]
    normed_mlp = layer_norm(middle, vec_rows[2], vec_rows[3]).astype(low_type)
    hidden = matmul(normed_mlp, w_grow)
    active = jax.nn.gelu(hidden).astype(low_type)
    output = middle + matmul(active, w_shrink) + vec_rows[5]
    return output, (residual, normed, queries, keys_values, mixed, lse, middle, normed_mlp, hidden, active)


def layer_backward(upstream, kept, first, vec_rows, weights, bias):
    w_joined, w_mix, w_grow, w_shrink = weights
    width = w_joined.shape[2] // 3
    residual, normed, queries, keys_values, mixed, lse, middle, normed_mlp, hidden, active = kept
    down_low = upstream.astype(low_type)
    grad_shrink = matmul_tn(active, down_low).astype(low_type)
    grad_hidden = gelu_back(hidden, matmul_nt(down_low, w_shrink)).astype(low_type)
    grad_grow = matmul_tn(normed_mlp, grad_hidden).astype(low_type)
    grad_middle, gain_mlp, shift_mlp = norm_back(
        middle, vec_rows[2], vec_rows[3], matmul_nt(grad_hidden, w_grow))
    grad_middle = grad_middle + upstream
    mix_low = grad_middle.astype(low_type)
    grad_mix = matmul_tn(mixed, mix_low).astype(low_type)
    grad_mixed = matmul_nt(mix_low, w_mix).astype(low_type)
    grad_q, grad_k, grad_v = attend_back(queries, keys_values, bias, grad_mixed, mixed, lse)

    def weight_grad(rows, grads):
        return jnp.einsum("rd,grc->gdc", rows, grads, preferred_element_type=wide_type).astype(low_type)

    def row_grad(grads, part):
        return jnp.einsum(
            "grc,gdc->rd", grads, w_joined[:, :, part * width : (part + 1) * width], preferred_element_type=wide_type)

    grad_joined = jnp.concatenate(
        [weight_grad(normed[first:], grad_q), weight_grad(normed[:CTX], grad_k), weight_grad(normed[:CTX], grad_v)], 2)
    from_q = row_grad(grad_q, 0)
    from_kv = row_grad(grad_k, 1) + row_grad(grad_v, 2)
    rows = residual.shape[0]
    below = jnp.zeros((first, from_q.shape[1]), wide_type)
    tail = jnp.zeros((rows - CTX, from_q.shape[1]), wide_type)
    grad_normed = jnp.concatenate([below, from_q], 0) + jnp.concatenate([from_kv, tail], 0)
    grad_input, gain_attn, shift_attn = norm_back(residual, vec_rows[0], vec_rows[1], grad_normed)
    vec_grads = [gain_attn, shift_attn, gain_mlp, shift_mlp, jnp.sum(grad_middle, 0), jnp.sum(upstream, 0)]
    grad_out = grad_input + jnp.concatenate([below, grad_middle], 0)
    return grad_out, (grad_joined, grad_mix, grad_grow, grad_shrink), vec_grads


def update(weight, moment_old, average, grad_in, scale):
    applied = grad_in * scale + decay_wd * weight
    moment_new = moment * moment_old + applied
    weight_new = weight - rate * (applied + moment * moment_new)
    return (weight_new, moment_new, keep_avg * average + (1.0 - keep_avg) * weight_new)


BY_CORE = (True, True, False, False)


def gather_weights(shard_list, direct, number):
    if direct:
        pieces = [s.reshape((PIECES, s.shape[0] // PIECES, s.shape[1])) for s in shard_list]
        return all_gather_layer(pieces, BY_CORE, number)
    out = []
    for shard, by_core in zip(shard_list, BY_CORE):
        whole = lax.all_gather(shard, "dp", axis=0)
        out.append(lax.all_gather(whole, "head", axis=0 if by_core else 1))
    return out


def scatter_grads(grads, by_core_list, rows_list, direct, number):
    chips, cores = lax.axis_size("dp"), lax.axis_size("head")
    if direct:
        pieces = []
        for grad, by_core, rows in zip(grads, by_core_list, rows_list):
            lead = (cores, chips) if by_core else (chips, cores)
            pieces.append(grad.reshape(lead + (PIECES, rows // PIECES, -1)))
        outs = reduce_scatter_layer(pieces, by_core_list, number)
        return [o.reshape((rows, -1)) for o, rows in zip(outs, rows_list)]
    outs = []
    for grad, by_core, rows in zip(grads, by_core_list, rows_list):
        lead = (cores, chips) if by_core else (chips, cores)
        grad = grad.reshape(lead + (rows, -1)).astype(wide_type)
        half = lax.psum_scatter(grad, "head", scatter_dimension=0 if by_core else 1)
        outs.append(lax.psum_scatter(half, "dp", scatter_dimension=0))
    return outs


def gather_small(arrays, direct, number):
    if direct:
        return all_gather_layer(arrays, (False,) * len(arrays), number)
    return [lax.all_gather(lax.all_gather(a, "dp", axis=0), "head", axis=1) for a in arrays]


def shards(
    rows_in, feat_mask, counts, ctx_vals, targets, query_mask,
    w_emb, m_emb, a_emb, vectors, m_vec, a_vec,
    w_qkv, m_qkv, a_qkv, w_out, m_out, a_out, w_up, m_up, a_up, w_down, m_down, a_down,
    w_head, m_head, a_head,
):
    chips, cores = lax.axis_size("dp"), lax.axis_size("head")
    direct = (chips, cores) == (16, 2)
    _, row_count, feat_count = rows_in.shape
    layer_total = w_qkv.shape[0]
    width = w_emb.shape[1]
    joined_rows = w_qkv.shape[1]
    kinds = w_qkv.shape[2] * w_qkv.shape[4]

    weights = []
    for at in range(layer_total):
        own = [
            w_qkv[at].reshape((joined_rows, kinds)).astype(low_type),
            w_out[at, 0].astype(low_type),
            w_up[at].astype(low_type),
            w_down[at].astype(low_type),
        ]
        qkv, out, up, down = gather_weights(own, direct, 1 + at)
        weights.append((
            qkv.reshape((cores, width, kinds)),
            out.reshape((width, width)),
            up.reshape((width, -1)),
            down.reshape((-1, width)),
        ))

    table = lax.axis_index("dp") * cores + lax.axis_index("head")
    count = lax.dynamic_slice_in_dim(counts, table, 1, 0)
    bias = jnp.where(jnp.arange(CTX) < count, 0.0, -1e30).astype(low_type)
    bias = jnp.broadcast_to(bias[:, None], (CTX, 128))
    masked = rows_in[0] * feat_mask[0][None, :].astype(low_type)
    leading = jnp.concatenate([ctx_vals[0], jnp.zeros((row_count - CTX,), wide_type)])[:, None]
    residual = matmul(masked, w_emb.astype(low_type)) + vectors[1] + leading * vectors[0]
    kept_all = []
    for at in range(layer_total):
        first = CTX if at == layer_total - 1 else 0
        residual, kept = layer_forward(residual, first, vectors[2 + 6 * at : 8 + 6 * at], weights[at], bias)
        kept_all.append(kept)

    head_low = w_head.astype(low_type)
    final_rows = layer_norm(residual, vectors[-2], vectors[-1]).astype(low_type)
    logits = matmul(final_rows, head_low)
    row_peak = jnp.max(logits, -1, keepdims=True)
    log_total = row_peak[:, 0] + jnp.log(jnp.sum(jnp.exp(logits - row_peak), -1))
    target_hit = (jnp.arange(logits.shape[1])[None, :] == targets[0][:, None]).astype(wide_type)
    picked = jnp.sum(logits * target_hit, -1)
    row_weight = query_mask[0].astype(wide_type)
    loss_part = jnp.sum((log_total - picked) * row_weight)
    grad_logits = ((jnp.exp(logits - log_total[:, None]) - target_hit) * row_weight[:, None]).astype(low_type)
    grad_head = matmul_tn(final_rows, grad_logits).astype(low_type)
    upstream, gain_final, shift_final = norm_back(
        residual, vectors[-2], vectors[-1], matmul_nt(grad_logits, head_low))

    rows_list = [joined_rows, w_out.shape[2], w_up.shape[1], w_down.shape[1]]
    parts = [None] * layer_total
    vec_grads = [None] * layer_total
    for at in reversed(range(layer_total)):
        first = CTX if at == layer_total - 1 else 0
        upstream, big, vec_grads[at] = layer_backward(
            upstream, kept_all[at], first, vectors[2 + 6 * at : 8 + 6 * at], weights[at], bias)
        if at > 0:
            parts[at] = scatter_grads(big, BY_CORE, rows_list, direct, 11 + at)
    grad_emb = matmul_tn(masked, upstream.astype(low_type))
    vec_list = [jnp.sum(upstream * leading, 0), jnp.sum(upstream, 0)]
    for at in range(layer_total):
        vec_list = vec_list + vec_grads[at]
    grad_vec = jnp.stack(vec_list + [gain_final, shift_final])

    devices = chips * cores
    n_emb = feat_count * width // (devices * 128)
    n_vec = -(-grad_vec.size // (devices * 128))
    emb_part = grad_emb.reshape((devices, n_emb, 128))
    vec_flat = jnp.pad(grad_vec.reshape(-1), (0, n_vec * devices * 128 - grad_vec.size))
    vec_part = vec_flat.reshape((devices, n_vec, 128))
    n_all = 48 if direct else n_emb + n_vec
    small = jnp.concatenate([emb_part, vec_part, jnp.zeros((devices, n_all - n_emb - n_vec, 128), wide_type)], 1)
    head_rows = width // devices
    sums = scatter_grads(
        list(big) + [grad_head, small.astype(low_type)], BY_CORE + (False, False),
        rows_list + [head_rows, n_all], direct, 11)
    parts[0] = sums[:4]
    head_sum, small_sum = sums[4], sums[5].reshape((n_all, 128))

    square = sum(jnp.sum(p * p) for ps in parts for p in ps)
    square = square + jnp.sum(head_sum * head_sum) + jnp.sum(small_sum * small_sum)
    scalars = jnp.stack([square, loss_part, jnp.sum(row_weight)])
    scalars = jnp.broadcast_to(scalars[:, None, None], (3, 8, 128))
    split = PIECES if direct else 1
    head_all, small_all, scalar_all = gather_small(
        [head_sum.reshape((split, head_rows // split, -1)), small_sum.reshape((split, n_all // split, 128)), scalars],
        direct, 10)
    totals = jnp.sum(scalar_all[..., 0, 0], (0, 1))
    pooled = totals[2]
    loss = totals[1] / pooled
    grad_norm = jnp.sqrt(totals[0]) / pooled
    scale = jnp.minimum(1.0, clip_at / grad_norm) / pooled
    grad_head = head_all.reshape(w_head.shape)
    small_all = small_all.reshape((devices, n_all, 128))
    grad_emb = small_all[:, :n_emb].reshape(w_emb.shape)
    grad_vec = small_all[:, n_emb : n_emb + n_vec].reshape(-1)[: vectors.size].reshape(vectors.shape)

    def big_update(weight, moment_old, average, kind):
        grad = jnp.stack([parts[at][kind].reshape(weight.shape[1:]) for at in range(layer_total)])
        return update(weight, moment_old, average, grad, scale)

    e_w, e_m, e_a = update(w_emb, m_emb, a_emb, grad_emb, scale)
    v_w, v_m, v_a = update(vectors, m_vec, a_vec, grad_vec, scale)
    q_w, q_m, q_a = big_update(w_qkv, m_qkv, a_qkv, 0)
    o_w, o_m, o_a = big_update(w_out, m_out, a_out, 1)
    u_w, u_m, u_a = big_update(w_up, m_up, a_up, 2)
    d_w, d_m, d_a = big_update(w_down, m_down, a_down, 3)
    h_w, h_m, h_a = update(w_head, m_head, a_head, grad_head, scale)
    return (
        loss, grad_norm, e_w, e_m, e_a, v_w, v_m, v_a, q_w, q_m, q_a, o_w, o_m, o_a,
        u_w, u_m, u_a, d_w, d_m, d_a, h_w, h_m, h_a,
    )


def solution(mesh):
    tables = [P(("dp", "head"), None, None)] + [P(("dp", "head"), None)] + [P()] + [P(("dp", "head"), None)] * 3
    joined = P(None, "dp", None, "head", None)
    mixed = P(None, "head", "dp", None)
    wide = P(None, ("dp", "head"), None)
    state = [P()] * 6 + [joined] * 3 + [mixed] * 3 + [wide] * 6 + [P()] * 3
    return jax.shard_map(
        shards, mesh=mesh, in_specs=tuple(tables + state), out_specs=tuple([P(), P()] + state), check_vma=False)
```

```python
import functools
import jax
import jax.numpy as jnp
from jax import lax
from jax.sharding import PartitionSpec as P
from jax.experimental import pallas as pl
from jax.experimental.pallas import tpu as pltpu

MESH = pl.DeviceIdType.MESH


class Place:
    def __init__(self):
        self.chip = lax.axis_index("dp")
        self.core = lax.axis_index("head")
        self.x = self.chip % 2
        self.y = (self.chip // 2) % 2
        self.z = self.chip // 4
        z = self.z
        self.z_from = (z, 1 + z % 2, (12 - 2 * z) % 5, 3 - 3 * (z // 2))

    def peer(self, way):
        step = {
            "x": 1 - 2 * self.x,
            "y": 2 - 4 * self.y,
            "u": 4,
            "d": -4,
            "c": 0,
        }[way]
        core = 1 - self.core if way == "c" else self.core
        return (self.chip + step, core)

    def block(self, k, ax, ay):
        sx = self.x if ax == 0 else 1 - self.x
        sy = self.y if ay == 0 else 1 - self.y
        return self.z_from[k] * 4 + sy * 2 + sx


def meet(place):
    barrier = pltpu.get_barrier_semaphore()
    for way in "xyc":
        pl.semaphore_signal(barrier, inc=1, device_id=place.peer(way), device_id_type=MESH)

    @pl.when(place.z < 3)
    def _():
        pl.semaphore_signal(barrier, inc=1, device_id=place.peer("u"), device_id_type=MESH)

    @pl.when(place.z > 0)
    def _():
        pl.semaphore_signal(barrier, inc=1, device_id=place.peer("d"), device_id_type=MESH)

    ends = place.z * (3 - place.z)
    pl.semaphore_wait(barrier, 4 + ends // 2)


def at_block(ref, chip, core, piece, by_core):
    return ref.at[core, chip, piece] if by_core else ref.at[chip, core, piece]


class Gather:
    def __init__(self, by_core, orders, shapes, dtype):
        self.by_core, self.orders, self.shapes, self.dtype = by_core, orders, shapes, dtype
        self.n, self.pieces = len(by_core), max(map(len, orders))

    def in_specs(self):
        return [pl.BlockSpec(memory_space=pl.ANY)] * self.n

    def out_specs(self):
        return [pl.BlockSpec(memory_space=pl.ANY)] * self.n

    def out_shape(self):
        return [
            jax.ShapeDtypeStruct(((2, 16) if bc else (16, 2)) + s, self.dtype)
            for s, bc in zip(self.shapes, self.by_core)]

    def scratch(self):
        n, pieces = self.n, self.pieces
        return [
            pltpu.SemaphoreType.DMA((n, pieces)),
            pltpu.SemaphoreType.DMA((n, pieces, 16)),
            pltpu.SemaphoreType.DMA((n,)),
            pltpu.SemaphoreType.DMA((n, pieces, 4)),
            pltpu.SemaphoreType.DMA((n,)),
        ]

    def steps(self, ins, outs, scratch):
        n, orders = self.n, self.orders
        local_sem, recv, core_recv, send, core_send = scratch
        place = Place()
        me = place.chip
        ways = {"x": 0, "y": 1, "u": 2, "d": 3}

        def slot(a, c, chip):
            return at_block(outs[a], chip, place.core, c, self.by_core[a])

        def copy(a, c, chip, way, src, sems):
            return pltpu.make_async_remote_copy(
                src_ref=src, dst_ref=slot(a, c, chip), send_sem=sems[0], recv_sem=sems[1],
                device_id=place.peer(way), device_id_type=MESH)

        def forward(a, c, order, k, ax, ay):
            chip = place.block(k, ax, ay)
            rel = {"x": ax, "y": ay, "z": k}
            last = max([i for i in range(3) if rel[order[i]] != 0], default=-1)
            src = ins[a].at[c] if last < 0 else slot(a, c, chip)
            for i in range(max(last, 0), 3):
                dim = order[i]
                if dim == "z":
                    sz = place.z_from[k]

                    @pl.when((sz <= place.z) & (place.z < 3))
                    def _():
                        copy(a, c, chip, "u", src, (send.at[a, c, 2], recv.at[a, c, chip])).start()

                    @pl.when((sz >= place.z) & (place.z > 0))
                    def _():
                        copy(a, c, chip, "d", src, (send.at[a, c, 3], recv.at[a, c, chip])).start()
                elif rel[dim] == 0:
                    copy(a, c, chip, dim, src, (send.at[a, c, ways[dim]], recv.at[a, c, chip])).start()
            copy(a, c, chip, "c", src, (core_send.at[a], core_recv.at[a])).start()

        def own(a, c):
            return pltpu.make_async_copy(ins[a].at[c], slot(a, c, me), local_sem.at[a, c])

        def entry(k, ax, ay):
            if (k, ax, ay) == (0, 0, 0):
                meet(place)
            for a in range(n):
                for c, order in enumerate(orders[a]):
                    chip = place.block(k, ax, ay)
                    if (k, ax, ay) != (0, 0, 0):
                        copy(a, c, chip, "x", slot(a, c, chip), (send.at[a, c, 0], recv.at[a, c, chip])).wait_recv()
                    forward(a, c, order, k, ax, ay)
                    if (k, ax, ay) == (0, 0, 0):
                        own(a, c).start()

        def finish():
            for a in range(n):
                for c in range(len(orders[a])):
                    own(a, c).wait()
            for a in range(n):
                whole = outs[a].at[0] if self.by_core[a] else outs[a].at[:, 0]
                pltpu.make_async_remote_copy(
                    src_ref=whole, dst_ref=whole, send_sem=core_send.at[a], recv_sem=core_recv.at[a],
                    device_id=place.peer("c"), device_id_type=MESH).wait()
                for c, order in enumerate(orders[a]):
                    def drain(way, count):
                        lead = outs[a].at[0] if self.by_core[a] else outs[a].at[:, 0]
                        part = lead.at[pl.ds(0, count), c]
                        pltpu.make_async_remote_copy(
                            src_ref=part, dst_ref=part, send_sem=send.at[a, c, ways[way]],
                            recv_sem=recv.at[a, c, 0],
                            device_id=place.peer("c"), device_id_type=MESH).wait_send()
                    before = 1
                    for dim in order:
                        if dim == "z":
                            for zz in range(4):
                                @pl.when(place.z == zz)
                                def _(zz=zz, before=before):
                                    if zz < 3:
                                        drain("u", before * (zz + 1))
                                    if zz > 0:
                                        drain("d", before * (4 - zz))
                            before *= 4
                        else:
                            drain(dim, before)
                            before *= 2

        entries = sorted(
            [(k, ax, ay) for k in range(4) for ax in range(2) for ay in range(2)], key=lambda e: e[0] + e[1] + e[2])
        return [functools.partial(entry, *e) for e in entries] + [finish]


class Reduce:
    def __init__(self, by_core, orders, shapes):
        self.by_core, self.orders, self.shapes = by_core, orders, shapes
        self.n, self.pieces = len(by_core), max(map(len, orders))

    def in_specs(self):
        return [pl.BlockSpec(memory_space=pl.ANY)] * self.n

    def out_specs(self):
        return [pl.BlockSpec(memory_space=pltpu.VMEM)] * self.n

    def out_shape(self):
        return [jax.ShapeDtypeStruct(s, jnp.float32) for s in self.shapes]

    def room(self, a, way):
        most = 1
        for order in self.orders[a]:
            if way in "ud":
                most = max(most, 4 if order[0] == "z" else 8)
            else:
                most = max(most, {2: 8, 1: 4, 0: 1}[order.index(way)])
        return most

    def scratch(self):
        n, pieces = self.n, self.pieces
        buffers = []
        for sizes in ([16] * n, [16] * n, *[[self.room(a, w) for a in range(n)] for w in "xyud"]):
            buffers += [pltpu.VMEM((k,) + s, jnp.bfloat16) for k, s in zip(sizes, self.shapes)]
        return buffers + [
            pltpu.SemaphoreType.DMA((n,)),
            pltpu.SemaphoreType.DMA((n, pieces, 16)),
            pltpu.SemaphoreType.DMA((n, pieces)),
            pltpu.SemaphoreType.DMA((n, pieces, 4, 8)),
            pltpu.SemaphoreType.DMA((n, pieces, 4)),
        ]

    def steps(self, ins, outs, scratch):
        n, orders, by_core = self.n, self.orders, self.by_core
        mine, other = scratch[:n], scratch[n : 2 * n]
        got = {w: scratch[(2 + i) * n : (3 + i) * n] for i, w in enumerate("xyud")}
        load_sem, core_recv, core_send, recv, send = scratch[6 * n :]
        ways = {"x": 0, "y": 1, "u": 2, "d": 3}
        place = Place()

        def number(at):
            sx, sy, sz = at
            return sz * 4 + sy * 2 + sx

        def load(a):
            src = ins[a].at[place.core] if by_core[a] else ins[a].at[:, place.core]
            return pltpu.make_async_copy(src, mine[a], load_sem.at[a])

        def to_core(a, c, at):
            chip = number(at)
            return pltpu.make_async_remote_copy(
                src_ref=at_block(ins[a], chip, 1 - place.core, c, by_core[a]), dst_ref=other[a].at[chip, c],
                send_sem=core_send.at[a, c], recv_sem=core_recv.at[a, c, chip],
                device_id=place.peer("c"), device_id_type=MESH)

        def landing(order, at, way):
            sx, sy, sz = at
            if way in "ud":
                return sz if order[0] == "z" else sz * 2 + (sx if order[0] == "x" else sy)
            turn = order.index(way)
            return (0, sz, sz * 2 + (sx if way == "y" else sy))[turn]

        def hop(a, c, order, at, way):
            spot = landing(order, at, way)
            return pltpu.make_async_remote_copy(
                src_ref=mine[a].at[number(at), c], dst_ref=got[way][a].at[spot, c],
                send_sem=send.at[a, c, ways[way]], recv_sem=recv.at[a, c, ways[way], spot],
                device_id=place.peer(way), device_id_type=MESH)

        def take(a, c, order, at, way):
            hop(a, c, order, at, way).wait_recv()
            mine[a][number(at), c] = mine[a][number(at), c] + got[way][a][landing(order, at, way), c]

        def fold(a, c, at):
            to_core(a, c, at).wait_recv()
            chip = number(at)
            mine[a][chip, c] = mine[a][chip, c] + other[a][chip, c]

        items = [(a, c, order) for a in range(n) for c, order in enumerate(orders[a])]
        lined = [it for it in items if it[2][1] == "z"]
        flat = [it for it in items if it[2][0] == "z"]
        items = lined + flat

        def side(dim, far):
            m = place.x if dim == "x" else place.y
            return 1 - m if far else m

        def spot(order, wave, i, far):
            sz = wave + (3 - 2 * wave) * (i // 2)
            if order[2] == "y":
                return (i % 2, side("y", far), sz)
            return (side("x", far), i % 2, sz)

        def loop(count, body):
            def run(i, carry):
                body(i)
                return carry
            lax.fori_loop(0, count, run, 0)

        def start(wave, far):
            for a, c, order in items:
                loop(4, lambda i: to_core(a, c, spot(order, wave, i, far)).start())

        def begin():
            meet(place)
            for a in range(n):
                load(a).start()
            for wave, far in ((0, True), (0, False), (1, True), (1, False)):
                start(wave, far)
            for a in range(n):
                load(a).wait()

        def far(wave):
            for a, c, order in items:
                def one(i):
                    at = spot(order, wave, i, True)
                    fold(a, c, at)
                    hop(a, c, order, at, order[2]).start()
                loop(4, one)

        def near(wave):
            for a, c, order in items:
                loop(4, lambda i: fold(a, c, spot(order, wave, i, False)))

        def second(it, wave):
            a, c, order = it
            if order[1] == "z":
                loop(4, lambda i: take(a, c, order, spot(order, wave, i, False), order[2]))
                return
            for away in (True, False):
                def one(i):
                    sz = wave + (3 - 2 * wave) * i
                    at = (side("x", away and order[1] == "x"), side("y", away and order[1] == "y"), sz)
                    take(a, c, order, at, order[2])
                    if away:
                        hop(a, c, order, at, order[1]).start()
                loop(2, one)

        def third(it, wave):
            a, c, order = it
            loop(2, lambda i: take(a, c, order, (place.x, place.y, wave + (3 - 2 * wave) * i), order[1]))

        def here(order):
            if order[0] == "z":
                return [(place.x, place.y)]
            return [(side("x", order[0] == "x"), side("y", order[0] == "y")), (place.x, place.y)]

        def line(it, j):
            a, c, order = it
            for way, target, active, inner in (
                ("u", 3 - j, place.z < 3 - j, place.z > 0),
                ("d", j, place.z > j, place.z < 3),
            ):
                @pl.when(active)
                def _():
                    for sx, sy in here(order):
                        at = (sx, sy, target)

                        @pl.when(inner)
                        def _():
                            take(a, c, order, at, way)
                        hop(a, c, order, at, way).start()

        def owned(it):
            a, c, order = it
            for first, (sx, sy) in enumerate(here(order)):
                at = (sx, sy, place.z)

                @pl.when(place.z > 0)
                def _():
                    take(a, c, order, at, "u")

                @pl.when(place.z < 3)
                def _():
                    take(a, c, order, at, "d")
                if order[0] != "z" and first == 0:
                    hop(a, c, order, at, order[0]).start()

        def last(it):
            a, c, order = it
            if order[0] != "z":
                take(a, c, order, (place.x, place.y, place.z), order[0])
            outs[a][c] = mine[a][place.chip, c].astype(jnp.float32)

        def drain(a, c, sem, count):
            part = other[a].at[pl.ds(0, count), c]
            pltpu.make_async_remote_copy(
                src_ref=part, dst_ref=part, send_sem=sem, recv_sem=recv.at[a, c, 0, 0],
                device_id=place.peer("c"), device_id_type=MESH).wait_send()

        def finish():
            for it in lined:
                last(it)
            for a, c, order in items:
                drain(a, c, core_send.at[a, c], 16)
                left = 16
                for turn in (2, 1, 0):
                    dim = order[turn]
                    if dim == "z":
                        left //= 4
                        for zz in range(4):
                            @pl.when(place.z == zz)
                            def _(zz=zz, left=left):
                                if zz < 3:
                                    drain(a, c, send.at[a, c, 2], left * (3 - zz))
                                if zz > 0:
                                    drain(a, c, send.at[a, c, 3], left * zz)
                    else:
                        left //= 2
                        drain(a, c, send.at[a, c, ways[dim]], left)

        part = functools.partial
        out = [begin, part(far, 0), part(near, 0), part(far, 1)]
        for it in lined:
            out += [part(second, it, 0), part(line, it, 0)]
        out += [part(second, it, 0) for it in flat]
        out += [part(near, 1)]
        for i, it in enumerate(lined):
            out += [part(second, it, 1), part(line, it, 1), part(line, it, 2)]
            if i == 0:
                for fl in flat:
                    out += [part(third, fl, 0), part(line, fl, 0)]
        if not lined:
            for fl in flat:
                out += [part(third, fl, 0), part(line, fl, 0)]
        out += [part(second, it, 1) for it in flat]
        out += [part(owned, it) for it in lined]
        for it in flat:
            out += [part(third, it, 1), part(line, it, 1), part(line, it, 2), part(owned, it), part(last, it)]
        return out + [finish]


VMEM_ALL = 64 * 1024 * 1024 - 65536


class Aside:
    def __init__(self, plan, arrays, collective_id):
        self.plan, self.arrays, self.collective_id = plan, arrays, collective_id


def with_aside(body, aside, *, grid, in_specs, out_specs, out_shape, scratch_shapes=(), cost, operands):
    if aside is None:
        out = pl.pallas_call(
            body, grid=grid, in_specs=in_specs, out_specs=out_specs, out_shape=tuple(out_shape),
            scratch_shapes=scratch_shapes, cost_estimate=cost,
            compiler_params=pltpu.CompilerParams(vmem_limit_bytes=VMEM_ALL))(*operands)
        return out, None
    plan = aside.plan
    n_in, n_out, n_scr, n = len(in_specs), len(out_specs), len(scratch_shapes), plan.n
    cells = 1
    for extent in grid:
        cells *= extent

    def kernel(*refs):
        refs = list(refs)
        ins, refs = refs[:n_in], refs[n_in:]
        plan_ins, refs = refs[:n], refs[n:]
        outs, refs = refs[:n_out], refs[n_out:]
        plan_outs, refs = refs[:n], refs[n:]
        scratch, plan_scratch = refs[:n_scr], refs[n_scr:]
        steps = plan.steps(plan_ins, plan_outs, plan_scratch)
        cell = 0
        for axis, extent in enumerate(grid):
            cell = cell * extent + pl.program_id(axis)
        by_cell = {}
        for i, step in enumerate(steps):
            by_cell.setdefault(i * (cells - 1) // (len(steps) - 1), []).append(step)
        for index in sorted(by_cell):
            if index < cells - 1:
                @pl.when(cell == index)
                def _():
                    for step in by_cell[index]:
                        step()
        body(*ins, *outs, *scratch)

        @pl.when(cell == cells - 1)
        def _():
            for step in by_cell[cells - 1]:
                step()

    out = pl.pallas_call(
        kernel, grid=grid,
        in_specs=list(in_specs) + plan.in_specs(), out_specs=list(out_specs) + plan.out_specs(),
        out_shape=tuple(out_shape) + tuple(plan.out_shape()),
        scratch_shapes=list(scratch_shapes) + plan.scratch(), cost_estimate=cost,
        compiler_params=pltpu.CompilerParams(
            collective_id=aside.collective_id, has_side_effects=True, vmem_limit_bytes=VMEM_ALL),
    )(*operands, *aside.arrays)
    return out[:n_out], out[n_out:]


def exchange(plan, arrays, collective_id):
    n = plan.n

    def kernel(*refs):
        for step in plan.steps(refs[:n], refs[n : 2 * n], refs[2 * n :]):
            step()

    moved = sum(a.size for a in arrays) * 2
    return pl.pallas_call(
        kernel,
        out_shape=tuple(plan.out_shape()),
        in_specs=plan.in_specs(),
        out_specs=plan.out_specs(),
        scratch_shapes=plan.scratch(),
        compiler_params=pltpu.CompilerParams(
            collective_id=collective_id, has_side_effects=True, vmem_limit_bytes=VMEM_ALL),
        cost_estimate=pl.CostEstimate(flops=0, bytes_accessed=32 * moved, transcendentals=0),
    )(*arrays)


def gather_plan(arrays, by_core, orders):
    return Gather(by_core, orders, [a.shape for a in arrays], arrays[0].dtype)


def reduce_plan(arrays, by_core, orders):
    return Reduce(by_core, orders, [a.shape[2:] for a in arrays])


def all_gather_layer(arrays, by_core, orders, collective_id):
    return exchange(gather_plan(arrays, by_core, orders), arrays, collective_id)


def reduce_scatter_layer(arrays, by_core, orders, collective_id):
    return exchange(reduce_plan(arrays, by_core, orders), arrays, collective_id)


HD = 64
CTX = 768

eps_norm = 1e-05
clip_at = 0.01
rate = 3000.0
moment = 0.9
keep_avg = 0.9
decay_wd = 1e-05
low_type = jnp.bfloat16
wide_type = jnp.float32


def layer_norm(values, gain_row, shift_row):
    center = values - jnp.mean(values, -1, keepdims=True)
    spread = jnp.mean(center * center, -1, keepdims=True)
    return center * lax.rsqrt(spread + eps_norm) * gain_row + shift_row


def norm_back(values, gain_row, shift_row, upstream):
    _, pull = jax.vjp(layer_norm, values, gain_row, shift_row)
    return pull(upstream)


def gelu_back(values, upstream):
    _, pull = jax.vjp(jax.nn.gelu, values)
    return pull(upstream)[0]


def matmul(first_op, second_op):
    return jnp.dot(first_op, second_op, preferred_element_type=wide_type)


def contract(first_op, second_op, first_dim, second_dim):
    return lax.dot_general(
        first_op, second_op, (((first_dim,), (second_dim,)), ((), ())), preferred_element_type=wide_type
    )


def matmul_tn(first_op, second_op):
    return contract(first_op, second_op, 0, 0)


def matmul_nt(first_op, second_op):
    return contract(first_op, second_op, 1, 1)


def head_lanes(shape, head):
    lane = lax.broadcasted_iota(jnp.int32, shape, 1)
    mine = (lane < HD) if head == 0 else (lane >= HD)
    return mine, lane == (HD if head == 0 else 0)


def attend_kernel(q_ref, k_ref, v_ref, bias_ref, out_ref, lse_ref):
    q_block = q_ref[0] * jnp.asarray(HD ** -0.5, low_type)
    k_block, v_block, bias = k_ref[0], v_ref[0], bias_ref[...]
    v_turned = v_block.T
    parts = []
    for head in range(2):
        q_mine, q_one = head_lanes(q_block.shape, head)
        k_mine, _ = head_lanes(k_block.shape, head)
        one = jnp.where(q_one, jnp.ones_like(q_block), jnp.zeros_like(q_block))
        score = matmul_nt(jnp.where(k_mine, k_block, bias), jnp.where(q_mine, q_block, one))
        peak = jnp.max(score, 0, keepdims=True)
        lifted = jnp.exp(score - peak)
        total = jnp.sum(lifted, 0, keepdims=True)
        mixed = matmul(v_turned[head * HD : (head + 1) * HD], lifted.astype(low_type))
        parts.append(mixed / total)
        lse_ref[0, head : head + 1, :] = peak + jnp.log(total)
    out_ref[...] = jnp.concatenate(parts, 0).T.astype(low_type)


def attend(queries, keys_values, bias, aside):
    groups, rows, width = queries.shape
    pairs = width // 128
    block = min(256, rows)
    grid = (groups * pairs, rows // block)
    (mixed, lse), extra = with_aside(
        attend_kernel,
        aside,
        grid=grid,
        in_specs=[
            pl.BlockSpec((1, block, 128), lambda p, i: (p // pairs, i, p % pairs)),
            pl.BlockSpec((1, CTX, 128), lambda p, i: (p // pairs, 0, p % pairs)),
            pl.BlockSpec((1, CTX, 128), lambda p, i: (p // pairs, 0, pairs + p % pairs)),
            pl.BlockSpec((CTX, 128), lambda p, i: (0, 0)),
        ],
        out_specs=[
            pl.BlockSpec((block, 128), lambda p, i: (i, p)),
            pl.BlockSpec((1, 2, block), lambda p, i: (p, 0, i)),
        ],
        out_shape=(
            jax.ShapeDtypeStruct((rows, groups * width), low_type),
            jax.ShapeDtypeStruct((groups * pairs, 2, rows), wide_type),
        ),
        cost=pl.CostEstimate(
            flops=4 * rows * CTX * groups * width, bytes_accessed=8 * rows * groups * width,
            transcendentals=rows * CTX * groups * width // HD),
        operands=(queries, keys_values, keys_values, bias),
    )
    return mixed, lse, extra


def attend_back_kernel(q_ref, k_ref, v_ref, bias_ref, g_ref, o_ref, lse_ref, gq_ref, gk_ref, gv_ref, k_sum, v_sum):
    step = pl.program_id(1)

    @pl.when(step == 0)
    def _():
        k_sum[...] = jnp.zeros_like(k_sum)
        v_sum[...] = jnp.zeros_like(v_sum)

    scale = HD ** -0.5
    q_block = q_ref[0] * jnp.asarray(scale, low_type)
    k_block, v_block, bias = k_ref[0], v_ref[0], bias_ref[...]
    g_block = g_ref[...]
    k_turned = k_block.T
    both = (g_block.astype(wide_type) * o_ref[...].astype(wide_type)).T
    parts = []
    for head in range(2):
        q_mine, q_one = head_lanes(q_block.shape, head)
        k_mine, _ = head_lanes(k_block.shape, head)
        nothing = jnp.zeros_like(q_block)
        one = jnp.where(q_one, jnp.ones_like(q_block), nothing)
        score = matmul_nt(jnp.where(k_mine, k_block, bias), jnp.where(q_mine, q_block, one))
        prob = jnp.exp(score - lse_ref[0, head : head + 1, :])
        g_mine = jnp.where(q_mine, g_block, nothing)
        grad_prob = matmul_nt(v_block, g_mine)
        inner = jnp.sum(both[head * HD : (head + 1) * HD], 0, keepdims=True)
        grad_score = (prob * (grad_prob - inner)).astype(low_type)
        v_sum[...] += matmul(prob.astype(low_type), g_mine)
        k_sum[...] += matmul(grad_score, jnp.where(q_mine, q_block, nothing))
        parts.append(matmul(k_turned[head * HD : (head + 1) * HD], grad_score) * scale)
    gq_ref[0] = jnp.concatenate(parts, 0).T.astype(low_type)

    @pl.when(step == pl.num_programs(1) - 1)
    def _():
        gk_ref[0] = k_sum[...].astype(low_type)
        gv_ref[0] = v_sum[...].astype(low_type)


def attend_back(queries, keys_values, bias, grad_mixed, mixed, lse, aside):
    groups, rows, width = queries.shape
    pairs = width // 128
    block = min(256, rows)
    grid = (groups * pairs, rows // block)
    row_spec = pl.BlockSpec((block, 128), lambda p, i: (i, p))
    key_out = pl.BlockSpec((1, CTX, 128), lambda p, i: (p // pairs, 0, p % pairs))
    grads, extra = with_aside(
        attend_back_kernel,
        aside,
        grid=grid,
        in_specs=[
            pl.BlockSpec((1, block, 128), lambda p, i: (p // pairs, i, p % pairs)),
            pl.BlockSpec((1, CTX, 128), lambda p, i: (p // pairs, 0, p % pairs)),
            pl.BlockSpec((1, CTX, 128), lambda p, i: (p // pairs, 0, pairs + p % pairs)),
            pl.BlockSpec((CTX, 128), lambda p, i: (0, 0)),
            row_spec,
            row_spec,
            pl.BlockSpec((1, 2, block), lambda p, i: (p, 0, i)),
        ],
        out_specs=[
            pl.BlockSpec((1, block, 128), lambda p, i: (p // pairs, i, p % pairs)),
            key_out,
            key_out,
        ],
        out_shape=(
            jax.ShapeDtypeStruct(queries.shape, low_type),
            jax.ShapeDtypeStruct((groups, CTX, width), low_type),
            jax.ShapeDtypeStruct((groups, CTX, width), low_type),
        ),
        scratch_shapes=[pltpu.VMEM((CTX, 128), wide_type)] * 2,
        cost=pl.CostEstimate(
            flops=10 * rows * CTX * groups * width, bytes_accessed=16 * rows * groups * width,
            transcendentals=rows * CTX * groups * width // HD),
        operands=(queries, keys_values, keys_values, bias, grad_mixed, mixed, lse),
    )
    return tuple(grads) + (extra,)


def grouped(rows, weight):
    return jnp.einsum("rd,gdc->grc", rows, weight, preferred_element_type=wide_type)


def layer_forward(residual, first, vec_rows, weights, bias, aside):
    w_joined, w_mix, w_grow, w_shrink = weights
    width = w_joined.shape[2] // 3
    normed = layer_norm(residual, vec_rows[0], vec_rows[1]).astype(low_type)
    queries = grouped(normed[first:], w_joined[:, :, :width]).astype(low_type)
    keys_values = grouped(normed[:CTX], w_joined[:, :, width:]).astype(low_type)
    mixed, lse, extra = attend(queries, keys_values, bias, aside)
    middle = residual[first:] + matmul(mixed, w_mix) + vec_rows[4]
    normed_mlp = layer_norm(middle, vec_rows[2], vec_rows[3]).astype(low_type)
    hidden = matmul(normed_mlp, w_grow)
    active = jax.nn.gelu(hidden).astype(low_type)
    output = middle + matmul(active, w_shrink) + vec_rows[5]
    return output, extra, (residual, normed, queries, keys_values, mixed, lse, middle, normed_mlp, hidden, active)


def layer_backward(upstream, kept, first, vec_rows, weights, bias, aside):
    w_joined, w_mix, w_grow, w_shrink = weights
    width = w_joined.shape[2] // 3
    residual, normed, queries, keys_values, mixed, lse, middle, normed_mlp, hidden, active = kept
    down_low = upstream.astype(low_type)
    grad_shrink = matmul_tn(active, down_low).astype(low_type)
    grad_hidden = gelu_back(hidden, matmul_nt(down_low, w_shrink)).astype(low_type)
    grad_grow = matmul_tn(normed_mlp, grad_hidden).astype(low_type)
    grad_middle, gain_mlp, shift_mlp = norm_back(
        middle, vec_rows[2], vec_rows[3], matmul_nt(grad_hidden, w_grow))
    grad_middle = grad_middle + upstream
    mix_low = grad_middle.astype(low_type)
    grad_mix = matmul_tn(mixed, mix_low).astype(low_type)
    grad_mixed = matmul_nt(mix_low, w_mix).astype(low_type)
    grad_q, grad_k, grad_v, extra = attend_back(queries, keys_values, bias, grad_mixed, mixed, lse, aside)

    def weight_grad(rows, grads):
        return jnp.einsum("rd,grc->gdc", rows, grads, preferred_element_type=wide_type).astype(low_type)

    def row_grad(grads, part):
        return jnp.einsum(
            "grc,gdc->rd", grads, w_joined[:, :, part * width : (part + 1) * width], preferred_element_type=wide_type)

    grad_joined = jnp.concatenate(
        [weight_grad(normed[first:], grad_q), weight_grad(normed[:CTX], grad_k), weight_grad(normed[:CTX], grad_v)], 2)
    from_q = row_grad(grad_q, 0)
    from_kv = row_grad(grad_k, 1) + row_grad(grad_v, 2)
    rows = residual.shape[0]
    below = jnp.zeros((first, from_q.shape[1]), wide_type)
    tail = jnp.zeros((rows - CTX, from_q.shape[1]), wide_type)
    grad_normed = jnp.concatenate([below, from_q], 0) + jnp.concatenate([from_kv, tail], 0)
    grad_input, gain_attn, shift_attn = norm_back(residual, vec_rows[0], vec_rows[1], grad_normed)
    vec_grads = [gain_attn, shift_attn, gain_mlp, shift_mlp, jnp.sum(grad_middle, 0), jnp.sum(upstream, 0)]
    grad_out = grad_input + jnp.concatenate([below, grad_middle], 0)
    return grad_out, extra, (grad_joined, grad_mix, grad_grow, grad_shrink), vec_grads


def update(weight, moment_old, average, grad_in, scale):
    applied = grad_in * scale + decay_wd * weight
    moment_new = moment * moment_old + applied
    weight_new = weight - rate * (applied + moment * moment_new)
    return (weight_new, moment_new, keep_avg * average + (1.0 - keep_avg) * weight_new)


BY_CORE = (True, True, False, False)
ROUTES = (("zxy",), ("zxy",), ("xzy",), ("yzx",))
HALVES = (("zxy", "zyx"),)


def whole_gather(shard_list, by_core):
    return [
        lax.all_gather(lax.all_gather(shard, "dp", axis=0), "head", axis=0 if bc else 1)
        for shard, bc in zip(shard_list, by_core)]


def as_blocks(grads, by_core, rows_list, routes):
    chips, cores = lax.axis_size("dp"), lax.axis_size("head")
    return [
        grad.reshape(((cores, chips) if bc else (chips, cores)) + (len(route), rows // len(route), -1))
        for grad, bc, rows, route in zip(grads, by_core, rows_list, routes)]


def whole_scatter(grads, by_core, rows_list):
    outs = []
    for grad, bc in zip(as_blocks(grads, by_core, rows_list, ROUTES + (("zyx",),)), by_core):
        half = lax.psum_scatter(grad.astype(wide_type), "head", scatter_dimension=0 if bc else 1)
        outs.append(lax.psum_scatter(half, "dp", scatter_dimension=0))
    return outs


def shards(
    rows_in, feat_mask, counts, ctx_vals, targets, query_mask,
    w_emb, m_emb, a_emb, vectors, m_vec, a_vec,
    w_qkv, m_qkv, a_qkv, w_out, m_out, a_out, w_up, m_up, a_up, w_down, m_down, a_down,
    w_head, m_head, a_head,
):
    chips, cores = lax.axis_size("dp"), lax.axis_size("head")
    direct = (chips, cores) == (16, 2)
    _, row_count, feat_count = rows_in.shape
    layer_total = w_qkv.shape[0]
    width = w_emb.shape[1]
    joined_rows = w_qkv.shape[1]
    kinds = w_qkv.shape[2] * w_qkv.shape[4]

    def own_weights(at):
        return [
            w_qkv[at].reshape((joined_rows, kinds)).astype(low_type)[None],
            w_out[at, 0].astype(low_type)[None],
            w_up[at].astype(low_type)[None],
            w_down[at].astype(low_type)[None],
        ]

    def as_weights(gathered):
        qkv, out, up, down = gathered
        return (
            qkv.reshape((cores, width, kinds)),
            out.reshape((width, width)),
            up.reshape((width, -1)),
            down.reshape((-1, width)),
        )

    own = [own_weights(at) for at in range(layer_total)]
    forward_aside = [None] * layer_total
    if direct:
        got = all_gather_layer(own[0] + own[1][:2], BY_CORE + BY_CORE[:2], ROUTES + (("zyx",), ("zyx",)), 1)
        gathered = [list(got[:4]), list(got[4:])]
        last_two = own[1][2:]
        forward_aside[0] = Aside(gather_plan(last_two, BY_CORE[2:], (("zxy",), ("zyx",))), last_two, 2)
    else:
        gathered = [whole_gather(o, BY_CORE) for o in own]

    table = lax.axis_index("dp") * cores + lax.axis_index("head")
    count = lax.dynamic_slice_in_dim(counts, table, 1, 0)
    bias = jnp.where(jnp.arange(CTX) < count, 0.0, -1e30).astype(low_type)
    bias = jnp.broadcast_to(bias[:, None], (CTX, 128))
    masked = rows_in[0] * feat_mask[0][None, :].astype(low_type)
    leading = jnp.concatenate([ctx_vals[0], jnp.zeros((row_count - CTX,), wide_type)])[:, None]
    residual = matmul(masked, w_emb.astype(low_type)) + vectors[1] + leading * vectors[0]
    kept_all = []
    weights = []
    for at in range(layer_total):
        first = CTX if at == layer_total - 1 else 0
        weights.append(as_weights(gathered[at]))
        residual, extra, kept = layer_forward(
            residual, first, vectors[2 + 6 * at : 8 + 6 * at], weights[at], bias, forward_aside[at])
        if extra is not None:
            gathered[at + 1] += list(extra)
        kept_all.append(kept)

    head_low = w_head.astype(low_type)
    final_rows = layer_norm(residual, vectors[-2], vectors[-1]).astype(low_type)
    logits = matmul(final_rows, head_low)
    row_peak = jnp.max(logits, -1, keepdims=True)
    log_total = row_peak[:, 0] + jnp.log(jnp.sum(jnp.exp(logits - row_peak), -1))
    target_hit = (jnp.arange(logits.shape[1])[None, :] == targets[0][:, None]).astype(wide_type)
    picked = jnp.sum(logits * target_hit, -1)
    row_weight = query_mask[0].astype(wide_type)
    loss_part = jnp.sum((log_total - picked) * row_weight)
    grad_logits = ((jnp.exp(logits - log_total[:, None]) - target_hit) * row_weight[:, None]).astype(low_type)
    grad_head = matmul_tn(final_rows, grad_logits).astype(low_type)
    upstream, gain_final, shift_final = norm_back(
        residual, vectors[-2], vectors[-1], matmul_nt(grad_logits, head_low))

    rows_list = [joined_rows, w_out.shape[2], w_up.shape[1], w_down.shape[1]]
    sums = [None] * layer_total
    vec_grads = [None] * layer_total
    aside = None
    for at in reversed(range(layer_total)):
        first = CTX if at == layer_total - 1 else 0
        upstream, extra, big, vec_grads[at] = layer_backward(
            upstream, kept_all[at], first, vectors[2 + 6 * at : 8 + 6 * at], weights[at], bias, aside)
        if extra is not None:
            sums[at + 1] = extra
        if at > 0 and direct:
            blocks = as_blocks(big, BY_CORE, rows_list, ROUTES)
            aside = Aside(reduce_plan(blocks, BY_CORE, ROUTES), blocks, 3)
        elif at > 0:
            sums[at] = whole_scatter(big, BY_CORE, rows_list)
    grad_emb = matmul_tn(masked, upstream.astype(low_type))
    vec_list = [jnp.sum(upstream * leading, 0), jnp.sum(upstream, 0)]
    for at in range(layer_total):
        vec_list = vec_list + vec_grads[at]
    grad_vec = jnp.stack(vec_list + [gain_final, shift_final])

    devices = chips * cores
    n_head, n_emb = w_head.size // (devices * 128), w_emb.size // (devices * 128)
    n_vec = -(-vectors.size // (devices * 128))
    vec_flat = jnp.pad(grad_vec.astype(low_type).reshape(-1), (0, n_vec * devices * 128 - vectors.size))
    used = n_head + n_emb + n_vec
    n_all = -(-(used + 1) // 32) * 32
    small = jnp.concatenate([
        grad_head.reshape((devices, n_head, 128)),
        grad_emb.astype(low_type).reshape((devices, n_emb, 128)),
        vec_flat.reshape((devices, n_vec, 128)),
        jnp.zeros((devices, n_all - used, 128), low_type)], 1)
    last_grads, last_rows, last_core = list(big) + [small], rows_list + [n_all], BY_CORE + (False,)
    if direct:
        routes = ROUTES + (("zyx",),)
        blocks = as_blocks(last_grads, last_core, last_rows, routes)
        *sums[0], small_sum = reduce_scatter_layer(blocks, last_core, routes, 4)
    else:
        *sums[0], small_sum = whole_scatter(last_grads, last_core, last_rows)
    small_sum = small_sum.reshape((n_all, 128))

    square = sum(jnp.sum(p * p) for ps in sums for p in ps) + jnp.sum(small_sum * small_sum)
    scalars = jnp.pad(jnp.stack([square, loss_part, jnp.sum(row_weight)]), (0, 125))
    small_sum = jnp.concatenate([small_sum[: n_all - 1], scalars[None]], 0)
    if direct:
        small_all = all_gather_layer([small_sum.reshape((2, n_all // 2, 128))], (False,), HALVES, 5)[0]
    else:
        small_all = whole_gather([small_sum], (False,))[0]
    small_all = small_all.reshape((devices, n_all, 128))
    totals = jnp.sum(small_all[:, n_all - 1, :3], 0)
    pooled = totals[2]
    loss = totals[1] / pooled
    grad_norm = jnp.sqrt(totals[0]) / pooled
    scale = jnp.minimum(1.0, clip_at / grad_norm) / pooled
    grad_head = small_all[:, :n_head].reshape(w_head.shape)
    grad_emb = small_all[:, n_head : n_head + n_emb].reshape(w_emb.shape)
    grad_vec = small_all[:, n_head + n_emb : used].reshape(-1)[: vectors.size].reshape(vectors.shape)

    def big_update(weight, moment_old, average, kind):
        grad = jnp.stack([sums[at][kind].reshape(weight.shape[1:]) for at in range(layer_total)])
        return update(weight, moment_old, average, grad, scale)

    e_w, e_m, e_a = update(w_emb, m_emb, a_emb, grad_emb, scale)
    v_w, v_m, v_a = update(vectors, m_vec, a_vec, grad_vec, scale)
    q_w, q_m, q_a = big_update(w_qkv, m_qkv, a_qkv, 0)
    o_w, o_m, o_a = big_update(w_out, m_out, a_out, 1)
    u_w, u_m, u_a = big_update(w_up, m_up, a_up, 2)
    d_w, d_m, d_a = big_update(w_down, m_down, a_down, 3)
    h_w, h_m, h_a = update(w_head, m_head, a_head, grad_head, scale)
    return (
        loss, grad_norm, e_w, e_m, e_a, v_w, v_m, v_a, q_w, q_m, q_a, o_w, o_m, o_a,
        u_w, u_m, u_a, d_w, d_m, d_a, h_w, h_m, h_a,
    )


def solution(mesh):
    tables = [P(("dp", "head"), None, None)] + [P(("dp", "head"), None)] + [P()] + [P(("dp", "head"), None)] * 3
    joined = P(None, "dp", None, "head", None)
    mixed = P(None, "head", "dp", None)
    wide = P(None, ("dp", "head"), None)
    state = [P()] * 6 + [joined] * 3 + [mixed] * 3 + [wide] * 6 + [P()] * 3
    return jax.shard_map(
        shards, mesh=mesh, in_specs=tuple(tables + state), out_specs=tuple([P(), P()] + state), check_vma=False)
```

```python
import functools
import jax
import jax.numpy as jnp
from jax import lax
from jax.sharding import PartitionSpec as P
from jax.experimental import pallas as pl
from jax.experimental.pallas import tpu as pltpu

MESH = pl.DeviceIdType.MESH


class Place:
    def __init__(self):
        self.chip = lax.axis_index("dp")
        self.core = lax.axis_index("head")
        self.x = self.chip % 2
        self.y = (self.chip // 2) % 2
        self.z = self.chip // 4
        z = self.z
        self.z_from = (z, 1 + z % 2, (12 - 2 * z) % 5, 3 - 3 * (z // 2))

    def peer(self, way):
        step = {
            "x": 1 - 2 * self.x,
            "y": 2 - 4 * self.y,
            "u": 4,
            "d": -4,
            "c": 0,
        }[way]
        core = 1 - self.core if way == "c" else self.core
        return (self.chip + step, core)

    def block(self, k, ax, ay):
        sx = self.x if ax == 0 else 1 - self.x
        sy = self.y if ay == 0 else 1 - self.y
        return self.z_from[k] * 4 + sy * 2 + sx


def meet(place):
    barrier = pltpu.get_barrier_semaphore()
    for way in "xyc":
        pl.semaphore_signal(barrier, inc=1, device_id=place.peer(way), device_id_type=MESH)

    @pl.when(place.z < 3)
    def _():
        pl.semaphore_signal(barrier, inc=1, device_id=place.peer("u"), device_id_type=MESH)

    @pl.when(place.z > 0)
    def _():
        pl.semaphore_signal(barrier, inc=1, device_id=place.peer("d"), device_id_type=MESH)

    ends = place.z * (3 - place.z)
    pl.semaphore_wait(barrier, 4 + ends // 2)


def at_block(ref, chip, core, piece, by_core):
    return ref.at[core, chip, piece] if by_core else ref.at[chip, core, piece]


class Gather:
    def __init__(self, by_core, orders, shapes, dtype):
        self.by_core, self.orders, self.shapes, self.dtype = by_core, orders, shapes, dtype
        self.n, self.pieces = len(by_core), max(map(len, orders))

    def in_specs(self):
        return [pl.BlockSpec(memory_space=pl.ANY)] * self.n

    def out_specs(self):
        return [pl.BlockSpec(memory_space=pl.ANY)] * self.n

    def out_shape(self):
        return [
            jax.ShapeDtypeStruct(((2, 16) if bc else (16, 2)) + s, self.dtype)
            for s, bc in zip(self.shapes, self.by_core)]

    def scratch(self):
        n, pieces = self.n, self.pieces
        return [
            pltpu.SemaphoreType.DMA((n, pieces)),
            pltpu.SemaphoreType.DMA((n, pieces, 16)),
            pltpu.SemaphoreType.DMA((n,)),
            pltpu.SemaphoreType.DMA((n, pieces, 4)),
            pltpu.SemaphoreType.DMA((n,)),
        ]

    def steps(self, ins, outs, scratch):
        n, orders = self.n, self.orders
        local_sem, recv, core_recv, send, core_send = scratch
        place = Place()
        me = place.chip
        ways = {"x": 0, "y": 1, "u": 2, "d": 3}

        def slot(a, c, chip):
            return at_block(outs[a], chip, place.core, c, self.by_core[a])

        def copy(a, c, chip, way, src, sems):
            return pltpu.make_async_remote_copy(
                src_ref=src, dst_ref=slot(a, c, chip), send_sem=sems[0], recv_sem=sems[1],
                device_id=place.peer(way), device_id_type=MESH)

        def forward(a, c, order, k, ax, ay):
            chip = place.block(k, ax, ay)
            rel = {"x": ax, "y": ay, "z": k}
            last = max([i for i in range(3) if rel[order[i]] != 0], default=-1)
            src = ins[a].at[c] if last < 0 else slot(a, c, chip)
            for i in range(max(last, 0), 3):
                dim = order[i]
                if dim == "z":
                    sz = place.z_from[k]

                    @pl.when((sz <= place.z) & (place.z < 3))
                    def _():
                        copy(a, c, chip, "u", src, (send.at[a, c, 2], recv.at[a, c, chip])).start()

                    @pl.when((sz >= place.z) & (place.z > 0))
                    def _():
                        copy(a, c, chip, "d", src, (send.at[a, c, 3], recv.at[a, c, chip])).start()
                elif rel[dim] == 0:
                    copy(a, c, chip, dim, src, (send.at[a, c, ways[dim]], recv.at[a, c, chip])).start()
            copy(a, c, chip, "c", src, (core_send.at[a], core_recv.at[a])).start()

        def own(a, c):
            return pltpu.make_async_copy(ins[a].at[c], slot(a, c, me), local_sem.at[a, c])

        def entry(k, ax, ay):
            if (k, ax, ay) == (0, 0, 0):
                meet(place)
            for a in range(n):
                for c, order in enumerate(orders[a]):
                    chip = place.block(k, ax, ay)
                    if (k, ax, ay) != (0, 0, 0):
                        copy(a, c, chip, "x", slot(a, c, chip), (send.at[a, c, 0], recv.at[a, c, chip])).wait_recv()
                    forward(a, c, order, k, ax, ay)
                    if (k, ax, ay) == (0, 0, 0):
                        own(a, c).start()

        def finish():
            for a in range(n):
                for c in range(len(orders[a])):
                    own(a, c).wait()
            for a in range(n):
                whole = outs[a].at[0] if self.by_core[a] else outs[a].at[:, 0]
                pltpu.make_async_remote_copy(
                    src_ref=whole, dst_ref=whole, send_sem=core_send.at[a], recv_sem=core_recv.at[a],
                    device_id=place.peer("c"), device_id_type=MESH).wait()
                for c, order in enumerate(orders[a]):
                    def drain(way, count):
                        lead = outs[a].at[0] if self.by_core[a] else outs[a].at[:, 0]
                        part = lead.at[pl.ds(0, count), c]
                        pltpu.make_async_remote_copy(
                            src_ref=part, dst_ref=part, send_sem=send.at[a, c, ways[way]],
                            recv_sem=recv.at[a, c, 0],
                            device_id=place.peer("c"), device_id_type=MESH).wait_send()
                    before = 1
                    for dim in order:
                        if dim == "z":
                            for zz in range(4):
                                @pl.when(place.z == zz)
                                def _(zz=zz, before=before):
                                    if zz < 3:
                                        drain("u", before * (zz + 1))
                                    if zz > 0:
                                        drain("d", before * (4 - zz))
                            before *= 4
                        else:
                            drain(dim, before)
                            before *= 2

        entries = sorted(
            [(k, ax, ay) for k in range(4) for ax in range(2) for ay in range(2)], key=lambda e: e[0] + e[1] + e[2])
        return [functools.partial(entry, *e) for e in entries] + [finish]


class Reduce:
    def __init__(self, by_core, orders, shapes):
        self.by_core, self.orders, self.shapes = by_core, orders, shapes
        self.n, self.pieces = len(by_core), max(map(len, orders))

    def in_specs(self):
        return [pl.BlockSpec(memory_space=pl.ANY)] * self.n

    def out_specs(self):
        return [pl.BlockSpec(memory_space=pltpu.VMEM)] * self.n

    def out_shape(self):
        return [jax.ShapeDtypeStruct(s, jnp.float32) for s in self.shapes]

    def room(self, a, way):
        most = 1
        for order in self.orders[a]:
            if way in "ud":
                most = max(most, 4 if order[0] == "z" else 8)
            else:
                most = max(most, {2: 8, 1: 4, 0: 1}[order.index(way)])
        return most

    def scratch(self):
        n, pieces = self.n, self.pieces
        buffers = []
        for sizes in ([16] * n, [16] * n, *[[self.room(a, w) for a in range(n)] for w in "xyud"]):
            buffers += [pltpu.VMEM((k,) + s, jnp.bfloat16) for k, s in zip(sizes, self.shapes)]
        return buffers + [
            pltpu.SemaphoreType.DMA((n,)),
            pltpu.SemaphoreType.DMA((n, pieces, 16)),
            pltpu.SemaphoreType.DMA((n, pieces)),
            pltpu.SemaphoreType.DMA((n, pieces, 4, 8)),
            pltpu.SemaphoreType.DMA((n, pieces, 4)),
        ]

    def steps(self, ins, outs, scratch):
        n, orders, by_core = self.n, self.orders, self.by_core
        mine, other = scratch[:n], scratch[n : 2 * n]
        got = {w: scratch[(2 + i) * n : (3 + i) * n] for i, w in enumerate("xyud")}
        load_sem, core_recv, core_send, recv, send = scratch[6 * n :]
        ways = {"x": 0, "y": 1, "u": 2, "d": 3}
        place = Place()

        def number(at):
            sx, sy, sz = at
            return sz * 4 + sy * 2 + sx

        def load(a):
            src = ins[a].at[place.core] if by_core[a] else ins[a].at[:, place.core]
            return pltpu.make_async_copy(src, mine[a], load_sem.at[a])

        def to_core(a, c, at):
            chip = number(at)
            return pltpu.make_async_remote_copy(
                src_ref=at_block(ins[a], chip, 1 - place.core, c, by_core[a]), dst_ref=other[a].at[chip, c],
                send_sem=core_send.at[a, c], recv_sem=core_recv.at[a, c, chip],
                device_id=place.peer("c"), device_id_type=MESH)

        def landing(order, at, way):
            sx, sy, sz = at
            if way in "ud":
                return sz if order[0] == "z" else sz * 2 + (sx if order[0] == "x" else sy)
            turn = order.index(way)
            return (0, sz, sz * 2 + (sx if way == "y" else sy))[turn]

        def hop(a, c, order, at, way):
            spot = landing(order, at, way)
            return pltpu.make_async_remote_copy(
                src_ref=mine[a].at[number(at), c], dst_ref=got[way][a].at[spot, c],
                send_sem=send.at[a, c, ways[way]], recv_sem=recv.at[a, c, ways[way], spot],
                device_id=place.peer(way), device_id_type=MESH)

        def take(a, c, order, at, way):
            hop(a, c, order, at, way).wait_recv()
            mine[a][number(at), c] = mine[a][number(at), c] + got[way][a][landing(order, at, way), c]

        def fold(a, c, at):
            to_core(a, c, at).wait_recv()
            chip = number(at)
            mine[a][chip, c] = mine[a][chip, c] + other[a][chip, c]

        items = [(a, c, order) for a in range(n) for c, order in enumerate(orders[a])]
        lined = [it for it in items if it[2][1] == "z"]
        flat = [it for it in items if it[2][0] == "z"]
        items = lined + flat

        def side(dim, far):
            m = place.x if dim == "x" else place.y
            return 1 - m if far else m

        def spot(order, wave, i, far):
            sz = wave + (3 - 2 * wave) * (i // 2)
            if order[2] == "y":
                return (i % 2, side("y", far), sz)
            return (side("x", far), i % 2, sz)

        def loop(count, body):
            def run(i, carry):
                body(i)
                return carry
            lax.fori_loop(0, count, run, 0)

        def start(wave, far):
            for a, c, order in items:
                loop(4, lambda i: to_core(a, c, spot(order, wave, i, far)).start())

        def begin():
            meet(place)
            for a in range(n):
                load(a).start()
            for wave, far in ((0, True), (0, False), (1, True), (1, False)):
                start(wave, far)
            for a in range(n):
                load(a).wait()

        def far(wave):
            for a, c, order in items:
                def one(i):
                    at = spot(order, wave, i, True)
                    fold(a, c, at)
                    hop(a, c, order, at, order[2]).start()
                loop(4, one)

        def near(wave):
            for a, c, order in items:
                loop(4, lambda i: fold(a, c, spot(order, wave, i, False)))

        def second(it, wave):
            a, c, order = it
            if order[1] == "z":
                loop(4, lambda i: take(a, c, order, spot(order, wave, i, False), order[2]))
                return
            for away in (True, False):
                def one(i):
                    sz = wave + (3 - 2 * wave) * i
                    at = (side("x", away and order[1] == "x"), side("y", away and order[1] == "y"), sz)
                    take(a, c, order, at, order[2])
                    if away:
                        hop(a, c, order, at, order[1]).start()
                loop(2, one)

        def third(it, wave):
            a, c, order = it
            loop(2, lambda i: take(a, c, order, (place.x, place.y, wave + (3 - 2 * wave) * i), order[1]))

        def here(order):
            if order[0] == "z":
                return [(place.x, place.y)]
            return [(side("x", order[0] == "x"), side("y", order[0] == "y")), (place.x, place.y)]

        def line(it, j):
            a, c, order = it
            for way, target, active, inner in (
                ("u", 3 - j, place.z < 3 - j, place.z > 0),
                ("d", j, place.z > j, place.z < 3),
            ):
                @pl.when(active)
                def _():
                    for sx, sy in here(order):
                        at = (sx, sy, target)

                        @pl.when(inner)
                        def _():
                            take(a, c, order, at, way)
                        hop(a, c, order, at, way).start()

        def owned(it):
            a, c, order = it
            for first, (sx, sy) in enumerate(here(order)):
                at = (sx, sy, place.z)

                @pl.when(place.z > 0)
                def _():
                    take(a, c, order, at, "u")

                @pl.when(place.z < 3)
                def _():
                    take(a, c, order, at, "d")
                if order[0] != "z" and first == 0:
                    hop(a, c, order, at, order[0]).start()

        def last(it):
            a, c, order = it
            if order[0] != "z":
                take(a, c, order, (place.x, place.y, place.z), order[0])
            outs[a][c] = mine[a][place.chip, c].astype(jnp.float32)

        def drain(a, c, sem, count):
            part = other[a].at[pl.ds(0, count), c]
            pltpu.make_async_remote_copy(
                src_ref=part, dst_ref=part, send_sem=sem, recv_sem=recv.at[a, c, 0, 0],
                device_id=place.peer("c"), device_id_type=MESH).wait_send()

        def finish():
            for it in lined:
                last(it)
            for a, c, order in items:
                drain(a, c, core_send.at[a, c], 16)
                left = 16
                for turn in (2, 1, 0):
                    dim = order[turn]
                    if dim == "z":
                        left //= 4
                        for zz in range(4):
                            @pl.when(place.z == zz)
                            def _(zz=zz, left=left):
                                if zz < 3:
                                    drain(a, c, send.at[a, c, 2], left * (3 - zz))
                                if zz > 0:
                                    drain(a, c, send.at[a, c, 3], left * zz)
                    else:
                        left //= 2
                        drain(a, c, send.at[a, c, ways[dim]], left)

        part = functools.partial
        out = [begin, part(far, 0), part(near, 0), part(far, 1)]
        for it in lined:
            out += [part(second, it, 0), part(line, it, 0)]
        out += [part(second, it, 0) for it in flat]
        out += [part(near, 1)]
        for i, it in enumerate(lined):
            out += [part(second, it, 1), part(line, it, 1), part(line, it, 2)]
            if i == 0:
                for fl in flat:
                    out += [part(third, fl, 0), part(line, fl, 0)]
        if not lined:
            for fl in flat:
                out += [part(third, fl, 0), part(line, fl, 0)]
        out += [part(second, it, 1) for it in flat]
        out += [part(owned, it) for it in lined]
        for it in flat:
            out += [part(third, it, 1), part(line, it, 1), part(line, it, 2), part(owned, it), part(last, it)]
        return out + [finish]


VMEM_ALL = 64 * 1024 * 1024 - 65536


class Aside:
    def __init__(self, plan, arrays, collective_id):
        self.plan, self.arrays, self.collective_id = plan, arrays, collective_id


def with_aside(body, aside, *, grid, in_specs, out_specs, out_shape, scratch_shapes=(), cost, operands):
    if aside is None:
        out = pl.pallas_call(
            body, grid=grid, in_specs=in_specs, out_specs=out_specs, out_shape=tuple(out_shape),
            scratch_shapes=scratch_shapes, cost_estimate=cost,
            compiler_params=pltpu.CompilerParams(vmem_limit_bytes=VMEM_ALL))(*operands)
        return out, None
    plan = aside.plan
    n_in, n_out, n_scr, n = len(in_specs), len(out_specs), len(scratch_shapes), plan.n
    cells = 1
    for extent in grid:
        cells *= extent

    def kernel(*refs):
        refs = list(refs)
        ins, refs = refs[:n_in], refs[n_in:]
        plan_ins, refs = refs[:n], refs[n:]
        outs, refs = refs[:n_out], refs[n_out:]
        plan_outs, refs = refs[:n], refs[n:]
        scratch, plan_scratch = refs[:n_scr], refs[n_scr:]
        steps = plan.steps(plan_ins, plan_outs, plan_scratch)
        cell = 0
        for axis, extent in enumerate(grid):
            cell = cell * extent + pl.program_id(axis)
        by_cell = {}
        for i, step in enumerate(steps):
            by_cell.setdefault(i * (cells - 1) // (len(steps) - 1), []).append(step)
        for index in sorted(by_cell):
            if index < cells - 1:
                @pl.when(cell == index)
                def _():
                    for step in by_cell[index]:
                        step()
        body(*ins, *outs, *scratch)

        @pl.when(cell == cells - 1)
        def _():
            for step in by_cell[cells - 1]:
                step()

    out = pl.pallas_call(
        kernel, grid=grid,
        in_specs=list(in_specs) + plan.in_specs(), out_specs=list(out_specs) + plan.out_specs(),
        out_shape=tuple(out_shape) + tuple(plan.out_shape()),
        scratch_shapes=list(scratch_shapes) + plan.scratch(), cost_estimate=cost,
        compiler_params=pltpu.CompilerParams(
            collective_id=aside.collective_id, has_side_effects=True, vmem_limit_bytes=VMEM_ALL),
    )(*operands, *aside.arrays)
    return out[:n_out], out[n_out:]


def exchange(plan, arrays, collective_id):
    n = plan.n

    def kernel(*refs):
        for step in plan.steps(refs[:n], refs[n : 2 * n], refs[2 * n :]):
            step()

    moved = sum(a.size for a in arrays) * 2
    return pl.pallas_call(
        kernel,
        out_shape=tuple(plan.out_shape()),
        in_specs=plan.in_specs(),
        out_specs=plan.out_specs(),
        scratch_shapes=plan.scratch(),
        compiler_params=pltpu.CompilerParams(
            collective_id=collective_id, has_side_effects=True, vmem_limit_bytes=VMEM_ALL),
        cost_estimate=pl.CostEstimate(flops=0, bytes_accessed=32 * moved, transcendentals=0),
    )(*arrays)


def gather_plan(arrays, by_core, orders):
    return Gather(by_core, orders, [a.shape for a in arrays], arrays[0].dtype)


def reduce_plan(arrays, by_core, orders):
    return Reduce(by_core, orders, [a.shape[2:] for a in arrays])


def all_gather_layer(arrays, by_core, orders, collective_id):
    return exchange(gather_plan(arrays, by_core, orders), arrays, collective_id)


def reduce_scatter_layer(arrays, by_core, orders, collective_id):
    return exchange(reduce_plan(arrays, by_core, orders), arrays, collective_id)


HD = 64
CTX = 768

eps_norm = 1e-05
clip_at = 0.01
rate = 3000.0
moment = 0.9
keep_avg = 0.9
decay_wd = 1e-05
low_type = jnp.bfloat16
wide_type = jnp.float32


def layer_norm(values, gain_row, shift_row):
    center = values - jnp.mean(values, -1, keepdims=True)
    spread = jnp.mean(center * center, -1, keepdims=True)
    return center * lax.rsqrt(spread + eps_norm) * gain_row + shift_row


def norm_back(values, gain_row, shift_row, upstream):
    _, pull = jax.vjp(layer_norm, values, gain_row, shift_row)
    return pull(upstream)


def gelu_back(values, upstream):
    _, pull = jax.vjp(jax.nn.gelu, values)
    return pull(upstream)[0]


def matmul(first_op, second_op):
    return jnp.dot(first_op, second_op, preferred_element_type=wide_type)


def contract(first_op, second_op, first_dim, second_dim):
    return lax.dot_general(
        first_op, second_op, (((first_dim,), (second_dim,)), ((), ())), preferred_element_type=wide_type
    )


def matmul_tn(first_op, second_op):
    return contract(first_op, second_op, 0, 0)


def matmul_nt(first_op, second_op):
    return contract(first_op, second_op, 1, 1)


def head_lanes(shape, head):
    lane = lax.broadcasted_iota(jnp.int32, shape, 1)
    mine = (lane < HD) if head == 0 else (lane >= HD)
    return mine, lane == (HD if head == 0 else 0)


def attend_kernel(q_ref, k_ref, v_ref, bias_ref, out_ref, lse_ref):
    q_block = q_ref[0] * jnp.asarray(HD ** -0.5, low_type)
    k_block, v_block, bias = k_ref[0], v_ref[0], bias_ref[...]
    v_turned = v_block.T
    parts = []
    for head in range(2):
        q_mine, q_one = head_lanes(q_block.shape, head)
        k_mine, _ = head_lanes(k_block.shape, head)
        one = jnp.where(q_one, jnp.ones_like(q_block), jnp.zeros_like(q_block))
        score = matmul_nt(jnp.where(k_mine, k_block, bias), jnp.where(q_mine, q_block, one))
        peak = jnp.max(score, 0, keepdims=True)
        lifted = jnp.exp(score - peak)
        total = jnp.sum(lifted, 0, keepdims=True)
        mixed = matmul(v_turned[head * HD : (head + 1) * HD], lifted.astype(low_type))
        parts.append(mixed / total)
        lse_ref[0, head : head + 1, :] = peak + jnp.log(total)
    out_ref[...] = jnp.concatenate(parts, 0).T.astype(low_type)


def attend(queries, keys_values, bias, aside):
    groups, rows, width = queries.shape
    pairs = width // 128
    block = min(256, rows)
    grid = (groups * pairs, rows // block)
    (mixed, lse), extra = with_aside(
        attend_kernel,
        aside,
        grid=grid,
        in_specs=[
            pl.BlockSpec((1, block, 128), lambda p, i: (p // pairs, i, p % pairs)),
            pl.BlockSpec((1, CTX, 128), lambda p, i: (p // pairs, 0, p % pairs)),
            pl.BlockSpec((1, CTX, 128), lambda p, i: (p // pairs, 0, pairs + p % pairs)),
            pl.BlockSpec((CTX, 128), lambda p, i: (0, 0)),
        ],
        out_specs=[
            pl.BlockSpec((block, 128), lambda p, i: (i, p)),
            pl.BlockSpec((1, 2, block), lambda p, i: (p, 0, i)),
        ],
        out_shape=(
            jax.ShapeDtypeStruct((rows, groups * width), low_type),
            jax.ShapeDtypeStruct((groups * pairs, 2, rows), wide_type),
        ),
        cost=pl.CostEstimate(
            flops=4 * rows * CTX * groups * width, bytes_accessed=8 * rows * groups * width,
            transcendentals=rows * CTX * groups * width // HD),
        operands=(queries, keys_values, keys_values, bias),
    )
    return mixed, lse, extra


def attend_back_kernel(q_ref, k_ref, v_ref, bias_ref, g_ref, o_ref, lse_ref, gq_ref, gk_ref, gv_ref, k_sum, v_sum):
    step = pl.program_id(1)

    @pl.when(step == 0)
    def _():
        k_sum[...] = jnp.zeros_like(k_sum)
        v_sum[...] = jnp.zeros_like(v_sum)

    scale = HD ** -0.5
    q_block = q_ref[0] * jnp.asarray(scale, low_type)
    k_block, v_block, bias = k_ref[0], v_ref[0], bias_ref[...]
    g_block = g_ref[...]
    k_turned = k_block.T
    both = (g_block.astype(wide_type) * o_ref[...].astype(wide_type)).T
    parts = []
    for head in range(2):
        q_mine, q_one = head_lanes(q_block.shape, head)
        k_mine, _ = head_lanes(k_block.shape, head)
        nothing = jnp.zeros_like(q_block)
        one = jnp.where(q_one, jnp.ones_like(q_block), nothing)
        score = matmul_nt(jnp.where(k_mine, k_block, bias), jnp.where(q_mine, q_block, one))
        prob = jnp.exp(score - lse_ref[0, head : head + 1, :])
        g_mine = jnp.where(q_mine, g_block, nothing)
        grad_prob = matmul_nt(v_block, g_mine)
        inner = jnp.sum(both[head * HD : (head + 1) * HD], 0, keepdims=True)
        grad_score = (prob * (grad_prob - inner)).astype(low_type)
        v_sum[...] += matmul(prob.astype(low_type), g_mine)
        k_sum[...] += matmul(grad_score, jnp.where(q_mine, q_block, nothing))
        parts.append(matmul(k_turned[head * HD : (head + 1) * HD], grad_score) * scale)
    gq_ref[0] = jnp.concatenate(parts, 0).T.astype(low_type)

    @pl.when(step == pl.num_programs(1) - 1)
    def _():
        gk_ref[0] = k_sum[...].astype(low_type)
        gv_ref[0] = v_sum[...].astype(low_type)


def attend_back(queries, keys_values, bias, grad_mixed, mixed, lse, aside):
    groups, rows, width = queries.shape
    pairs = width // 128
    block = min(256, rows)
    grid = (groups * pairs, rows // block)
    row_spec = pl.BlockSpec((block, 128), lambda p, i: (i, p))
    key_out = pl.BlockSpec((1, CTX, 128), lambda p, i: (p // pairs, 0, p % pairs))
    grads, extra = with_aside(
        attend_back_kernel,
        aside,
        grid=grid,
        in_specs=[
            pl.BlockSpec((1, block, 128), lambda p, i: (p // pairs, i, p % pairs)),
            pl.BlockSpec((1, CTX, 128), lambda p, i: (p // pairs, 0, p % pairs)),
            pl.BlockSpec((1, CTX, 128), lambda p, i: (p // pairs, 0, pairs + p % pairs)),
            pl.BlockSpec((CTX, 128), lambda p, i: (0, 0)),
            row_spec,
            row_spec,
            pl.BlockSpec((1, 2, block), lambda p, i: (p, 0, i)),
        ],
        out_specs=[
            pl.BlockSpec((1, block, 128), lambda p, i: (p // pairs, i, p % pairs)),
            key_out,
            key_out,
        ],
        out_shape=(
            jax.ShapeDtypeStruct(queries.shape, low_type),
            jax.ShapeDtypeStruct((groups, CTX, width), low_type),
            jax.ShapeDtypeStruct((groups, CTX, width), low_type),
        ),
        scratch_shapes=[pltpu.VMEM((CTX, 128), wide_type)] * 2,
        cost=pl.CostEstimate(
            flops=10 * rows * CTX * groups * width, bytes_accessed=16 * rows * groups * width,
            transcendentals=rows * CTX * groups * width // HD),
        operands=(queries, keys_values, keys_values, bias, grad_mixed, mixed, lse),
    )
    return tuple(grads) + (extra,)


def grouped(rows, weight):
    return jnp.einsum("rd,gdc->grc", rows, weight, preferred_element_type=wide_type)


GELU_K = 0.7978845608028654
GELU_C = 0.044715


def center_scale(values):
    center = values - jnp.mean(values, -1, keepdims=True)
    return center, lax.rsqrt(jnp.mean(center * center, -1, keepdims=True) + eps_norm)


def mlp_kernel(res_ref, mixed_ref, mix_ref, up_ref, down_ref, vec_ref, out_ref, middle_ref, hidden_ref, normed, total):
    step, last = pl.program_id(1), pl.num_programs(1) - 1
    size = hidden_ref.shape[1]

    @pl.when(step == 0)
    def _():
        middle = res_ref[...] + matmul(mixed_ref[...], mix_ref[...]) + vec_ref[4:5]
        middle_ref[...] = middle
        center, spread = center_scale(middle)
        normed[...] = (center * spread * vec_ref[2:3] + vec_ref[3:4]).astype(low_type)
        total[...] = middle + vec_ref[5:6]

    part = pl.ds(pl.multiple_of(step * size, size), size)
    hidden = matmul(normed[...], up_ref[:, part])
    hidden_ref[...] = hidden.astype(low_type)
    inner = jnp.tanh(GELU_K * (hidden + GELU_C * hidden * hidden * hidden))
    active = (0.5 * hidden * (1.0 + inner)).astype(low_type)
    total[...] += matmul(active, down_ref[part, :])

    @pl.when(step == last)
    def _():
        out_ref[...] = total[...]


def mlp_forward(residual, first, mixed, weights, vec_rows, aside):
    _, w_mix, w_grow, w_shrink = weights
    rows, width = mixed.shape
    wide = w_grow.shape[1]
    block, chunk = 256, 512
    skip = first // block

    def whole(a):
        return pl.BlockSpec(a.shape, lambda i, j: (0, 0), pipeline_mode=pl.Buffered(1))

    row_spec = pl.BlockSpec((block, width), lambda i, j: (i, 0))
    outs, extra = with_aside(
        mlp_kernel,
        aside,
        grid=(rows // block, wide // chunk),
        in_specs=[
            pl.BlockSpec((block, width), lambda i, j: (i + skip, 0)), row_spec,
            whole(w_mix), whole(w_grow), whole(w_shrink), whole(vec_rows),
        ],
        out_specs=[row_spec, row_spec, pl.BlockSpec((block, chunk), lambda i, j: (i, j))],
        out_shape=(
            jax.ShapeDtypeStruct((rows, width), wide_type),
            jax.ShapeDtypeStruct((rows, width), wide_type),
            jax.ShapeDtypeStruct((rows, wide), low_type),
        ),
        scratch_shapes=[pltpu.VMEM((block, width), low_type), pltpu.VMEM((block, width), wide_type)],
        cost=pl.CostEstimate(
            flops=2 * rows * width * (2 * wide + width), bytes_accessed=rows * width * 24, transcendentals=rows * wide),
        operands=(residual, mixed, w_mix, w_grow, w_shrink, vec_rows),
    )
    return outs, extra


def mlp_back_kernel(
    u_ref, middle_ref, mixed_ref, mix_ref, up_ref, down_ref, vec_ref, hidden_ref,
    up_grad_ref, down_grad_ref, mix_grad_ref, mixed_grad_ref, mid_grad_ref, vec_grad_ref,
    u_low, normed_turned, normed_grad,
):
    step, last = pl.program_id(0), pl.num_programs(0) - 1
    rows, width = u_ref.shape
    block = 256

    @pl.when(step == 0)
    def _():
        @pl.loop(0, rows // block)
        def _(i):
            part = pl.ds(pl.multiple_of(i * block, block), block)
            center, spread = center_scale(middle_ref[part, :])
            normed = (center * spread * vec_ref[2:3] + vec_ref[3:4]).astype(low_type)
            normed_turned[:, part] = normed.T
            u_low[part, :] = u_ref[part, :].astype(low_type)
            normed_grad[part, :] = jnp.zeros((block, width), wide_type)

    hidden = hidden_ref[...].astype(wide_type)
    square = hidden * hidden
    inner = jnp.tanh(GELU_K * hidden * (1.0 + GELU_C * square))
    half = 0.5 * (1.0 + inner)
    active = (hidden * half).astype(low_type)
    slope = half + 0.5 * hidden * (1.0 - inner * inner) * (GELU_K * (1.0 + 3.0 * GELU_C * square))
    grad = (matmul_nt(u_low[...], down_ref[...]) * slope).astype(low_type)
    down_grad_ref[...] = matmul(active.T, u_low[...]).astype(low_type)
    up_grad_ref[...] = matmul(normed_turned[...], grad).astype(low_type)
    normed_grad[...] += matmul_nt(grad, up_ref[...])

    @pl.when(step == last)
    def _():
        vec_grad_ref[...] = jnp.zeros_like(vec_grad_ref)

        @pl.loop(0, rows // block)
        def _(i):
            part = pl.ds(pl.multiple_of(i * block, block), block)
            center, spread = center_scale(middle_ref[part, :])
            shape = center * spread
            grads = normed_grad[part, :]
            scaled = grads * vec_ref[2:3]
            from_norm = spread * (
                scaled - jnp.mean(scaled, -1, keepdims=True) - shape * jnp.mean(scaled * shape, -1, keepdims=True))
            u_part = u_ref[part, :]
            total = from_norm + u_part
            mid_grad_ref[part, :] = total
            vec_grad_ref[0:1] += jnp.sum(grads * shape, 0, keepdims=True)
            vec_grad_ref[1:2] += jnp.sum(grads, 0, keepdims=True)
            vec_grad_ref[2:3] += jnp.sum(total, 0, keepdims=True)
            vec_grad_ref[3:4] += jnp.sum(u_part, 0, keepdims=True)
            low = total.astype(low_type)
            u_low[part, :] = low
            mixed_grad_ref[part, :] = matmul_nt(low, mix_ref[...]).astype(low_type)
            normed_turned[:, part] = mixed_ref[part, :].T
        mix_grad_ref[...] = matmul(normed_turned[...], u_low[...]).astype(low_type)


def mlp_backward(upstream, middle, mixed, weights, vec_rows, hidden, aside):
    _, w_mix, w_grow, w_shrink = weights
    rows, width = upstream.shape
    wide = hidden.shape[1]
    chunk = 256

    def whole(shape):
        return pl.BlockSpec(shape, lambda j: (0, 0), pipeline_mode=pl.Buffered(1))

    square, row_shape = (width, width), (rows, width)
    up_spec = pl.BlockSpec((width, chunk), lambda j: (0, j))
    down_spec = pl.BlockSpec((chunk, width), lambda j: (j, 0))
    return with_aside(
        mlp_back_kernel,
        aside,
        grid=(wide // chunk,),
        in_specs=[
            whole(row_shape), whole(row_shape), whole(row_shape), whole(square), up_spec, down_spec,
            whole(vec_rows.shape), pl.BlockSpec((rows, chunk), lambda j: (0, j)),
        ],
        out_specs=[up_spec, down_spec] + [
            pl.BlockSpec(s, lambda j: (0, 0)) for s in (square, row_shape, row_shape, (8, width))],
        out_shape=(
            jax.ShapeDtypeStruct((width, wide), low_type),
            jax.ShapeDtypeStruct((wide, width), low_type),
            jax.ShapeDtypeStruct(square, low_type),
            jax.ShapeDtypeStruct(row_shape, low_type),
            jax.ShapeDtypeStruct(row_shape, wide_type),
            jax.ShapeDtypeStruct((8, width), wide_type),
        ),
        scratch_shapes=[
            pltpu.VMEM(row_shape, low_type), pltpu.VMEM((width, rows), low_type), pltpu.VMEM(row_shape, wide_type)],
        cost=pl.CostEstimate(
            flops=4 * rows * width * (2 * wide + width), bytes_accessed=rows * width * 40, transcendentals=rows * wide),
        operands=(upstream, middle, mixed, w_mix, w_grow, w_shrink, vec_rows, hidden),
    )


def layer_forward(residual, first, vec_rows, weights, bias, asides):
    w_joined = weights[0]
    width = w_joined.shape[2] // 3
    normed = layer_norm(residual, vec_rows[0], vec_rows[1]).astype(low_type)
    queries = grouped(normed[first:], w_joined[:, :, :width]).astype(low_type)
    keys_values = grouped(normed[:CTX], w_joined[:, :, width:]).astype(low_type)
    mixed, lse, extra = attend(queries, keys_values, bias, asides[0])
    (output, middle, hidden), more = mlp_forward(residual, first, mixed, weights, vec_rows, asides[1])
    return output, (extra, more), (residual, normed, queries, keys_values, mixed, lse, middle, hidden)


def layer_backward(upstream, kept, first, vec_rows, weights, bias, make_asides):
    w_joined = weights[0]
    width = w_joined.shape[2] // 3
    residual, normed, queries, keys_values, mixed, lse, middle, hidden = kept
    outs, extra = mlp_backward(upstream, middle, mixed, weights, vec_rows, hidden, make_asides(0, None))
    grad_grow, grad_shrink, grad_mix, grad_mixed, grad_middle, mlp_vec = outs
    grad_q, grad_k, grad_v, more = attend_back(
        queries, keys_values, bias, grad_mixed, mixed, lse, make_asides(1, (grad_grow, grad_shrink)))

    def weight_grad(rows, grads):
        return jnp.einsum("rd,grc->gdc", rows, grads, preferred_element_type=wide_type).astype(low_type)

    def row_grad(grads, part):
        return jnp.einsum(
            "grc,gdc->rd", grads, w_joined[:, :, part * width : (part + 1) * width], preferred_element_type=wide_type)

    grad_joined = jnp.concatenate(
        [weight_grad(normed[first:], grad_q), weight_grad(normed[:CTX], grad_k), weight_grad(normed[:CTX], grad_v)], 2)
    from_q = row_grad(grad_q, 0)
    from_kv = row_grad(grad_k, 1) + row_grad(grad_v, 2)
    rows = residual.shape[0]
    below = jnp.zeros((first, from_q.shape[1]), wide_type)
    tail = jnp.zeros((rows - CTX, from_q.shape[1]), wide_type)
    grad_normed = jnp.concatenate([below, from_q], 0) + jnp.concatenate([from_kv, tail], 0)
    grad_input, gain_attn, shift_attn = norm_back(residual, vec_rows[0], vec_rows[1], grad_normed)
    vec_grads = [gain_attn, shift_attn, mlp_vec[0], mlp_vec[1], mlp_vec[2], mlp_vec[3]]
    grad_out = grad_input + jnp.concatenate([below, grad_middle], 0)
    return grad_out, (extra, more), (grad_joined, grad_mix, grad_grow, grad_shrink), vec_grads


def update(weight, moment_old, average, grad_in, scale):
    applied = grad_in * scale + decay_wd * weight
    moment_new = moment * moment_old + applied
    weight_new = weight - rate * (applied + moment * moment_new)
    return (weight_new, moment_new, keep_avg * average + (1.0 - keep_avg) * weight_new)


BY_CORE = (True, True, False, False)
ROUTES = (("zxy",), ("zxy",), ("xzy",), ("yzx",))
HALVES = (("zxy", "zyx"),)


def whole_gather(shard_list, by_core):
    return [
        lax.all_gather(lax.all_gather(shard, "dp", axis=0), "head", axis=0 if bc else 1)
        for shard, bc in zip(shard_list, by_core)]


def as_blocks(grads, by_core, rows_list, routes):
    chips, cores = lax.axis_size("dp"), lax.axis_size("head")
    return [
        grad.reshape(((cores, chips) if bc else (chips, cores)) + (len(route), rows // len(route), -1))
        for grad, bc, rows, route in zip(grads, by_core, rows_list, routes)]


def whole_scatter(grads, by_core, rows_list):
    outs = []
    for grad, bc in zip(as_blocks(grads, by_core, rows_list, ROUTES), by_core):
        half = lax.psum_scatter(grad.astype(wide_type), "head", scatter_dimension=0 if bc else 1)
        outs.append(lax.psum_scatter(half, "dp", scatter_dimension=0))
    return outs


def shards(
    rows_in, feat_mask, counts, ctx_vals, targets, query_mask,
    w_emb, m_emb, a_emb, vectors, m_vec, a_vec,
    w_qkv, m_qkv, a_qkv, w_out, m_out, a_out, w_up, m_up, a_up, w_down, m_down, a_down,
    w_head, m_head, a_head,
):
    chips, cores = lax.axis_size("dp"), lax.axis_size("head")
    direct = (chips, cores) == (16, 2)
    _, row_count, feat_count = rows_in.shape
    layer_total = w_qkv.shape[0]
    width = w_emb.shape[1]
    joined_rows = w_qkv.shape[1]
    kinds = w_qkv.shape[2] * w_qkv.shape[4]

    def own_weights(at):
        return [
            w_qkv[at].reshape((joined_rows, kinds)).astype(low_type)[None],
            w_out[at, 0].astype(low_type)[None],
            w_up[at].astype(low_type)[None],
            w_down[at].astype(low_type)[None],
        ]

    def as_weights(gathered):
        qkv, out, up, down = gathered
        return (
            qkv.reshape((cores, width, kinds)),
            out.reshape((width, width)),
            up.reshape((width, -1)),
            down.reshape((-1, width)),
        )

    own = [own_weights(at) for at in range(layer_total)]
    forward_asides = [[None, None] for _ in own]
    if direct:
        gathered = [all_gather_layer(own[0], BY_CORE, ROUTES, 1)]
        first_two, last_two = own[1][:2], own[1][2:]
        forward_asides[0] = [
            Aside(gather_plan(last_two, BY_CORE[2:], (("zxy",), ("zyx",))), last_two, 2),
            Aside(gather_plan(first_two, BY_CORE[:2], (("zxy",), ("zyx",))), first_two, 6),
        ]
    else:
        gathered = [whole_gather(o, BY_CORE) for o in own]

    table = lax.axis_index("dp") * cores + lax.axis_index("head")
    count = lax.dynamic_slice_in_dim(counts, table, 1, 0)
    bias = jnp.where(jnp.arange(CTX) < count, 0.0, -1e30).astype(low_type)
    bias = jnp.broadcast_to(bias[:, None], (CTX, 128))
    masked = rows_in[0] * feat_mask[0][None, :].astype(low_type)
    leading = jnp.concatenate([ctx_vals[0], jnp.zeros((row_count - CTX,), wide_type)])[:, None]
    residual = matmul(masked, w_emb.astype(low_type)) + vectors[1] + leading * vectors[0]
    kept_all = []
    weights = []
    for at in range(layer_total):
        first = CTX if at == layer_total - 1 else 0
        weights.append(as_weights(gathered[at]))
        residual, extra, kept = layer_forward(
            residual, first, vectors[2 + 6 * at : 8 + 6 * at], weights[at], bias, forward_asides[at])
        if extra[0] is not None:
            gathered.append(list(extra[1]) + list(extra[0]))
        kept_all.append(kept)

    head_low = w_head.astype(low_type)
    final_rows = layer_norm(residual, vectors[-2], vectors[-1]).astype(low_type)
    logits = matmul(final_rows, head_low)
    row_peak = jnp.max(logits, -1, keepdims=True)
    log_total = row_peak[:, 0] + jnp.log(jnp.sum(jnp.exp(logits - row_peak), -1))
    target_hit = (jnp.arange(logits.shape[1])[None, :] == targets[0][:, None]).astype(wide_type)
    picked = jnp.sum(logits * target_hit, -1)
    row_weight = query_mask[0].astype(wide_type)
    loss_part = jnp.sum((log_total - picked) * row_weight)
    grad_logits = ((jnp.exp(logits - log_total[:, None]) - target_hit) * row_weight[:, None]).astype(low_type)
    grad_head = matmul_tn(final_rows, grad_logits).astype(low_type)
    upstream, gain_final, shift_final = norm_back(
        residual, vectors[-2], vectors[-1], matmul_nt(grad_logits, head_low))

    rows_list = [joined_rows, w_out.shape[2], w_up.shape[1], w_down.shape[1]]
    sums = [None] * layer_total
    vec_grads = [None] * layer_total
    big = None
    for at in reversed(range(layer_total)):
        first = CTX if at == layer_total - 1 else 0
        above = big

        def make_asides(turn, ready):
            if not direct or above is None:
                return None
            if turn == 0:
                blocks = as_blocks(above[2:], BY_CORE[2:], rows_list[2:], ROUTES[2:])
                return Aside(reduce_plan(blocks, BY_CORE[2:], ROUTES[2:]), blocks, 3)
            blocks = as_blocks(list(above[:2]) + list(ready), BY_CORE, rows_list, ROUTES)
            return Aside(reduce_plan(blocks, BY_CORE, ROUTES), blocks, 7)

        upstream, extra, big, vec_grads[at] = layer_backward(
            upstream, kept_all[at], first, vectors[2 + 6 * at : 8 + 6 * at], weights[at], bias, make_asides)
        if not direct:
            sums[at] = whole_scatter(big, BY_CORE, rows_list)
        elif extra[0] is not None:
            sums[at + 1] = list(extra[1][:2]) + list(extra[0])
            sums[at] = list(extra[1][2:])
    grad_emb = matmul_tn(masked, upstream.astype(low_type))
    vec_list = [jnp.sum(upstream * leading, 0), jnp.sum(upstream, 0)]
    for at in range(layer_total):
        vec_list = vec_list + vec_grads[at]
    grad_vec = jnp.stack(vec_list + [gain_final, shift_final])

    devices = chips * cores
    n_head, n_emb = w_head.size // (devices * 128), w_emb.size // (devices * 128)
    n_vec = -(-vectors.size // (devices * 128))
    vec_flat = jnp.pad(grad_vec.astype(low_type).reshape(-1), (0, n_vec * devices * 128 - vectors.size))
    used = n_head + n_emb + n_vec
    n_all = -(-(used + 1) // 32) * 32
    small = jnp.concatenate([
        grad_head.reshape((devices, n_head, 128)),
        grad_emb.astype(low_type).reshape((devices, n_emb, 128)),
        vec_flat.reshape((devices, n_vec, 128)),
        jnp.zeros((devices, n_all - used, 128), low_type)], 1)
    if direct:
        last_grads, last_rows, last_core = list(big[:2]) + [small], rows_list[:2] + [n_all], BY_CORE[:2] + (False,)
        routes = (("xzy", "yzx", "zyx"), ("zxy",), ("zxy", "zyx"))
        blocks = as_blocks(last_grads, last_core, last_rows, routes)
        qkv_sum, out_sum, small_sum = reduce_scatter_layer(blocks, last_core, routes, 4)
        sums[0] = [qkv_sum, out_sum] + sums[0]
    else:
        small_sum = whole_scatter([small], (False,), [n_all])[0]
    small_sum = small_sum.reshape((n_all, 128))

    square = sum(jnp.sum(p * p) for ps in sums for p in ps) + jnp.sum(small_sum * small_sum)
    scalars = jnp.pad(jnp.stack([square, loss_part, jnp.sum(row_weight)]), (0, 125))
    small_sum = jnp.concatenate([small_sum[: n_all - 1], scalars[None]], 0)
    if direct:
        small_all = all_gather_layer([small_sum.reshape((2, n_all // 2, 128))], (False,), HALVES, 5)[0]
    else:
        small_all = whole_gather([small_sum], (False,))[0]
    small_all = small_all.reshape((devices, n_all, 128))
    totals = jnp.sum(small_all[:, n_all - 1, :3], 0)
    pooled = totals[2]
    loss = totals[1] / pooled
    grad_norm = jnp.sqrt(totals[0]) / pooled
    scale = jnp.minimum(1.0, clip_at / grad_norm) / pooled
    grad_head = small_all[:, :n_head].reshape(w_head.shape)
    grad_emb = small_all[:, n_head : n_head + n_emb].reshape(w_emb.shape)
    grad_vec = small_all[:, n_head + n_emb : used].reshape(-1)[: vectors.size].reshape(vectors.shape)

    def big_update(weight, moment_old, average, kind):
        grad = jnp.stack([sums[at][kind].reshape(weight.shape[1:]) for at in range(layer_total)])
        return update(weight, moment_old, average, grad, scale)

    e_w, e_m, e_a = update(w_emb, m_emb, a_emb, grad_emb, scale)
    v_w, v_m, v_a = update(vectors, m_vec, a_vec, grad_vec, scale)
    q_w, q_m, q_a = big_update(w_qkv, m_qkv, a_qkv, 0)
    o_w, o_m, o_a = big_update(w_out, m_out, a_out, 1)
    u_w, u_m, u_a = big_update(w_up, m_up, a_up, 2)
    d_w, d_m, d_a = big_update(w_down, m_down, a_down, 3)
    h_w, h_m, h_a = update(w_head, m_head, a_head, grad_head, scale)
    return (
        loss, grad_norm, e_w, e_m, e_a, v_w, v_m, v_a, q_w, q_m, q_a, o_w, o_m, o_a,
        u_w, u_m, u_a, d_w, d_m, d_a, h_w, h_m, h_a,
    )


def solution(mesh):
    tables = [P(("dp", "head"), None, None)] + [P(("dp", "head"), None)] + [P()] + [P(("dp", "head"), None)] * 3
    joined = P(None, "dp", None, "head", None)
    mixed = P(None, "head", "dp", None)
    wide = P(None, ("dp", "head"), None)
    state = [P()] * 6 + [joined] * 3 + [mixed] * 3 + [wide] * 6 + [P()] * 3
    return jax.shard_map(
        shards, mesh=mesh, in_specs=tuple(tables + state), out_specs=tuple([P(), P()] + state), check_vma=False)
```

```python
import functools
import jax
import jax.numpy as jnp
from jax import lax
from jax.sharding import PartitionSpec as P
from jax.experimental import pallas as pl
from jax.experimental.pallas import tpu as pltpu

MESH = pl.DeviceIdType.MESH


class Place:
    def __init__(self):
        self.chip = lax.axis_index("dp")
        self.core = lax.axis_index("head")
        self.x = self.chip % 2
        self.y = (self.chip // 2) % 2
        self.z = self.chip // 4
        z = self.z
        self.z_from = (z, 1 + z % 2, (12 - 2 * z) % 5, 3 - 3 * (z // 2))

    def peer(self, way):
        step = {
            "x": 1 - 2 * self.x,
            "y": 2 - 4 * self.y,
            "u": 4,
            "d": -4,
            "c": 0,
        }[way]
        core = 1 - self.core if way == "c" else self.core
        return (self.chip + step, core)

    def group(self, k):
        return (
            1 - self.y if k & 4 else self.y, 1 - self.x if k & 2 else self.x, 1 - self.core if k & 1 else self.core)

    def block(self, k, ax, ay):
        sx = self.x if ax == 0 else 1 - self.x
        sy = self.y if ay == 0 else 1 - self.y
        return self.z_from[k] * 4 + sy * 2 + sx


def meet(place, wide=False):
    barrier = pltpu.get_barrier_semaphore()
    to = [place.peer(way) for way in "xyc"]
    if wide:
        to = []
        for k in range(1, 8):
            y, x, core = place.group(k)
            to.append((place.z * 4 + y * 2 + x, core))
    to += [(place.chip + 4 * ((place.z + d) % 4 - place.z), place.core) for d in (1, 2, 3)]
    for device in to:
        pl.semaphore_signal(barrier, inc=1, device_id=device, device_id_type=MESH)
    pl.semaphore_wait(barrier, len(to))


def at_block(ref, chip, core, piece, by_core):
    return ref.at[core, chip, piece] if by_core else ref.at[chip, core, piece]


class Gather:
    def __init__(self, by_core, orders, shapes, dtype):
        self.by_core, self.orders, self.shapes, self.dtype = by_core, orders, shapes, dtype
        self.n, self.pieces = len(by_core), max(map(len, orders))

    def in_specs(self):
        return [pl.BlockSpec(memory_space=pl.ANY)] * self.n

    def out_specs(self):
        return [pl.BlockSpec(memory_space=pl.ANY)] * self.n

    def out_shape(self):
        return [
            jax.ShapeDtypeStruct(((2, 16) if bc else (16, 2)) + s, self.dtype)
            for s, bc in zip(self.shapes, self.by_core)]

    def scratch(self):
        n, pieces = self.n, self.pieces
        return [
            pltpu.SemaphoreType.DMA((n, pieces)),
            pltpu.SemaphoreType.DMA((n, pieces, 16)),
            pltpu.SemaphoreType.DMA((n,)),
            pltpu.SemaphoreType.DMA((n, pieces, 4)),
            pltpu.SemaphoreType.DMA((n,)),
        ]

    def steps(self, ins, outs, scratch):
        n, orders = self.n, self.orders
        local_sem, recv, core_recv, send, core_send = scratch
        place = Place()
        me = place.chip
        ways = {"x": 0, "y": 1, "u": 2, "d": 3}

        def slot(a, c, chip):
            return at_block(outs[a], chip, place.core, c, self.by_core[a])

        def copy(a, c, chip, way, src, sems):
            return pltpu.make_async_remote_copy(
                src_ref=src, dst_ref=slot(a, c, chip), send_sem=sems[0], recv_sem=sems[1],
                device_id=place.peer(way), device_id_type=MESH)

        def forward(a, c, order, k, ax, ay):
            chip = place.block(k, ax, ay)
            rel = {"x": ax, "y": ay, "z": k}
            last = max([i for i in range(3) if rel[order[i]] != 0], default=-1)
            src = ins[a].at[c] if last < 0 else slot(a, c, chip)
            for i in range(max(last, 0), 3):
                dim = order[i]
                if dim == "z":
                    sz = place.z_from[k]

                    @pl.when((sz <= place.z) & (place.z < 3))
                    def _():
                        copy(a, c, chip, "u", src, (send.at[a, c, 2], recv.at[a, c, chip])).start()

                    @pl.when((sz >= place.z) & (place.z > 0))
                    def _():
                        copy(a, c, chip, "d", src, (send.at[a, c, 3], recv.at[a, c, chip])).start()
                elif rel[dim] == 0:
                    copy(a, c, chip, dim, src, (send.at[a, c, ways[dim]], recv.at[a, c, chip])).start()
            copy(a, c, chip, "c", src, (core_send.at[a], core_recv.at[a])).start()

        def own(a, c):
            return pltpu.make_async_copy(ins[a].at[c], slot(a, c, me), local_sem.at[a, c])

        def entry(k, ax, ay):
            if (k, ax, ay) == (0, 0, 0):
                meet(place)
            for a in range(n):
                for c, order in enumerate(orders[a]):
                    chip = place.block(k, ax, ay)
                    if (k, ax, ay) != (0, 0, 0):
                        copy(a, c, chip, "x", slot(a, c, chip), (send.at[a, c, 0], recv.at[a, c, chip])).wait_recv()
                    forward(a, c, order, k, ax, ay)
                    if (k, ax, ay) == (0, 0, 0):
                        own(a, c).start()

        def finish():
            for a in range(n):
                for c in range(len(orders[a])):
                    own(a, c).wait()
            for a in range(n):
                whole = outs[a].at[0] if self.by_core[a] else outs[a].at[:, 0]
                pltpu.make_async_remote_copy(
                    src_ref=whole, dst_ref=whole, send_sem=core_send.at[a], recv_sem=core_recv.at[a],
                    device_id=place.peer("c"), device_id_type=MESH).wait()
                for c, order in enumerate(orders[a]):
                    def drain(way, count):
                        lead = outs[a].at[0] if self.by_core[a] else outs[a].at[:, 0]
                        part = lead.at[pl.ds(0, count), c]
                        pltpu.make_async_remote_copy(
                            src_ref=part, dst_ref=part, send_sem=send.at[a, c, ways[way]],
                            recv_sem=recv.at[a, c, 0],
                            device_id=place.peer("c"), device_id_type=MESH).wait_send()
                    before = 1
                    for dim in order:
                        if dim == "z":
                            for zz in range(4):
                                @pl.when(place.z == zz)
                                def _(zz=zz, before=before):
                                    if zz < 3:
                                        drain("u", before * (zz + 1))
                                    if zz > 0:
                                        drain("d", before * (4 - zz))
                            before *= 4
                        else:
                            drain(dim, before)
                            before *= 2

        entries = sorted(
            [(k, ax, ay) for k in range(4) for ax in range(2) for ay in range(2)], key=lambda e: e[0] + e[1] + e[2])
        return [functools.partial(entry, *e) for e in entries] + [finish]


QUARTERS = ((True, True), (True, False), (False, True), (False, False))


def as_grid(array, kind):
    lead = {True: (2, 4, 2, 2), False: (4, 2, 2, 2), "group": (2, 2, 2, 4)}[kind]
    return array.reshape(lead + array.shape[2:])


def quarter_of(ref, kind, core, y, x, c):
    if kind == "group":
        return ref.at[y, x, core, :, c]
    return ref.at[core, :, y, x, c] if kind else ref.at[:, y, x, core, c]


class Reduce:
    def __init__(self, kinds, orders, shapes):
        self.kinds, self.orders, self.shapes = kinds, orders, shapes
        self.n, self.pieces = len(kinds), max(map(len, orders))

    def in_specs(self):
        return [pl.BlockSpec(memory_space=pl.ANY)] * self.n

    def out_specs(self):
        return [pl.BlockSpec(memory_space=pltpu.VMEM)] * (self.n + 1)

    def out_shape(self):
        return [jax.ShapeDtypeStruct(s, jnp.float32) for s in self.shapes + [(1, 128)]]

    def scratch(self):
        n, pieces = self.n, self.pieces
        buffers = []
        for lead in ((2, 2, 4), (2, 2, 4), (2, 4), (4,), (4,)):
            buffers += [pltpu.VMEM(lead + s, jnp.bfloat16) for s in self.shapes]
        return buffers + [
            pltpu.SemaphoreType.DMA((n, pieces, 4)),
            pltpu.SemaphoreType.DMA((2, n, pieces, 4)),
            pltpu.SemaphoreType.DMA((2, n, pieces, 2)),
            pltpu.SemaphoreType.DMA((2, n, pieces)),
            pltpu.SemaphoreType.DMA((2, n, pieces, 4)),
        ]

    def steps(self, ins, outs, scratch, meeting=True):
        n, kinds = self.n, self.kinds
        mine, other, first, second, line = [scratch[i * n : (i + 1) * n] for i in range(5)]
        load_sem, core_sem, first_sem, second_sem, line_sem = scratch[5 * n :]
        squares = outs[n]
        place = Place()
        items = [(a, c, order) for a in range(n) for c, order in enumerate(self.orders[a])]

        def at(order, far_first, far_second):
            far = {order[2]: far_first, order[1]: far_second}
            return (1 - place.y if far["y"] else place.y, 1 - place.x if far["x"] else place.x)

        def send(src, dst, sems, index, to, index_there=None):
            return pltpu.make_async_remote_copy(
                src_ref=src, dst_ref=dst, send_sem=sems.at[(0,) + index],
                recv_sem=sems.at[(1,) + (index if index_there is None else index_there)],
                device_id=to, device_id_type=MESH)

        def load(a, c, y, x):
            return pltpu.make_async_copy(
                quarter_of(ins[a], kinds[a], place.core, y, x, c), mine[a].at[y, x, :, c], load_sem.at[a, c, y * 2 + x])

        def to_core(a, c, y, x):
            return send(
                quarter_of(ins[a], kinds[a], 1 - place.core, y, x, c), other[a].at[y, x, :, c],
                core_sem, (a, c, y * 2 + x), place.peer("c"))

        def to_first(a, c, order, far):
            y, x = at(order, True, far)
            return send(
                mine[a].at[y, x, :, c], first[a].at[int(far), :, c], first_sem, (a, c, int(far)), place.peer(order[2]))

        def to_second(a, c, order):
            y, x = at(order, False, True)
            return send(mine[a].at[y, x, :, c], second[a].at[:, c], second_sem, (a, c), place.peer(order[1]))

        def to_owner(a, c, d):
            z = (place.z + d) % 4
            return send(
                mine[a].at[place.y, place.x, z, c], line[a].at[place.z, c], line_sem, (a, c, d),
                (place.chip + 4 * (z - place.z), place.core), (a, c, place.z))

        def from_line(a, c, d):
            z = (place.z + d) % 4
            return send(
                mine[a].at[place.y, place.x, z, c], line[a].at[z, c], line_sem, (a, c, d),
                (place.chip + 4 * (z - place.z), place.core), (a, c, z))

        def add(a, c, y, x, more):
            def one(z, carry):
                mine[a][y, x, z, c] = mine[a][y, x, z, c] + more(z)
                return carry
            lax.fori_loop(0, 4, one, 0)

        def begin():
            if meeting:
                meet(place)
            squares[...] = jnp.zeros_like(squares)
            for quarter in QUARTERS:
                for a, c, order in items:
                    y, x = at(order, *quarter)
                    to_core(a, c, y, x).start()
                    load(a, c, y, x).start()

        def fold(item, quarter):
            a, c, order = item
            y, x = at(order, *quarter)
            load(a, c, y, x).wait()
            to_core(a, c, y, x).wait_recv()
            add(a, c, y, x, lambda z: other[a][y, x, z, c])
            if quarter[0]:
                to_first(a, c, order, quarter[1]).start()

        def take_first(item, far):
            a, c, order = item
            y, x = at(order, False, far)
            to_first(a, c, order, far).wait_recv()
            add(a, c, y, x, lambda z: first[a][int(far), z, c])
            if far:
                to_second(a, c, order).start()

        def take_second(item):
            a, c, order = item
            to_second(a, c, order).wait_recv()
            add(a, c, place.y, place.x, lambda z: second[a][z, c])
            for d in (1, 2, 3):
                to_owner(a, c, d).start()

        def last(item):
            a, c, order = item
            total = mine[a][place.y, place.x, place.z, c].astype(jnp.float32)
            for d in (1, 2, 3):
                from_line(a, c, d).wait_recv()
                total += line[a][(place.z + d) % 4, c].astype(jnp.float32)
            outs[a][c] = total
            by_lane = jnp.sum(total * total, 0, keepdims=True)
            for k in range(by_lane.shape[1] // 128):
                squares[...] += by_lane[:, k * 128 : (k + 1) * 128]

        def finish():
            for a, c, order in items:
                for quarter in QUARTERS:
                    to_core(a, c, *at(order, *quarter)).wait_send()
                to_first(a, c, order, True).wait_send()
                to_first(a, c, order, False).wait_send()
                to_second(a, c, order).wait_send()
                for d in (1, 2, 3):
                    to_owner(a, c, d).wait_send()

        part = functools.partial
        out = [begin]
        for quarter in QUARTERS:
            out += [part(fold, it, quarter) for it in items]
        for far in (True, False):
            out += [part(take_first, it, far) for it in items]
        out += [part(take_second, it) for it in items]
        return out + [part(last, it) for it in items] + [finish]


class Spread:
    wide = True

    def __init__(self, shapes, dtypes):
        self.shapes, self.dtypes, self.n = shapes, dtypes, len(shapes)

    def in_specs(self):
        return [pl.BlockSpec(memory_space=pl.ANY)] * self.n

    def out_specs(self):
        return [pl.BlockSpec(memory_space=pl.ANY)] * self.n

    def out_shape(self):
        return [jax.ShapeDtypeStruct((2, 2, 2, 4) + s, d) for s, d in zip(self.shapes, self.dtypes)]

    def scratch(self):
        n = self.n
        return [
            pltpu.SemaphoreType.DMA((n,)),
            pltpu.SemaphoreType.DMA((2, n, 4)),
            pltpu.SemaphoreType.DMA((2, n, 8)),
        ]

    def steps(self, ins, outs, scratch, meeting=True):
        local_sem, line_sem, group_sem = scratch
        place = Place()

        def own(a):
            return pltpu.make_async_copy(
                ins[a], outs[a].at[place.y, place.x, place.core, place.z], local_sem.at[a])

        def along(a, d, back):
            z = (place.z + d) % 4
            at = z if back else place.z
            return pltpu.make_async_remote_copy(
                src_ref=ins[a], dst_ref=outs[a].at[place.y, place.x, place.core, at],
                send_sem=line_sem.at[0, a, d], recv_sem=line_sem.at[1, a, at],
                device_id=(place.chip + 4 * (z - place.z), place.core), device_id_type=MESH)

        def across(a, k, back):
            to = place.group(k)
            y, x, core = to if back else (place.y, place.x, place.core)
            part = outs[a].at[y, x, core]
            return pltpu.make_async_remote_copy(
                src_ref=part, dst_ref=part, send_sem=group_sem.at[0, a, k], recv_sem=group_sem.at[1, a, k],
                device_id=(place.z * 4 + to[0] * 2 + to[1], to[2]), device_id_type=MESH)

        def begin():
            if meeting:
                meet(place, True)
            for a in range(self.n):
                for d in (1, 2, 3):
                    along(a, d, False).start()
                own(a).start()

        def middle():
            for a in range(self.n):
                own(a).wait()
                for d in (1, 2, 3):
                    along(a, d, True).wait_recv()
                for k in range(1, 8):
                    across(a, k, False).start()

        def end():
            for a in range(self.n):
                for k in range(1, 8):
                    across(a, k, True).wait_recv()
            for a in range(self.n):
                for d in (1, 2, 3):
                    along(a, d, False).wait_send()
                for k in range(1, 8):
                    across(a, k, False).wait_send()

        return [begin, middle, end]


class Both:
    wide = True

    def __init__(self, one, two):
        self.parts, self.n = (one, two), one.n + two.n

    def both(self, name):
        return getattr(self.parts[0], name)() + getattr(self.parts[1], name)()

    def in_specs(self):
        return self.both("in_specs")

    def out_specs(self):
        return self.both("out_specs")

    def out_shape(self):
        return self.both("out_shape")

    def scratch(self):
        return self.both("scratch")

    def steps(self, ins, outs, scratch, meeting=True):
        one, two = self.parts
        n_out, n_scratch = len(one.out_shape()), len(one.scratch())
        lists = (
            one.steps(ins[: one.n], outs[:n_out], scratch[:n_scratch], False),
            two.steps(ins[one.n :], outs[n_out:], scratch[n_scratch:], False))
        timed = [(i / (len(steps) - 1), step) for steps in lists for i, step in enumerate(steps)]
        return [lambda: meet(Place(), True)] + [step for _, step in sorted(timed, key=lambda t: t[0])]


VMEM_ALL = 64 * 1024 * 1024 - 65536


class Aside:
    def __init__(self, plan, arrays, collective_id):
        self.plan, self.arrays, self.collective_id = plan, arrays, collective_id


def with_aside(body, aside, *, grid, in_specs, out_specs, out_shape, scratch_shapes=(), cost, operands):
    if aside is None:
        out = pl.pallas_call(
            body, grid=grid, in_specs=in_specs, out_specs=out_specs, out_shape=tuple(out_shape),
            scratch_shapes=scratch_shapes, cost_estimate=cost,
            compiler_params=pltpu.CompilerParams(vmem_limit_bytes=VMEM_ALL))(*operands)
        return out, None
    plan = aside.plan
    n_in, n_out, n_scr, n, n_plan = len(in_specs), len(out_specs), len(scratch_shapes), plan.n, len(plan.out_shape())
    cells = 1
    for extent in grid:
        cells *= extent

    def kernel(*refs):
        refs = list(refs)
        ins, refs = refs[:n_in], refs[n_in:]
        plan_ins, refs = refs[:n], refs[n:]
        outs, refs = refs[:n_out], refs[n_out:]
        plan_outs, refs = refs[:n_plan], refs[n_plan:]
        scratch, plan_scratch = refs[:n_scr], refs[n_scr:]
        steps = plan.steps(plan_ins, plan_outs, plan_scratch)
        cell = 0
        for axis, extent in enumerate(grid):
            cell = cell * extent + pl.program_id(axis)
        by_cell = {}
        for i, step in enumerate(steps):
            by_cell.setdefault(i * (cells - 1) // (len(steps) - 1), []).append(step)
        for index in sorted(by_cell):
            if index < cells - 1:
                @pl.when(cell == index)
                def _():
                    for step in by_cell[index]:
                        step()
        body(*ins, *outs, *scratch)

        @pl.when(cell == cells - 1)
        def _():
            for step in by_cell[cells - 1]:
                step()

    out = pl.pallas_call(
        kernel, grid=grid,
        in_specs=list(in_specs) + plan.in_specs(), out_specs=list(out_specs) + plan.out_specs(),
        out_shape=tuple(out_shape) + tuple(plan.out_shape()),
        scratch_shapes=list(scratch_shapes) + plan.scratch(), cost_estimate=cost,
        compiler_params=pltpu.CompilerParams(
            collective_id=aside.collective_id, has_side_effects=True, vmem_limit_bytes=VMEM_ALL),
    )(*operands, *aside.arrays)
    return out[:n_out], out[n_out:]


def exchange(plan, arrays, collective_id):
    n = plan.n
    n_all = n + len(plan.out_shape())

    def kernel(*refs):
        for step in plan.steps(refs[:n], refs[n:n_all], refs[n_all:]):
            step()

    moved = sum(a.size for a in arrays) * 2
    return pl.pallas_call(
        kernel,
        out_shape=tuple(plan.out_shape()),
        in_specs=plan.in_specs(),
        out_specs=plan.out_specs(),
        scratch_shapes=plan.scratch(),
        compiler_params=pltpu.CompilerParams(
            collective_id=collective_id, has_side_effects=True, vmem_limit_bytes=VMEM_ALL),
        cost_estimate=pl.CostEstimate(flops=0, bytes_accessed=32 * moved, transcendentals=0),
    )(*arrays)


def gather_plan(arrays, by_core, orders):
    return Gather(by_core, orders, [a.shape for a in arrays], arrays[0].dtype)


def reduce_plan(arrays, kinds, orders):
    return Reduce(kinds, orders, [a.shape[2:] for a in arrays]), [as_grid(a, kind) for a, kind in zip(arrays, kinds)]


def spread_plan(arrays):
    return Spread([a.shape for a in arrays], [a.dtype for a in arrays])


def all_gather_layer(arrays, by_core, orders, collective_id):
    return exchange(gather_plan(arrays, by_core, orders), arrays, collective_id)


def reduce_scatter_layer(arrays, kinds, orders, collective_id):
    plan, operands = reduce_plan(arrays, kinds, orders)
    return exchange(plan, operands, collective_id)


HD = 64
CTX = 768

eps_norm = 1e-05
clip_at = 0.01
rate = 3000.0
moment = 0.9
keep_avg = 0.9
decay_wd = 1e-05
low_type = jnp.bfloat16
wide_type = jnp.float32


def layer_norm(values, gain_row, shift_row):
    center = values - jnp.mean(values, -1, keepdims=True)
    spread = jnp.mean(center * center, -1, keepdims=True)
    return center * lax.rsqrt(spread + eps_norm) * gain_row + shift_row


def norm_back(values, gain_row, shift_row, upstream):
    _, pull = jax.vjp(layer_norm, values, gain_row, shift_row)
    return pull(upstream)


def gelu_back(values, upstream):
    _, pull = jax.vjp(jax.nn.gelu, values)
    return pull(upstream)[0]


def matmul(first_op, second_op):
    return jnp.dot(first_op, second_op, preferred_element_type=wide_type)


def contract(first_op, second_op, first_dim, second_dim):
    return lax.dot_general(
        first_op, second_op, (((first_dim,), (second_dim,)), ((), ())), preferred_element_type=wide_type
    )


def matmul_tn(first_op, second_op):
    return contract(first_op, second_op, 0, 0)


def matmul_nt(first_op, second_op):
    return contract(first_op, second_op, 1, 1)


def head_lanes(shape, head):
    lane = lax.broadcasted_iota(jnp.int32, shape, 1)
    mine = (lane < HD) if head == 0 else (lane >= HD)
    return mine, lane == (HD if head == 0 else 0)


def attend_kernel(q_ref, k_ref, v_ref, bias_ref, out_ref, lse_ref):
    q_block = q_ref[0] * jnp.asarray(HD ** -0.5, low_type)
    k_block, v_block, bias = k_ref[0], v_ref[0], bias_ref[...]
    v_turned = v_block.T
    parts = []
    for head in range(2):
        q_mine, q_one = head_lanes(q_block.shape, head)
        k_mine, _ = head_lanes(k_block.shape, head)
        one = jnp.where(q_one, jnp.ones_like(q_block), jnp.zeros_like(q_block))
        score = matmul_nt(jnp.where(k_mine, k_block, bias), jnp.where(q_mine, q_block, one))
        peak = jnp.max(score, 0, keepdims=True)
        lifted = jnp.exp(score - peak)
        total = jnp.sum(lifted, 0, keepdims=True)
        mixed = matmul(v_turned[head * HD : (head + 1) * HD], lifted.astype(low_type))
        parts.append(mixed / total)
        lse_ref[0, head : head + 1, :] = peak + jnp.log(total)
    out_ref[...] = jnp.concatenate(parts, 0).T.astype(low_type)


def attend(queries, keys_values, bias, aside):
    groups, rows, width = queries.shape
    pairs = width // 128
    block = min(256, rows)
    grid = (groups * pairs, rows // block)
    (mixed, lse), extra = with_aside(
        attend_kernel,
        aside,
        grid=grid,
        in_specs=[
            pl.BlockSpec((1, block, 128), lambda p, i: (p // pairs, i, p % pairs)),
            pl.BlockSpec((1, CTX, 128), lambda p, i: (p // pairs, 0, p % pairs)),
            pl.BlockSpec((1, CTX, 128), lambda p, i: (p // pairs, 0, pairs + p % pairs)),
            pl.BlockSpec((CTX, 128), lambda p, i: (0, 0)),
        ],
        out_specs=[
            pl.BlockSpec((block, 128), lambda p, i: (i, p)),
            pl.BlockSpec((1, 2, block), lambda p, i: (p, 0, i)),
        ],
        out_shape=(
            jax.ShapeDtypeStruct((rows, groups * width), low_type),
            jax.ShapeDtypeStruct((groups * pairs, 2, rows), wide_type),
        ),
        cost=pl.CostEstimate(
            flops=4 * rows * CTX * groups * width, bytes_accessed=8 * rows * groups * width,
            transcendentals=rows * CTX * groups * width // HD),
        operands=(queries, keys_values, keys_values, bias),
    )
    return mixed, lse, extra


def attend_back_kernel(q_ref, k_ref, v_ref, bias_ref, g_ref, o_ref, lse_ref, gq_ref, gk_ref, gv_ref, k_sum, v_sum):
    step = pl.program_id(1)

    @pl.when(step == 0)
    def _():
        k_sum[...] = jnp.zeros_like(k_sum)
        v_sum[...] = jnp.zeros_like(v_sum)

    scale = HD ** -0.5
    q_block = q_ref[0] * jnp.asarray(scale, low_type)
    k_block, v_block, bias = k_ref[0], v_ref[0], bias_ref[...]
    g_block = g_ref[...]
    k_turned = k_block.T
    both = (g_block.astype(wide_type) * o_ref[...].astype(wide_type)).T
    parts = []
    for head in range(2):
        q_mine, q_one = head_lanes(q_block.shape, head)
        k_mine, _ = head_lanes(k_block.shape, head)
        nothing = jnp.zeros_like(q_block)
        one = jnp.where(q_one, jnp.ones_like(q_block), nothing)
        score = matmul_nt(jnp.where(k_mine, k_block, bias), jnp.where(q_mine, q_block, one))
        prob = jnp.exp(score - lse_ref[0, head : head + 1, :])
        g_mine = jnp.where(q_mine, g_block, nothing)
        grad_prob = matmul_nt(v_block, g_mine)
        inner = jnp.sum(both[head * HD : (head + 1) * HD], 0, keepdims=True)
        grad_score = (prob * (grad_prob - inner)).astype(low_type)
        v_sum[...] += matmul(prob.astype(low_type), g_mine)
        k_sum[...] += matmul(grad_score, jnp.where(q_mine, q_block, nothing))
        parts.append(matmul(k_turned[head * HD : (head + 1) * HD], grad_score) * scale)
    gq_ref[0] = jnp.concatenate(parts, 0).T.astype(low_type)

    @pl.when(step == pl.num_programs(1) - 1)
    def _():
        gk_ref[0] = k_sum[...].astype(low_type)
        gv_ref[0] = v_sum[...].astype(low_type)


def attend_back(queries, keys_values, bias, grad_mixed, mixed, lse, aside):
    groups, rows, width = queries.shape
    pairs = width // 128
    block = min(256, rows)
    grid = (groups * pairs, rows // block)
    row_spec = pl.BlockSpec((block, 128), lambda p, i: (i, p))
    key_out = pl.BlockSpec((1, CTX, 128), lambda p, i: (p // pairs, 0, p % pairs))
    grads, extra = with_aside(
        attend_back_kernel,
        aside,
        grid=grid,
        in_specs=[
            pl.BlockSpec((1, block, 128), lambda p, i: (p // pairs, i, p % pairs)),
            pl.BlockSpec((1, CTX, 128), lambda p, i: (p // pairs, 0, p % pairs)),
            pl.BlockSpec((1, CTX, 128), lambda p, i: (p // pairs, 0, pairs + p % pairs)),
            pl.BlockSpec((CTX, 128), lambda p, i: (0, 0)),
            row_spec,
            row_spec,
            pl.BlockSpec((1, 2, block), lambda p, i: (p, 0, i)),
        ],
        out_specs=[
            pl.BlockSpec((1, block, 128), lambda p, i: (p // pairs, i, p % pairs)),
            key_out,
            key_out,
        ],
        out_shape=(
            jax.ShapeDtypeStruct(queries.shape, low_type),
            jax.ShapeDtypeStruct((groups, CTX, width), low_type),
            jax.ShapeDtypeStruct((groups, CTX, width), low_type),
        ),
        scratch_shapes=[pltpu.VMEM((CTX, 128), wide_type)] * 2,
        cost=pl.CostEstimate(
            flops=10 * rows * CTX * groups * width, bytes_accessed=16 * rows * groups * width,
            transcendentals=rows * CTX * groups * width // HD),
        operands=(queries, keys_values, keys_values, bias, grad_mixed, mixed, lse),
    )
    return tuple(grads) + (extra,)


def grouped(rows, weight):
    return jnp.einsum("rd,gdc->grc", rows, weight, preferred_element_type=wide_type)


GELU_K = 0.7978845608028654
GELU_C = 0.044715


def center_scale(values):
    center = values - jnp.mean(values, -1, keepdims=True)
    return center, lax.rsqrt(jnp.mean(center * center, -1, keepdims=True) + eps_norm)


def mlp_kernel(res_ref, mixed_ref, mix_ref, up_ref, down_ref, vec_ref, out_ref, middle_ref, hidden_ref, normed, total):
    step, last = pl.program_id(1), pl.num_programs(1) - 1
    size = hidden_ref.shape[1]

    @pl.when(step == 0)
    def _():
        middle = res_ref[...] + matmul(mixed_ref[...], mix_ref[...]) + vec_ref[4:5]
        middle_ref[...] = middle
        center, spread = center_scale(middle)
        normed[...] = (center * spread * vec_ref[2:3] + vec_ref[3:4]).astype(low_type)
        total[...] = middle + vec_ref[5:6]

    part = pl.ds(pl.multiple_of(step * size, size), size)
    hidden = matmul(normed[...], up_ref[:, part])
    hidden_ref[...] = hidden.astype(low_type)
    inner = jnp.tanh(GELU_K * (hidden + GELU_C * hidden * hidden * hidden))
    active = (0.5 * hidden * (1.0 + inner)).astype(low_type)
    total[...] += matmul(active, down_ref[part, :])

    @pl.when(step == last)
    def _():
        out_ref[...] = total[...]


def mlp_forward(residual, first, mixed, weights, vec_rows, aside):
    _, w_mix, w_grow, w_shrink = weights
    rows, width = mixed.shape
    wide = w_grow.shape[1]
    block, chunk = 256, 512
    skip = first // block

    def whole(a):
        return pl.BlockSpec(a.shape, lambda i, j: (0, 0), pipeline_mode=pl.Buffered(1))

    row_spec = pl.BlockSpec((block, width), lambda i, j: (i, 0))
    outs, extra = with_aside(
        mlp_kernel,
        aside,
        grid=(rows // block, wide // chunk),
        in_specs=[
            pl.BlockSpec((block, width), lambda i, j: (i + skip, 0)), row_spec,
            whole(w_mix), whole(w_grow), whole(w_shrink), whole(vec_rows),
        ],
        out_specs=[row_spec, row_spec, pl.BlockSpec((block, chunk), lambda i, j: (i, j))],
        out_shape=(
            jax.ShapeDtypeStruct((rows, width), wide_type),
            jax.ShapeDtypeStruct((rows, width), wide_type),
            jax.ShapeDtypeStruct((rows, wide), low_type),
        ),
        scratch_shapes=[pltpu.VMEM((block, width), low_type), pltpu.VMEM((block, width), wide_type)],
        cost=pl.CostEstimate(
            flops=2 * rows * width * (2 * wide + width), bytes_accessed=rows * width * 24, transcendentals=rows * wide),
        operands=(residual, mixed, w_mix, w_grow, w_shrink, vec_rows),
    )
    return outs, extra


def mlp_back_kernel(
    u_ref, middle_ref, mixed_ref, mix_ref, up_ref, down_ref, vec_ref, hidden_ref,
    up_grad_ref, down_grad_ref, mix_grad_ref, mixed_grad_ref, mid_grad_ref, vec_grad_ref,
    u_low, normed_turned, normed_grad,
):
    step, last = pl.program_id(0), pl.num_programs(0) - 1
    rows, width = u_ref.shape
    block = 256

    @pl.when(step == 0)
    def _():
        @pl.loop(0, rows // block)
        def _(i):
            part = pl.ds(pl.multiple_of(i * block, block), block)
            center, spread = center_scale(middle_ref[part, :])
            normed = (center * spread * vec_ref[2:3] + vec_ref[3:4]).astype(low_type)
            normed_turned[:, part] = normed.T
            u_low[part, :] = u_ref[part, :].astype(low_type)
            normed_grad[part, :] = jnp.zeros((block, width), wide_type)

    hidden = hidden_ref[...].astype(wide_type)
    square = hidden * hidden
    inner = jnp.tanh(GELU_K * hidden * (1.0 + GELU_C * square))
    half = 0.5 * (1.0 + inner)
    active = (hidden * half).astype(low_type)
    slope = half + 0.5 * hidden * (1.0 - inner * inner) * (GELU_K * (1.0 + 3.0 * GELU_C * square))
    grad = (matmul_nt(u_low[...], down_ref[...]) * slope).astype(low_type)
    down_grad_ref[...] = matmul(active.T, u_low[...]).astype(low_type)
    up_grad_ref[...] = matmul(normed_turned[...], grad).astype(low_type)
    normed_grad[...] += matmul_nt(grad, up_ref[...])

    @pl.when(step == last)
    def _():
        vec_grad_ref[...] = jnp.zeros_like(vec_grad_ref)

        @pl.loop(0, rows // block)
        def _(i):
            part = pl.ds(pl.multiple_of(i * block, block), block)
            center, spread = center_scale(middle_ref[part, :])
            shape = center * spread
            grads = normed_grad[part, :]
            scaled = grads * vec_ref[2:3]
            from_norm = spread * (
                scaled - jnp.mean(scaled, -1, keepdims=True) - shape * jnp.mean(scaled * shape, -1, keepdims=True))
            u_part = u_ref[part, :]
            total = from_norm + u_part
            mid_grad_ref[part, :] = total
            vec_grad_ref[0:1] += jnp.sum(grads * shape, 0, keepdims=True)
            vec_grad_ref[1:2] += jnp.sum(grads, 0, keepdims=True)
            vec_grad_ref[2:3] += jnp.sum(total, 0, keepdims=True)
            vec_grad_ref[3:4] += jnp.sum(u_part, 0, keepdims=True)
            low = total.astype(low_type)
            u_low[part, :] = low
            mixed_grad_ref[part, :] = matmul_nt(low, mix_ref[...]).astype(low_type)
            normed_turned[:, part] = mixed_ref[part, :].T
        mix_grad_ref[...] = matmul(normed_turned[...], u_low[...]).astype(low_type)


def mlp_backward(upstream, middle, mixed, weights, vec_rows, hidden, aside):
    _, w_mix, w_grow, w_shrink = weights
    rows, width = upstream.shape
    wide = hidden.shape[1]
    chunk = 256

    def whole(shape):
        return pl.BlockSpec(shape, lambda j: (0, 0), pipeline_mode=pl.Buffered(1))

    square, row_shape = (width, width), (rows, width)
    up_spec = pl.BlockSpec((width, chunk), lambda j: (0, j))
    down_spec = pl.BlockSpec((chunk, width), lambda j: (j, 0))
    return with_aside(
        mlp_back_kernel,
        aside,
        grid=(wide // chunk,),
        in_specs=[
            whole(row_shape), whole(row_shape), whole(row_shape), whole(square), up_spec, down_spec,
            whole(vec_rows.shape), pl.BlockSpec((rows, chunk), lambda j: (0, j)),
        ],
        out_specs=[up_spec, down_spec] + [
            pl.BlockSpec(s, lambda j: (0, 0)) for s in (square, row_shape, row_shape, (8, width))],
        out_shape=(
            jax.ShapeDtypeStruct((width, wide), low_type),
            jax.ShapeDtypeStruct((wide, width), low_type),
            jax.ShapeDtypeStruct(square, low_type),
            jax.ShapeDtypeStruct(row_shape, low_type),
            jax.ShapeDtypeStruct(row_shape, wide_type),
            jax.ShapeDtypeStruct((8, width), wide_type),
        ),
        scratch_shapes=[
            pltpu.VMEM(row_shape, low_type), pltpu.VMEM((width, rows), low_type), pltpu.VMEM(row_shape, wide_type)],
        cost=pl.CostEstimate(
            flops=4 * rows * width * (2 * wide + width), bytes_accessed=rows * width * 40, transcendentals=rows * wide),
        operands=(upstream, middle, mixed, w_mix, w_grow, w_shrink, vec_rows, hidden),
    )


def layer_forward(residual, first, vec_rows, weights, bias, asides, as_rest):
    w_joined = weights[0]
    width = w_joined.shape[2] // 3
    normed = layer_norm(residual, vec_rows[0], vec_rows[1]).astype(low_type)
    queries = grouped(normed[first:], w_joined[:, :, :width]).astype(low_type)
    keys_values = grouped(normed[:CTX], w_joined[:, :, width:]).astype(low_type)
    mixed, lse, extra = attend(queries, keys_values, bias, asides[0])
    if len(weights) == 1:
        weights = weights + as_rest(extra)
    (output, middle, hidden), more = mlp_forward(residual, first, mixed, weights, vec_rows, asides[1])
    return output, weights, more, (residual, normed, queries, keys_values, mixed, lse, middle, hidden)


def layer_backward(upstream, kept, first, vec_rows, weights, bias, make_asides):
    w_joined = weights[0]
    width = w_joined.shape[2] // 3
    residual, normed, queries, keys_values, mixed, lse, middle, hidden = kept
    outs, extra = mlp_backward(upstream, middle, mixed, weights, vec_rows, hidden, make_asides(0, None, None))
    grad_grow, grad_shrink, grad_mix, grad_mixed, grad_middle, mlp_vec = outs
    grad_q, grad_k, grad_v, more = attend_back(
        queries, keys_values, bias, grad_mixed, mixed, lse, make_asides(1, (grad_mix, grad_grow, grad_shrink), extra))

    def weight_grad(rows, grads):
        return jnp.einsum("rd,grc->gdc", rows, grads, preferred_element_type=wide_type).astype(low_type)

    def row_grad(grads, part):
        return jnp.einsum(
            "grc,gdc->rd", grads, w_joined[:, :, part * width : (part + 1) * width], preferred_element_type=wide_type)

    grad_joined = jnp.concatenate(
        [weight_grad(normed[first:], grad_q), weight_grad(normed[:CTX], grad_k), weight_grad(normed[:CTX], grad_v)], 2)
    from_q = row_grad(grad_q, 0)
    from_kv = row_grad(grad_k, 1) + row_grad(grad_v, 2)
    rows = residual.shape[0]
    below = jnp.zeros((first, from_q.shape[1]), wide_type)
    tail = jnp.zeros((rows - CTX, from_q.shape[1]), wide_type)
    grad_normed = jnp.concatenate([below, from_q], 0) + jnp.concatenate([from_kv, tail], 0)
    grad_input, gain_attn, shift_attn = norm_back(residual, vec_rows[0], vec_rows[1], grad_normed)
    vec_grads = [gain_attn, shift_attn, mlp_vec[0], mlp_vec[1], mlp_vec[2], mlp_vec[3]]
    grad_out = grad_input + jnp.concatenate([below, grad_middle], 0)
    return grad_out, (extra, more), (grad_joined, grad_mix, grad_grow, grad_shrink), vec_grads


def update(weight, moment_old, average, grad_in, scale):
    applied = grad_in * scale + decay_wd * weight
    moment_new = moment * moment_old + applied
    weight_new = weight - rate * (applied + moment * moment_new)
    return (weight_new, moment_new, keep_avg * average + (1.0 - keep_avg) * weight_new)


BY_CORE = (True, True, False, False)
ROUTES = (("zxy",), ("zxy",), ("xzy",), ("yzx",))
REDUCE_ROUTES = (("zxy",), ("zyx",), ("zyx",), ("zxy",))


def whole_gather(shard_list, by_core):
    return [
        lax.all_gather(lax.all_gather(shard, "dp", axis=0), "head", axis=0 if bc else 1)
        for shard, bc in zip(shard_list, by_core)]


def as_blocks(grads, by_core, rows_list, routes):
    chips, cores = lax.axis_size("dp"), lax.axis_size("head")
    return [
        grad.reshape(((cores, chips) if bc else (chips, cores)) + (len(route), rows // len(route), -1))
        for grad, bc, rows, route in zip(grads, by_core, rows_list, routes)]


def whole_scatter(grads, by_core, rows_list):
    outs = []
    for grad, bc in zip(as_blocks(grads, by_core, rows_list, ROUTES), by_core):
        half = lax.psum_scatter(grad.astype(wide_type), "head", scatter_dimension=0 if bc else 1)
        outs.append(lax.psum_scatter(half, "dp", scatter_dimension=0))
    return outs


def shards(
    rows_in, feat_mask, counts, ctx_vals, targets, query_mask,
    w_emb, m_emb, a_emb, vectors, m_vec, a_vec,
    w_qkv, m_qkv, a_qkv, w_out, m_out, a_out, w_up, m_up, a_up, w_down, m_down, a_down,
    w_head, m_head, a_head,
):
    chips, cores = lax.axis_size("dp"), lax.axis_size("head")
    direct = (chips, cores) == (16, 2)
    _, row_count, feat_count = rows_in.shape
    layer_total = w_qkv.shape[0]
    width = w_emb.shape[1]
    joined_rows = w_qkv.shape[1]
    kinds = w_qkv.shape[2] * w_qkv.shape[4]

    def own_weights(at):
        return [
            w_qkv[at].reshape((joined_rows, kinds)).astype(low_type)[None],
            w_out[at, 0].astype(low_type)[None],
            w_up[at].astype(low_type)[None],
            w_down[at].astype(low_type)[None],
        ]

    def as_joined(qkv):
        return (qkv.reshape((cores, width, kinds)),)

    def as_rest(gathered):
        out, up, down = gathered
        return (out.reshape((width, width)), up.reshape((width, -1)), down.reshape((-1, width)))

    own = [own_weights(at) for at in range(layer_total)]
    forward_asides = [[None, None] for _ in own]
    if direct:
        joined = own[0][0].reshape((3, joined_rows // 3, kinds))
        weights = [as_joined(all_gather_layer([joined], (True,), (("xzy", "yzx", "zxy"),), 1)[0])]
        for at, layer in enumerate(own):
            if at == 0:
                forward_asides[at][0] = Aside(
                    gather_plan(layer[1:], BY_CORE[1:], (("xzy",), ("zxy",), ("zyx",))), layer[1:], 2)
            else:
                forward_asides[at - 1][1] = Aside(gather_plan(layer, BY_CORE, ROUTES), layer, 10 + at)
    else:
        gathered = [whole_gather(o, BY_CORE) for o in own]
        weights = [as_joined(g[0]) + as_rest(g[1:]) for g in gathered]

    table = lax.axis_index("dp") * cores + lax.axis_index("head")
    count = lax.dynamic_slice_in_dim(counts, table, 1, 0)
    bias = jnp.where(jnp.arange(CTX) < count, 0.0, -1e30).astype(low_type)
    bias = jnp.broadcast_to(bias[:, None], (CTX, 128))
    masked = rows_in[0] * feat_mask[0][None, :].astype(low_type)
    leading = jnp.concatenate([ctx_vals[0], jnp.zeros((row_count - CTX,), wide_type)])[:, None]
    residual = matmul(masked, w_emb.astype(low_type)) + vectors[1] + leading * vectors[0]
    kept_all = []
    for at in range(layer_total):
        first = CTX if at == layer_total - 1 else 0
        residual, weights[at], extra, kept = layer_forward(
            residual, first, vectors[2 + 6 * at : 8 + 6 * at], weights[at], bias, forward_asides[at], as_rest)
        if extra is not None:
            weights.append(as_joined(extra[0]) + as_rest(extra[1:]))
        kept_all.append(kept)

    head_low = w_head.astype(low_type)
    final_rows = layer_norm(residual, vectors[-2], vectors[-1]).astype(low_type)
    logits = matmul(final_rows, head_low)
    row_peak = jnp.max(logits, -1, keepdims=True)
    log_total = row_peak[:, 0] + jnp.log(jnp.sum(jnp.exp(logits - row_peak), -1))
    target_hit = (jnp.arange(logits.shape[1])[None, :] == targets[0][:, None]).astype(wide_type)
    picked = jnp.sum(logits * target_hit, -1)
    row_weight = query_mask[0].astype(wide_type)
    loss_part = jnp.sum((log_total - picked) * row_weight)
    grad_logits = ((jnp.exp(logits - log_total[:, None]) - target_hit) * row_weight[:, None]).astype(low_type)
    grad_head = matmul_tn(final_rows, grad_logits).astype(low_type)
    upstream, gain_final, shift_final = norm_back(
        residual, vectors[-2], vectors[-1], matmul_nt(grad_logits, head_low))

    devices = chips * cores
    rows_list = [joined_rows, w_out.shape[2], w_up.shape[1], w_down.shape[1]]
    sums = [None] * layer_total
    vec_grads = [None] * layer_total
    squares = []
    big = None
    for at in reversed(range(layer_total)):
        first = CTX if at == layer_total - 1 else 0
        above = big

        def make_asides(turn, ready, earlier):
            if not direct or above is None:
                return None
            if turn == 0:
                blocks = as_blocks(
                    list(above) + [grad_head], BY_CORE + (False,), rows_list + [w_head.shape[0] // devices],
                    REDUCE_ROUTES + (("zyx",),))
                plan, operands = reduce_plan(blocks, BY_CORE + ("group",), REDUCE_ROUTES + (("zyx",),))
                return Aside(plan, operands, 3)
            blocks = as_blocks(ready, BY_CORE[1:], rows_list[1:], REDUCE_ROUTES[1:])
            plan, operands = reduce_plan(blocks, BY_CORE[1:], REDUCE_ROUTES[1:])
            head_sum = [earlier[4][0].astype(low_type)]
            return Aside(Both(plan, spread_plan(head_sum)), operands + head_sum, 7)

        upstream, extra, big, vec_grads[at] = layer_backward(
            upstream, kept_all[at], first, vectors[2 + 6 * at : 8 + 6 * at], weights[at], bias, make_asides)
        if not direct:
            sums[at] = whole_scatter(big, BY_CORE, rows_list)
        elif extra[0] is not None:
            sums[at + 1] = list(extra[0][:4])
            sums[at] = list(extra[1][:3])
            squares += [extra[0][5], extra[1][3]]
            head_all = extra[1][4]
    grad_emb = matmul_tn(masked, upstream.astype(low_type))
    vec_list = [jnp.sum(upstream * leading, 0), jnp.sum(upstream, 0)]
    for at in range(layer_total):
        vec_list = vec_list + vec_grads[at]
    grad_vec = jnp.stack(vec_list + [gain_final, shift_final])

    scalars = [loss_part, jnp.sum(row_weight)]
    if direct:
        feats, vec_total = w_emb.shape[0], vectors.shape[0]
        n_small = -(-(feats + vec_total) // (8 * devices)) * 8
        small = jnp.concatenate([grad_emb, grad_vec], 0).astype(low_type)
        small = jnp.pad(small, ((0, n_small * devices - feats - vec_total), (0, 0)))
        kinds_last, routes = (True, "group"), (("zxy", "zyx"), ("zyx",))
        blocks = as_blocks([big[0], small], (True, False), [joined_rows, n_small], routes)
        qkv_sum, small_sum, square = reduce_scatter_layer(blocks, kinds_last, routes, 4)
        sums[0] = [qkv_sum] + sums[0]
        scalars = jnp.stack([jnp.sum(sum(squares + [square]))] + scalars)
        scalars = jnp.broadcast_to(jnp.pad(scalars, (0, 125))[None], (8, 128))
        last_parts = [small_sum[0].astype(low_type), scalars]
        small_all, totals = exchange(spread_plan(last_parts), last_parts, 5)
        small_all = small_all.reshape((devices * n_small, width)).astype(wide_type)
        totals = jnp.sum(totals[..., 0, :3].reshape((devices, 3)), 0)
        grad_emb, grad_vec = small_all[:feats], small_all[feats : feats + vec_total]
        grad_head = head_all.reshape(w_head.shape).astype(wide_type)
    else:
        names = ("dp", "head")
        square = sum(jnp.sum(p * p) for ps in sums for p in ps)
        totals = lax.psum(jnp.stack([square] + scalars), names)
        grad_head = lax.psum(grad_head.astype(wide_type), names)
        grad_emb, grad_vec = lax.psum(grad_emb, names), lax.psum(grad_vec, names)
        alike = sum(jnp.sum(g * g) for g in (grad_head, grad_emb, grad_vec))
        totals = jnp.stack([totals[0] + alike, totals[1], totals[2]])
    pooled = totals[2]
    loss = totals[1] / pooled
    grad_norm = jnp.sqrt(totals[0]) / pooled
    scale = jnp.minimum(1.0, clip_at / grad_norm) / pooled

    def big_update(weight, moment_old, average, kind):
        grad = jnp.stack([sums[at][kind].reshape(weight.shape[1:]) for at in range(layer_total)])
        return update(weight, moment_old, average, grad, scale)

    e_w, e_m, e_a = update(w_emb, m_emb, a_emb, grad_emb, scale)
    v_w, v_m, v_a = update(vectors, m_vec, a_vec, grad_vec, scale)
    q_w, q_m, q_a = big_update(w_qkv, m_qkv, a_qkv, 0)
    o_w, o_m, o_a = big_update(w_out, m_out, a_out, 1)
    u_w, u_m, u_a = big_update(w_up, m_up, a_up, 2)
    d_w, d_m, d_a = big_update(w_down, m_down, a_down, 3)
    h_w, h_m, h_a = update(w_head, m_head, a_head, grad_head, scale)
    return (
        loss, grad_norm, e_w, e_m, e_a, v_w, v_m, v_a, q_w, q_m, q_a, o_w, o_m, o_a,
        u_w, u_m, u_a, d_w, d_m, d_a, h_w, h_m, h_a,
    )


def solution(mesh):
    tables = [P(("dp", "head"), None, None)] + [P(("dp", "head"), None)] + [P()] + [P(("dp", "head"), None)] * 3
    joined = P(None, "dp", None, "head", None)
    mixed = P(None, "head", "dp", None)
    wide = P(None, ("dp", "head"), None)
    state = [P()] * 6 + [joined] * 3 + [mixed] * 3 + [wide] * 6 + [P()] * 3
    return jax.shard_map(
        shards, mesh=mesh, in_specs=tuple(tables + state), out_specs=tuple([P(), P()] + state), check_vma=False)
```

```python
import functools
import jax
import jax.numpy as jnp
from jax import lax
from jax.sharding import PartitionSpec as P
from jax.experimental import pallas as pl
from jax.experimental.pallas import tpu as pltpu

MESH = pl.DeviceIdType.MESH


class Place:
    def __init__(self):
        self.chip = lax.axis_index("dp")
        self.core = lax.axis_index("head")
        self.x = self.chip % 2
        self.y = (self.chip // 2) % 2
        self.z = self.chip // 4
        z = self.z
        self.z_from = (z, 1 + z % 2, (12 - 2 * z) % 5, 3 - 3 * (z // 2))

    def peer(self, way):
        step = {
            "x": 1 - 2 * self.x,
            "y": 2 - 4 * self.y,
            "u": 4,
            "d": -4,
            "c": 0,
        }[way]
        core = 1 - self.core if way == "c" else self.core
        return (self.chip + step, core)

    def group(self, k):
        return (
            1 - self.y if k & 4 else self.y, 1 - self.x if k & 2 else self.x, 1 - self.core if k & 1 else self.core)

    def block(self, k, ax, ay):
        sx = self.x if ax == 0 else 1 - self.x
        sy = self.y if ay == 0 else 1 - self.y
        return self.z_from[k] * 4 + sy * 2 + sx


def meet(place, wide=False):
    barrier = pltpu.get_barrier_semaphore()
    to = [place.peer(way) for way in "xyc"]
    if wide:
        to = []
        for k in range(1, 8):
            y, x, core = place.group(k)
            to.append((place.z * 4 + y * 2 + x, core))
    to += [(place.chip + 4 * ((place.z + d) % 4 - place.z), place.core) for d in (1, 2, 3)]
    for device in to:
        pl.semaphore_signal(barrier, inc=1, device_id=device, device_id_type=MESH)
    pl.semaphore_wait(barrier, len(to))


def at_block(ref, chip, core, piece, by_core):
    return ref.at[core, chip, piece] if by_core else ref.at[chip, core, piece]


class Gather:
    def __init__(self, by_core, orders, shapes, dtype):
        self.by_core, self.orders, self.shapes, self.dtype = by_core, orders, shapes, dtype
        self.n, self.pieces = len(by_core), max(map(len, orders))

    def in_specs(self):
        return [pl.BlockSpec(memory_space=pl.ANY)] * self.n

    def out_specs(self):
        return [pl.BlockSpec(memory_space=pl.ANY)] * self.n

    def out_shape(self):
        return [
            jax.ShapeDtypeStruct(((2, 16) if bc else (16, 2)) + s, self.dtype)
            for s, bc in zip(self.shapes, self.by_core)]

    def scratch(self):
        n, pieces = self.n, self.pieces
        return [
            pltpu.SemaphoreType.DMA((n, pieces)),
            pltpu.SemaphoreType.DMA((n, pieces, 16)),
            pltpu.SemaphoreType.DMA((n,)),
            pltpu.SemaphoreType.DMA((n, pieces, 4)),
            pltpu.SemaphoreType.DMA((n,)),
        ]

    def steps(self, ins, outs, scratch, meeting=True):
        n, orders = self.n, self.orders
        local_sem, recv, core_recv, send, core_send = scratch
        place = Place()
        me = place.chip
        ways = {"x": 0, "y": 1, "u": 2, "d": 3}

        def slot(a, c, chip):
            return at_block(outs[a], chip, place.core, c, self.by_core[a])

        def copy(a, c, chip, way, src, sems):
            return pltpu.make_async_remote_copy(
                src_ref=src, dst_ref=slot(a, c, chip), send_sem=sems[0], recv_sem=sems[1],
                device_id=place.peer(way), device_id_type=MESH)

        def forward(a, c, order, k, ax, ay):
            chip = place.block(k, ax, ay)
            rel = {"x": ax, "y": ay, "z": k}
            last = max([i for i in range(3) if rel[order[i]] != 0], default=-1)
            src = ins[a].at[c] if last < 0 else slot(a, c, chip)
            for i in range(max(last, 0), 3):
                dim = order[i]
                if dim == "z":
                    sz = place.z_from[k]

                    @pl.when((sz <= place.z) & (place.z < 3))
                    def _():
                        copy(a, c, chip, "u", src, (send.at[a, c, 2], recv.at[a, c, chip])).start()

                    @pl.when((sz >= place.z) & (place.z > 0))
                    def _():
                        copy(a, c, chip, "d", src, (send.at[a, c, 3], recv.at[a, c, chip])).start()
                elif rel[dim] == 0:
                    copy(a, c, chip, dim, src, (send.at[a, c, ways[dim]], recv.at[a, c, chip])).start()
            copy(a, c, chip, "c", src, (core_send.at[a], core_recv.at[a])).start()

        def own(a, c):
            return pltpu.make_async_copy(ins[a].at[c], slot(a, c, me), local_sem.at[a, c])

        def entry(k, ax, ay):
            if (k, ax, ay) == (0, 0, 0):
                if meeting:
                    meet(place)
            for a in range(n):
                for c, order in enumerate(orders[a]):
                    chip = place.block(k, ax, ay)
                    if (k, ax, ay) != (0, 0, 0):
                        copy(a, c, chip, "x", slot(a, c, chip), (send.at[a, c, 0], recv.at[a, c, chip])).wait_recv()
                    forward(a, c, order, k, ax, ay)
                    if (k, ax, ay) == (0, 0, 0):
                        own(a, c).start()

        def finish():
            for a in range(n):
                for c in range(len(orders[a])):
                    own(a, c).wait()
            for a in range(n):
                whole = outs[a].at[0] if self.by_core[a] else outs[a].at[:, 0]
                pltpu.make_async_remote_copy(
                    src_ref=whole, dst_ref=whole, send_sem=core_send.at[a], recv_sem=core_recv.at[a],
                    device_id=place.peer("c"), device_id_type=MESH).wait()
                for c, order in enumerate(orders[a]):
                    def drain(way, count):
                        lead = outs[a].at[0] if self.by_core[a] else outs[a].at[:, 0]
                        part = lead.at[pl.ds(0, count), c]
                        pltpu.make_async_remote_copy(
                            src_ref=part, dst_ref=part, send_sem=send.at[a, c, ways[way]],
                            recv_sem=recv.at[a, c, 0],
                            device_id=place.peer("c"), device_id_type=MESH).wait_send()
                    before = 1
                    for dim in order:
                        if dim == "z":
                            for zz in range(4):
                                @pl.when(place.z == zz)
                                def _(zz=zz, before=before):
                                    if zz < 3:
                                        drain("u", before * (zz + 1))
                                    if zz > 0:
                                        drain("d", before * (4 - zz))
                            before *= 4
                        else:
                            drain(dim, before)
                            before *= 2

        entries = sorted(
            [(k, ax, ay) for k in range(4) for ax in range(2) for ay in range(2)], key=lambda e: e[0] + e[1] + e[2])
        return [functools.partial(entry, *e) for e in entries] + [finish]


QUARTERS = ((True, True), (True, False), (False, True), (False, False))


def as_grid(array, kind):
    lead = {True: (2, 4, 2, 2), False: (4, 2, 2, 2), "group": (2, 2, 2, 4)}[kind]
    return array.reshape(lead + array.shape[2:])


def quarter_of(ref, kind, core, y, x, c):
    if kind == "group":
        return ref.at[y, x, core, :, c]
    return ref.at[core, :, y, x, c] if kind else ref.at[:, y, x, core, c]


class Reduce:
    def __init__(self, kinds, orders, shapes, waves):
        self.kinds, self.orders, self.shapes, self.waves = kinds, orders, shapes, waves
        self.n, self.pieces = len(kinds), max(map(len, orders))

    def in_specs(self):
        return [pl.BlockSpec(memory_space=pl.ANY)] * self.n

    def out_specs(self):
        return [pl.BlockSpec(memory_space=pltpu.VMEM)] * (self.n + 1)

    def out_shape(self):
        return [jax.ShapeDtypeStruct(s, jnp.float32) for s in self.shapes + [(1, 128)]]

    def scratch(self):
        n, pieces = self.n, self.pieces
        buffers = []
        for lead in ((2, 2, 4), (2, 2, 4), (2, 4), (4,), (4,)):
            buffers += [pltpu.VMEM(lead + s, jnp.bfloat16) for s in self.shapes]
        return buffers + [
            pltpu.SemaphoreType.DMA((n, pieces, 4)),
            pltpu.SemaphoreType.DMA((2, n, pieces, 4)),
            pltpu.SemaphoreType.DMA((2, n, pieces, 2)),
            pltpu.SemaphoreType.DMA((2, n, pieces)),
            pltpu.SemaphoreType.DMA((2, n, pieces, 4)),
        ]

    def steps(self, ins, outs, scratch, meeting=True):
        n, kinds = self.n, self.kinds
        mine, other, first, second, line = [scratch[i * n : (i + 1) * n] for i in range(5)]
        load_sem, core_sem, first_sem, second_sem, line_sem = scratch[5 * n :]
        squares = outs[n]
        place = Place()
        items = [(a, c, order) for a in range(n) for c, order in enumerate(self.orders[a])]

        def at(order, far_first, far_second):
            far = {order[2]: far_first, order[1]: far_second}
            return (1 - place.y if far["y"] else place.y, 1 - place.x if far["x"] else place.x)

        def send(src, dst, sems, index, to, index_there=None):
            return pltpu.make_async_remote_copy(
                src_ref=src, dst_ref=dst, send_sem=sems.at[(0,) + index],
                recv_sem=sems.at[(1,) + (index if index_there is None else index_there)],
                device_id=to, device_id_type=MESH)

        def load(a, c, y, x):
            return pltpu.make_async_copy(
                quarter_of(ins[a], kinds[a], place.core, y, x, c), mine[a].at[y, x, :, c], load_sem.at[a, c, y * 2 + x])

        def to_core(a, c, y, x):
            return send(
                quarter_of(ins[a], kinds[a], 1 - place.core, y, x, c), other[a].at[y, x, :, c],
                core_sem, (a, c, y * 2 + x), place.peer("c"))

        def to_first(a, c, order, far):
            y, x = at(order, True, far)
            return send(
                mine[a].at[y, x, :, c], first[a].at[int(far), :, c], first_sem, (a, c, int(far)), place.peer(order[2]))

        def to_second(a, c, order):
            y, x = at(order, False, True)
            return send(mine[a].at[y, x, :, c], second[a].at[:, c], second_sem, (a, c), place.peer(order[1]))

        def to_owner(a, c, d):
            z = (place.z + d) % 4
            return send(
                mine[a].at[place.y, place.x, z, c], line[a].at[place.z, c], line_sem, (a, c, d),
                (place.chip + 4 * (z - place.z), place.core), (a, c, place.z))

        def from_line(a, c, d):
            z = (place.z + d) % 4
            return send(
                mine[a].at[place.y, place.x, z, c], line[a].at[z, c], line_sem, (a, c, d),
                (place.chip + 4 * (z - place.z), place.core), (a, c, z))

        def add(a, c, y, x, more):
            def one(z, carry):
                mine[a][y, x, z, c] = mine[a][y, x, z, c] + more(z)
                return carry
            lax.fori_loop(0, 4, one, 0)

        def begin():
            if meeting:
                meet(place)
            squares[...] = jnp.zeros_like(squares)
            for wave in self.waves:
                for quarter in QUARTERS:
                    for a, c, order in (items[i] for i in wave):
                        y, x = at(order, *quarter)
                        to_core(a, c, y, x).start()
                        load(a, c, y, x).start()

        def fold(item, quarter):
            a, c, order = item
            y, x = at(order, *quarter)
            load(a, c, y, x).wait()
            to_core(a, c, y, x).wait_recv()
            add(a, c, y, x, lambda z: other[a][y, x, z, c])
            if quarter[0]:
                to_first(a, c, order, quarter[1]).start()

        def take_first(item, far):
            a, c, order = item
            y, x = at(order, False, far)
            to_first(a, c, order, far).wait_recv()
            add(a, c, y, x, lambda z: first[a][int(far), z, c])
            if far:
                to_second(a, c, order).start()

        def take_second(item):
            a, c, order = item
            to_second(a, c, order).wait_recv()
            add(a, c, place.y, place.x, lambda z: second[a][z, c])
            for d in (1, 2, 3):
                to_owner(a, c, d).start()

        def last(item):
            a, c, order = item
            total = mine[a][place.y, place.x, place.z, c].astype(jnp.float32)
            for d in (1, 2, 3):
                from_line(a, c, d).wait_recv()
                total += line[a][(place.z + d) % 4, c].astype(jnp.float32)
            outs[a][c] = total
            by_lane = jnp.sum(total * total, 0, keepdims=True)
            for k in range(by_lane.shape[1] // 128):
                squares[...] += by_lane[:, k * 128 : (k + 1) * 128]

        def finish():
            for a, c, order in items:
                for quarter in QUARTERS:
                    to_core(a, c, *at(order, *quarter)).wait_send()
                to_first(a, c, order, True).wait_send()
                to_first(a, c, order, False).wait_send()
                to_second(a, c, order).wait_send()
                for d in (1, 2, 3):
                    to_owner(a, c, d).wait_send()

        def stage(turn, chosen):
            part = functools.partial
            if turn < 4:
                return [part(fold, items[i], QUARTERS[turn]) for i in chosen]
            if turn < 6:
                return [part(take_first, items[i], turn == 4) for i in chosen]
            return [part((take_second, last)[turn - 6], items[i]) for i in chosen]

        out = [begin]
        for w, chosen in enumerate(self.waves):
            out += stage(0, chosen) + stage(1, chosen)
            if w > 0:
                out += stage(5, self.waves[w - 1]) + stage(6, self.waves[w - 1])
            out += stage(2, chosen) + stage(3, chosen) + stage(4, chosen)
        out += stage(5, self.waves[-1]) + stage(6, self.waves[-1])
        for chosen in self.waves:
            out += stage(7, chosen)
        return out + [finish]


class Spread:
    wide = True

    def __init__(self, shapes, dtypes):
        self.shapes, self.dtypes, self.n = shapes, dtypes, len(shapes)

    def in_specs(self):
        return [pl.BlockSpec(memory_space=pl.ANY)] * self.n

    def out_specs(self):
        return [pl.BlockSpec(memory_space=pl.ANY)] * self.n

    def out_shape(self):
        return [jax.ShapeDtypeStruct((2, 2, 2, 4) + s, d) for s, d in zip(self.shapes, self.dtypes)]

    def scratch(self):
        n = self.n
        return [
            pltpu.SemaphoreType.DMA((n,)),
            pltpu.SemaphoreType.DMA((2, n, 4)),
            pltpu.SemaphoreType.DMA((2, n, 8)),
        ]

    def steps(self, ins, outs, scratch, meeting=True):
        local_sem, line_sem, group_sem = scratch
        place = Place()

        def own(a):
            return pltpu.make_async_copy(
                ins[a], outs[a].at[place.y, place.x, place.core, place.z], local_sem.at[a])

        def along(a, d, back):
            z = (place.z + d) % 4
            at = z if back else place.z
            return pltpu.make_async_remote_copy(
                src_ref=ins[a], dst_ref=outs[a].at[place.y, place.x, place.core, at],
                send_sem=line_sem.at[0, a, d], recv_sem=line_sem.at[1, a, at],
                device_id=(place.chip + 4 * (z - place.z), place.core), device_id_type=MESH)

        def across(a, k, back):
            to = place.group(k)
            y, x, core = to if back else (place.y, place.x, place.core)
            part = outs[a].at[y, x, core]
            return pltpu.make_async_remote_copy(
                src_ref=part, dst_ref=part, send_sem=group_sem.at[0, a, k], recv_sem=group_sem.at[1, a, k],
                device_id=(place.z * 4 + to[0] * 2 + to[1], to[2]), device_id_type=MESH)

        def begin():
            if meeting:
                meet(place, True)
            for a in range(self.n):
                for d in (1, 2, 3):
                    along(a, d, False).start()
                own(a).start()

        def middle():
            for a in range(self.n):
                own(a).wait()
                for d in (1, 2, 3):
                    along(a, d, True).wait_recv()
                for k in range(1, 8):
                    across(a, k, False).start()

        def end():
            for a in range(self.n):
                for k in range(1, 8):
                    across(a, k, True).wait_recv()
            for a in range(self.n):
                for d in (1, 2, 3):
                    along(a, d, False).wait_send()
                for k in range(1, 8):
                    across(a, k, False).wait_send()

        return [begin, middle, end]


class Both:
    wide = True

    def __init__(self, one, two):
        self.parts, self.n = (one, two), one.n + two.n

    def both(self, name):
        return getattr(self.parts[0], name)() + getattr(self.parts[1], name)()

    def in_specs(self):
        return self.both("in_specs")

    def out_specs(self):
        return self.both("out_specs")

    def out_shape(self):
        return self.both("out_shape")

    def scratch(self):
        return self.both("scratch")

    def steps(self, ins, outs, scratch, meeting=True):
        one, two = self.parts
        n_out, n_scratch = len(one.out_shape()), len(one.scratch())
        lists = (
            one.steps(ins[: one.n], outs[:n_out], scratch[:n_scratch], False),
            two.steps(ins[one.n :], outs[n_out:], scratch[n_scratch:], False))
        timed = [(i / (len(steps) - 1), step) for steps in lists for i, step in enumerate(steps)]
        return [lambda: meet(Place(), True)] + [step for _, step in sorted(timed, key=lambda t: t[0])]


VMEM_ALL = 64 * 1024 * 1024 - 65536


class Aside:
    def __init__(self, plan, arrays, collective_id, pace):
        self.plan, self.arrays, self.collective_id, self.pace = plan, arrays, collective_id, pace


def with_aside(
    body, aside, *, ticks, grid, in_specs, out_specs, out_shape, scratch_shapes=(), cost, operands):
    if aside is None:
        out = pl.pallas_call(
            functools.partial(body, tick=lambda i: None), grid=grid, in_specs=in_specs, out_specs=out_specs,
            out_shape=tuple(out_shape), scratch_shapes=scratch_shapes, cost_estimate=cost,
            compiler_params=pltpu.CompilerParams(vmem_limit_bytes=VMEM_ALL))(*operands)
        return out, None
    plan = aside.plan
    n_in, n_out, n_scr, n, n_plan = len(in_specs), len(out_specs), len(scratch_shapes), plan.n, len(plan.out_shape())
    cells = 1
    for extent in grid:
        cells *= extent

    def kernel(*refs):
        refs = list(refs)
        ins, refs = refs[:n_in], refs[n_in:]
        plan_ins, refs = refs[:n], refs[n:]
        outs, refs = refs[:n_out], refs[n_out:]
        plan_outs, refs = refs[:n_plan], refs[n_plan:]
        scratch, plan_scratch = refs[:n_scr], refs[n_scr:]
        steps = plan.steps(plan_ins, plan_outs, plan_scratch)
        cell = 0
        for axis, extent in enumerate(grid):
            cell = cell * extent + pl.program_id(axis)
        by_slot = {}
        for i, step in enumerate(steps[:-1]):
            at = (i / (len(steps) - 1)) ** aside.pace
            by_slot.setdefault(int(at * cells * ticks), []).append(step)

        def tick(i):
            for slot in sorted(by_slot):
                if slot % ticks == i:
                    @pl.when(cell == slot // ticks)
                    def _():
                        for step in by_slot[slot]:
                            step()

        body(*ins, *outs, *scratch, tick=tick)

        @pl.when(cell == cells - 1)
        def _():
            steps[-1]()

    out = pl.pallas_call(
        kernel, grid=grid,
        in_specs=list(in_specs) + plan.in_specs(), out_specs=list(out_specs) + plan.out_specs(),
        out_shape=tuple(out_shape) + tuple(plan.out_shape()),
        scratch_shapes=list(scratch_shapes) + plan.scratch(), cost_estimate=cost,
        compiler_params=pltpu.CompilerParams(
            collective_id=aside.collective_id, has_side_effects=True, vmem_limit_bytes=VMEM_ALL),
    )(*operands, *aside.arrays)
    return out[:n_out], out[n_out:]


def exchange(plan, arrays, collective_id):
    n = plan.n
    n_all = n + len(plan.out_shape())

    def kernel(*refs):
        for step in plan.steps(refs[:n], refs[n:n_all], refs[n_all:]):
            step()

    moved = sum(a.size for a in arrays) * 2
    return pl.pallas_call(
        kernel,
        out_shape=tuple(plan.out_shape()),
        in_specs=plan.in_specs(),
        out_specs=plan.out_specs(),
        scratch_shapes=plan.scratch(),
        compiler_params=pltpu.CompilerParams(
            collective_id=collective_id, has_side_effects=True, vmem_limit_bytes=VMEM_ALL),
        cost_estimate=pl.CostEstimate(flops=0, bytes_accessed=32 * moved, transcendentals=0),
    )(*arrays)


def gather_plan(arrays, by_core, orders):
    return Gather(by_core, orders, [a.shape for a in arrays], arrays[0].dtype)


def reduce_plan(arrays, kinds, orders, waves):
    plan = Reduce(kinds, orders, [a.shape[2:] for a in arrays], waves)
    return plan, [as_grid(a, kind) for a, kind in zip(arrays, kinds)]


def spread_plan(arrays):
    return Spread([a.shape for a in arrays], [a.dtype for a in arrays])


def all_gather_layer(arrays, by_core, orders, collective_id):
    return exchange(gather_plan(arrays, by_core, orders), arrays, collective_id)


def reduce_scatter_layer(arrays, kinds, orders, waves, collective_id):
    plan, operands = reduce_plan(arrays, kinds, orders, waves)
    return exchange(plan, operands, collective_id)


HD = 64
CTX = 768

eps_norm = 1e-05
clip_at = 0.01
rate = 3000.0
moment = 0.9
keep_avg = 0.9
decay_wd = 1e-05
low_type = jnp.bfloat16
wide_type = jnp.float32


def layer_norm(values, gain_row, shift_row):
    center = values - jnp.mean(values, -1, keepdims=True)
    spread = jnp.mean(center * center, -1, keepdims=True)
    return center * lax.rsqrt(spread + eps_norm) * gain_row + shift_row


def norm_back(values, gain_row, shift_row, upstream):
    _, pull = jax.vjp(layer_norm, values, gain_row, shift_row)
    return pull(upstream)


def gelu_back(values, upstream):
    _, pull = jax.vjp(jax.nn.gelu, values)
    return pull(upstream)[0]


def matmul(first_op, second_op):
    return jnp.dot(first_op, second_op, preferred_element_type=wide_type)


def contract(first_op, second_op, first_dim, second_dim):
    return lax.dot_general(
        first_op, second_op, (((first_dim,), (second_dim,)), ((), ())), preferred_element_type=wide_type
    )


def matmul_tn(first_op, second_op):
    return contract(first_op, second_op, 0, 0)


def matmul_nt(first_op, second_op):
    return contract(first_op, second_op, 1, 1)


def head_lanes(shape, head):
    lane = lax.broadcasted_iota(jnp.int32, shape, 1)
    mine = (lane < HD) if head == 0 else (lane >= HD)
    return mine, lane == (HD if head == 0 else 0)


def attend_kernel(q_ref, k_ref, v_ref, bias_ref, out_ref, lse_ref, *, tick):
    q_block = q_ref[0] * jnp.asarray(HD ** -0.5, low_type)
    k_block, v_block, bias = k_ref[0], v_ref[0], bias_ref[...]
    v_turned = v_block.T
    parts = []
    for head in range(2):
        tick(head)
        q_mine, q_one = head_lanes(q_block.shape, head)
        k_mine, _ = head_lanes(k_block.shape, head)
        one = jnp.where(q_one, jnp.ones_like(q_block), jnp.zeros_like(q_block))
        score = matmul_nt(jnp.where(k_mine, k_block, bias), jnp.where(q_mine, q_block, one))
        peak = jnp.max(score, 0, keepdims=True)
        lifted = jnp.exp(score - peak)
        total = jnp.sum(lifted, 0, keepdims=True)
        mixed = matmul(v_turned[head * HD : (head + 1) * HD], lifted.astype(low_type))
        parts.append(mixed / total)
        lse_ref[0, head : head + 1, :] = peak + jnp.log(total)
    out_ref[...] = jnp.concatenate(parts, 0).T.astype(low_type)


def attend(queries, keys_values, bias, aside):
    groups, rows, width = queries.shape
    pairs = width // 128
    block = min(256, rows)
    grid = (groups * pairs, rows // block)
    (mixed, lse), extra = with_aside(
        attend_kernel,
        aside,
        ticks=2,
        grid=grid,
        in_specs=[
            pl.BlockSpec((1, block, 128), lambda p, i: (p // pairs, i, p % pairs)),
            pl.BlockSpec((1, CTX, 128), lambda p, i: (p // pairs, 0, p % pairs)),
            pl.BlockSpec((1, CTX, 128), lambda p, i: (p // pairs, 0, pairs + p % pairs)),
            pl.BlockSpec((CTX, 128), lambda p, i: (0, 0)),
        ],
        out_specs=[
            pl.BlockSpec((block, 128), lambda p, i: (i, p)),
            pl.BlockSpec((1, 2, block), lambda p, i: (p, 0, i)),
        ],
        out_shape=(
            jax.ShapeDtypeStruct((rows, groups * width), low_type),
            jax.ShapeDtypeStruct((groups * pairs, 2, rows), wide_type),
        ),
        cost=pl.CostEstimate(
            flops=4 * rows * CTX * groups * width, bytes_accessed=8 * rows * groups * width,
            transcendentals=rows * CTX * groups * width // HD),
        operands=(queries, keys_values, keys_values, bias),
    )
    return mixed, lse, extra


def attend_back_kernel(q_ref, k_ref, v_ref, bias_ref, g_ref, o_ref, lse_ref, gq_ref, gk_ref, gv_ref, k_sum, v_sum, *, tick):
    step = pl.program_id(1)

    @pl.when(step == 0)
    def _():
        k_sum[...] = jnp.zeros_like(k_sum)
        v_sum[...] = jnp.zeros_like(v_sum)

    scale = HD ** -0.5
    q_block = q_ref[0] * jnp.asarray(scale, low_type)
    k_block, v_block, bias = k_ref[0], v_ref[0], bias_ref[...]
    g_block = g_ref[...]
    k_turned = k_block.T
    both = (g_block.astype(wide_type) * o_ref[...].astype(wide_type)).T
    parts = []
    for head in range(2):
        tick(head)
        q_mine, q_one = head_lanes(q_block.shape, head)
        k_mine, _ = head_lanes(k_block.shape, head)
        nothing = jnp.zeros_like(q_block)
        one = jnp.where(q_one, jnp.ones_like(q_block), nothing)
        score = matmul_nt(jnp.where(k_mine, k_block, bias), jnp.where(q_mine, q_block, one))
        prob = jnp.exp(score - lse_ref[0, head : head + 1, :])
        g_mine = jnp.where(q_mine, g_block, nothing)
        grad_prob = matmul_nt(v_block, g_mine)
        inner = jnp.sum(both[head * HD : (head + 1) * HD], 0, keepdims=True)
        grad_score = (prob * (grad_prob - inner)).astype(low_type)
        v_sum[...] += matmul(prob.astype(low_type), g_mine)
        k_sum[...] += matmul(grad_score, jnp.where(q_mine, q_block, nothing))
        parts.append(matmul(k_turned[head * HD : (head + 1) * HD], grad_score) * scale)
    gq_ref[0] = jnp.concatenate(parts, 0).T.astype(low_type)

    @pl.when(step == pl.num_programs(1) - 1)
    def _():
        gk_ref[0] = k_sum[...].astype(low_type)
        gv_ref[0] = v_sum[...].astype(low_type)


def attend_back(queries, keys_values, bias, grad_mixed, mixed, lse, aside):
    groups, rows, width = queries.shape
    pairs = width // 128
    block = min(256, rows)
    grid = (groups * pairs, rows // block)
    row_spec = pl.BlockSpec((block, 128), lambda p, i: (i, p))
    key_out = pl.BlockSpec((1, CTX, 128), lambda p, i: (p // pairs, 0, p % pairs))
    grads, extra = with_aside(
        attend_back_kernel,
        aside,
        ticks=2,
        grid=grid,
        in_specs=[
            pl.BlockSpec((1, block, 128), lambda p, i: (p // pairs, i, p % pairs)),
            pl.BlockSpec((1, CTX, 128), lambda p, i: (p // pairs, 0, p % pairs)),
            pl.BlockSpec((1, CTX, 128), lambda p, i: (p // pairs, 0, pairs + p % pairs)),
            pl.BlockSpec((CTX, 128), lambda p, i: (0, 0)),
            row_spec,
            row_spec,
            pl.BlockSpec((1, 2, block), lambda p, i: (p, 0, i)),
        ],
        out_specs=[
            pl.BlockSpec((1, block, 128), lambda p, i: (p // pairs, i, p % pairs)),
            key_out,
            key_out,
        ],
        out_shape=(
            jax.ShapeDtypeStruct(queries.shape, low_type),
            jax.ShapeDtypeStruct((groups, CTX, width), low_type),
            jax.ShapeDtypeStruct((groups, CTX, width), low_type),
        ),
        scratch_shapes=[pltpu.VMEM((CTX, 128), wide_type)] * 2,
        cost=pl.CostEstimate(
            flops=10 * rows * CTX * groups * width, bytes_accessed=16 * rows * groups * width,
            transcendentals=rows * CTX * groups * width // HD),
        operands=(queries, keys_values, keys_values, bias, grad_mixed, mixed, lse),
    )
    return tuple(grads) + (extra,)


def grouped(rows, weight):
    return jnp.einsum("rd,gdc->grc", rows, weight, preferred_element_type=wide_type)


GELU_K = 0.7978845608028654
GELU_C = 0.044715


def center_scale(values):
    center = values - jnp.mean(values, -1, keepdims=True)
    return center, lax.rsqrt(jnp.mean(center * center, -1, keepdims=True) + eps_norm)


def mlp_kernel(res_ref, mixed_ref, mix_ref, up_ref, down_ref, vec_ref, out_ref, middle_ref, hidden_ref, normed, total, *, tick):
    step, last = pl.program_id(1), pl.num_programs(1) - 1
    size = hidden_ref.shape[1]
    tick(0)

    @pl.when(step == 0)
    def _():
        middle = res_ref[...] + matmul(mixed_ref[...], mix_ref[...]) + vec_ref[4:5]
        middle_ref[...] = middle
        center, spread = center_scale(middle)
        normed[...] = (center * spread * vec_ref[2:3] + vec_ref[3:4]).astype(low_type)
        total[...] = middle + vec_ref[5:6]

    part = pl.ds(pl.multiple_of(step * size, size), size)
    hidden = matmul(normed[...], up_ref[:, part])
    hidden_ref[...] = hidden.astype(low_type)
    inner = jnp.tanh(GELU_K * (hidden + GELU_C * hidden * hidden * hidden))
    active = (0.5 * hidden * (1.0 + inner)).astype(low_type)
    tick(1)
    total[...] += matmul(active, down_ref[part, :])

    @pl.when(step == last)
    def _():
        out_ref[...] = total[...]


def mlp_forward(residual, first, mixed, weights, vec_rows, aside):
    _, w_mix, w_grow, w_shrink = weights
    rows, width = mixed.shape
    wide = w_grow.shape[1]
    block, chunk = 256, 512
    skip = first // block

    def whole(a):
        return pl.BlockSpec(a.shape, lambda i, j: (0, 0), pipeline_mode=pl.Buffered(1))

    row_spec = pl.BlockSpec((block, width), lambda i, j: (i, 0))
    outs, extra = with_aside(
        mlp_kernel,
        aside,
        ticks=2,
        grid=(rows // block, wide // chunk),
        in_specs=[
            pl.BlockSpec((block, width), lambda i, j: (i + skip, 0)), row_spec,
            whole(w_mix), whole(w_grow), whole(w_shrink), whole(vec_rows),
        ],
        out_specs=[row_spec, row_spec, pl.BlockSpec((block, chunk), lambda i, j: (i, j))],
        out_shape=(
            jax.ShapeDtypeStruct((rows, width), wide_type),
            jax.ShapeDtypeStruct((rows, width), wide_type),
            jax.ShapeDtypeStruct((rows, wide), low_type),
        ),
        scratch_shapes=[pltpu.VMEM((block, width), low_type), pltpu.VMEM((block, width), wide_type)],
        cost=pl.CostEstimate(
            flops=2 * rows * width * (2 * wide + width), bytes_accessed=rows * width * 24, transcendentals=rows * wide),
        operands=(residual, mixed, w_mix, w_grow, w_shrink, vec_rows),
    )
    return outs, extra


def mlp_back_kernel(
    u_ref, middle_ref, mixed_ref, mix_ref, up_ref, down_ref, vec_ref, hidden_ref,
    up_grad_ref, down_grad_ref, mix_grad_ref, mixed_grad_ref, mid_grad_ref, vec_grad_ref,
    u_low, normed_turned, normed_grad, *, tick,
):
    step, last = pl.program_id(0), pl.num_programs(0) - 1
    rows, width = u_ref.shape
    block = 256
    tick(0)

    @pl.when(step == 0)
    def _():
        @pl.loop(0, rows // block)
        def _(i):
            part = pl.ds(pl.multiple_of(i * block, block), block)
            center, spread = center_scale(middle_ref[part, :])
            normed = (center * spread * vec_ref[2:3] + vec_ref[3:4]).astype(low_type)
            normed_turned[:, part] = normed.T
            u_low[part, :] = u_ref[part, :].astype(low_type)
            normed_grad[part, :] = jnp.zeros((block, width), wide_type)

    hidden = hidden_ref[...].astype(wide_type)
    square = hidden * hidden
    inner = jnp.tanh(GELU_K * hidden * (1.0 + GELU_C * square))
    half = 0.5 * (1.0 + inner)
    active = (hidden * half).astype(low_type)
    slope = half + 0.5 * hidden * (1.0 - inner * inner) * (GELU_K * (1.0 + 3.0 * GELU_C * square))
    grad = (matmul_nt(u_low[...], down_ref[...]) * slope).astype(low_type)
    down_grad_ref[...] = matmul(active.T, u_low[...]).astype(low_type)
    tick(1)
    up_grad_ref[...] = matmul(normed_turned[...], grad).astype(low_type)
    tick(2)
    normed_grad[...] += matmul_nt(grad, up_ref[...])

    @pl.when(step == last)
    def _():
        vec_grad_ref[...] = jnp.zeros_like(vec_grad_ref)

        @pl.loop(0, rows // block)
        def _(i):
            part = pl.ds(pl.multiple_of(i * block, block), block)
            center, spread = center_scale(middle_ref[part, :])
            shape = center * spread
            grads = normed_grad[part, :]
            scaled = grads * vec_ref[2:3]
            from_norm = spread * (
                scaled - jnp.mean(scaled, -1, keepdims=True) - shape * jnp.mean(scaled * shape, -1, keepdims=True))
            u_part = u_ref[part, :]
            total = from_norm + u_part
            mid_grad_ref[part, :] = total
            vec_grad_ref[0:1] += jnp.sum(grads * shape, 0, keepdims=True)
            vec_grad_ref[1:2] += jnp.sum(grads, 0, keepdims=True)
            vec_grad_ref[2:3] += jnp.sum(total, 0, keepdims=True)
            vec_grad_ref[3:4] += jnp.sum(u_part, 0, keepdims=True)
            low = total.astype(low_type)
            u_low[part, :] = low
            mixed_grad_ref[part, :] = matmul_nt(low, mix_ref[...]).astype(low_type)
            normed_turned[:, part] = mixed_ref[part, :].T
        mix_grad_ref[...] = matmul(normed_turned[...], u_low[...]).astype(low_type)


def mlp_backward(upstream, middle, mixed, weights, vec_rows, hidden, aside):
    _, w_mix, w_grow, w_shrink = weights
    rows, width = upstream.shape
    wide = hidden.shape[1]
    chunk = 256

    def whole(shape):
        return pl.BlockSpec(shape, lambda j: (0, 0), pipeline_mode=pl.Buffered(1))

    square, row_shape = (width, width), (rows, width)
    up_spec = pl.BlockSpec((width, chunk), lambda j: (0, j))
    down_spec = pl.BlockSpec((chunk, width), lambda j: (j, 0))
    return with_aside(
        mlp_back_kernel,
        aside,
        ticks=3,
        grid=(wide // chunk,),
        in_specs=[
            whole(row_shape), whole(row_shape), whole(row_shape), whole(square), up_spec, down_spec,
            whole(vec_rows.shape), pl.BlockSpec((rows, chunk), lambda j: (0, j)),
        ],
        out_specs=[up_spec, down_spec] + [
            pl.BlockSpec(s, lambda j: (0, 0)) for s in (square, row_shape, row_shape, (8, width))],
        out_shape=(
            jax.ShapeDtypeStruct((width, wide), low_type),
            jax.ShapeDtypeStruct((wide, width), low_type),
            jax.ShapeDtypeStruct(square, low_type),
            jax.ShapeDtypeStruct(row_shape, low_type),
            jax.ShapeDtypeStruct(row_shape, wide_type),
            jax.ShapeDtypeStruct((8, width), wide_type),
        ),
        scratch_shapes=[
            pltpu.VMEM(row_shape, low_type), pltpu.VMEM((width, rows), low_type), pltpu.VMEM(row_shape, wide_type)],
        cost=pl.CostEstimate(
            flops=4 * rows * width * (2 * wide + width), bytes_accessed=rows * width * 40, transcendentals=rows * wide),
        operands=(upstream, middle, mixed, w_mix, w_grow, w_shrink, vec_rows, hidden),
    )


def layer_forward(residual, first, vec_rows, weights, bias, asides, as_rest):
    w_joined = weights[0]
    width = w_joined.shape[2] // 3
    normed = layer_norm(residual, vec_rows[0], vec_rows[1]).astype(low_type)
    queries = grouped(normed[first:], w_joined[:, :, :width]).astype(low_type)
    keys_values = grouped(normed[:CTX], w_joined[:, :, width:]).astype(low_type)
    mixed, lse, extra = attend(queries, keys_values, bias, asides[0])
    if len(weights) == 1:
        weights = weights + as_rest(extra)
    (output, middle, hidden), more = mlp_forward(residual, first, mixed, weights, vec_rows, asides[1])
    return output, weights, more, (residual, normed, queries, keys_values, mixed, lse, middle, hidden)


def layer_backward(upstream, kept, first, vec_rows, weights, bias, make_asides):
    w_joined = weights[0]
    width = w_joined.shape[2] // 3
    residual, normed, queries, keys_values, mixed, lse, middle, hidden = kept
    outs, extra = mlp_backward(upstream, middle, mixed, weights, vec_rows, hidden, make_asides(0, None, None))
    grad_grow, grad_shrink, grad_mix, grad_mixed, grad_middle, mlp_vec = outs
    grad_q, grad_k, grad_v, more = attend_back(
        queries, keys_values, bias, grad_mixed, mixed, lse, make_asides(1, (grad_mix, grad_grow, grad_shrink), extra))

    def weight_grad(rows, grads):
        return jnp.einsum("rd,grc->gdc", rows, grads, preferred_element_type=wide_type).astype(low_type)

    def row_grad(grads, part):
        return jnp.einsum(
            "grc,gdc->rd", grads, w_joined[:, :, part * width : (part + 1) * width], preferred_element_type=wide_type)

    grads_joined = (
        weight_grad(normed[first:], grad_q), weight_grad(normed[:CTX], grad_k), weight_grad(normed[:CTX], grad_v))
    from_q = row_grad(grad_q, 0)
    from_kv = row_grad(grad_k, 1) + row_grad(grad_v, 2)
    rows = residual.shape[0]
    below = jnp.zeros((first, from_q.shape[1]), wide_type)
    tail = jnp.zeros((rows - CTX, from_q.shape[1]), wide_type)
    grad_normed = jnp.concatenate([below, from_q], 0) + jnp.concatenate([from_kv, tail], 0)
    grad_input, gain_attn, shift_attn = norm_back(residual, vec_rows[0], vec_rows[1], grad_normed)
    vec_grads = [gain_attn, shift_attn, mlp_vec[0], mlp_vec[1], mlp_vec[2], mlp_vec[3]]
    grad_out = grad_input + jnp.concatenate([below, grad_middle], 0)
    return grad_out, (extra, more), grads_joined + (grad_mix, grad_grow, grad_shrink), vec_grads


def update(weight, moment_old, average, grad_in, scale):
    applied = grad_in * scale + decay_wd * weight
    moment_new = moment * moment_old + applied
    weight_new = weight - rate * (applied + moment * moment_new)
    return (weight_new, moment_new, keep_avg * average + (1.0 - keep_avg) * weight_new)


BY_CORE = (True, True, False, False)
GATHER_ROUTES = (("zxy",), ("zxy",), ("xzy",), ("yzx",))
FORE_PACE, BACK_PACE = (1.0, 1.0), (1.0, 1.0)
BY_GRAD = (True, True, True, True, False, False)
ROUTES = (("zxy",), ("zyx",), ("zxy",), ("zyx",), ("zyx",), ("zxy",))


def whole_gather(shard_list, by_core):
    return [
        lax.all_gather(lax.all_gather(shard, "dp", axis=0), "head", axis=0 if bc else 1)
        for shard, bc in zip(shard_list, by_core)]


def as_blocks(grads, by_core, rows_list, routes):
    chips, cores = lax.axis_size("dp"), lax.axis_size("head")
    return [
        grad.reshape(((cores, chips) if bc else (chips, cores)) + (len(route), rows // len(route), -1))
        for grad, bc, rows, route in zip(grads, by_core, rows_list, routes)]


def whole_scatter(grads, by_core, rows_list):
    outs = []
    for grad, bc in zip(as_blocks(grads, by_core, rows_list, ROUTES), by_core):
        half = lax.psum_scatter(grad.astype(wide_type), "head", scatter_dimension=0 if bc else 1)
        outs.append(lax.psum_scatter(half, "dp", scatter_dimension=0))
    return outs


def shards(
    rows_in, feat_mask, counts, ctx_vals, targets, query_mask,
    w_emb, m_emb, a_emb, vectors, m_vec, a_vec,
    w_qkv, m_qkv, a_qkv, w_out, m_out, a_out, w_up, m_up, a_up, w_down, m_down, a_down,
    w_head, m_head, a_head,
):
    chips, cores = lax.axis_size("dp"), lax.axis_size("head")
    direct = (chips, cores) == (16, 2)
    _, row_count, feat_count = rows_in.shape
    layer_total = w_qkv.shape[0]
    width = w_emb.shape[1]
    joined_rows = w_qkv.shape[1]
    kinds = w_qkv.shape[2] * w_qkv.shape[4]

    def own_weights(at):
        return [
            w_qkv[at].reshape((joined_rows, kinds)).astype(low_type)[None],
            w_out[at, 0].astype(low_type)[None],
            w_up[at].astype(low_type)[None],
            w_down[at].astype(low_type)[None],
        ]

    def as_joined(qkv):
        return (qkv.reshape((cores, width, kinds)),)

    def as_rest(gathered):
        out, up, down = gathered
        return (out.reshape((width, width)), up.reshape((width, -1)), down.reshape((-1, width)))

    own = [own_weights(at) for at in range(layer_total)]
    forward_asides = [[None, None] for _ in own]
    if direct:
        joined = own[0][0].reshape((2, joined_rows // 2, kinds))
        weights = [as_joined(all_gather_layer([joined], (True,), (("zxy", "zyx"),), 1)[0])]
        for at, layer in enumerate(own):
            if at == 0:
                forward_asides[at][0] = Aside(
                    gather_plan(layer[1:], BY_CORE[1:], (("zxy",), ("xzy",), ("yzx",))), layer[1:], 2, FORE_PACE[0])
            else:
                forward_asides[at - 1][1] = Aside(
                    gather_plan(layer, BY_CORE, GATHER_ROUTES), layer, 10 + at, FORE_PACE[1])
    else:
        gathered = [whole_gather(o, BY_CORE) for o in own]
        weights = [as_joined(g[0]) + as_rest(g[1:]) for g in gathered]

    table = lax.axis_index("dp") * cores + lax.axis_index("head")
    count = lax.dynamic_slice_in_dim(counts, table, 1, 0)
    bias = jnp.where(jnp.arange(CTX) < count, 0.0, -1e30).astype(low_type)
    bias = jnp.broadcast_to(bias[:, None], (CTX, 128))
    masked = rows_in[0] * feat_mask[0][None, :].astype(low_type)
    leading = jnp.concatenate([ctx_vals[0], jnp.zeros((row_count - CTX,), wide_type)])[:, None]
    residual = matmul(masked, w_emb.astype(low_type)) + vectors[1] + leading * vectors[0]
    kept_all = []
    for at in range(layer_total):
        first = CTX if at == layer_total - 1 else 0
        residual, weights[at], extra, kept = layer_forward(
            residual, first, vectors[2 + 6 * at : 8 + 6 * at], weights[at], bias, forward_asides[at], as_rest)
        if extra is not None:
            weights.append(as_joined(extra[0]) + as_rest(extra[1:]))
        kept_all.append(kept)

    head_low = w_head.astype(low_type)
    final_rows = layer_norm(residual, vectors[-2], vectors[-1]).astype(low_type)
    logits = matmul(final_rows, head_low)
    row_peak = jnp.max(logits, -1, keepdims=True)
    log_total = row_peak[:, 0] + jnp.log(jnp.sum(jnp.exp(logits - row_peak), -1))
    target_hit = (jnp.arange(logits.shape[1])[None, :] == targets[0][:, None]).astype(wide_type)
    picked = jnp.sum(logits * target_hit, -1)
    row_weight = query_mask[0].astype(wide_type)
    loss_part = jnp.sum((log_total - picked) * row_weight)
    grad_logits = ((jnp.exp(logits - log_total[:, None]) - target_hit) * row_weight[:, None]).astype(low_type)
    grad_head = matmul_tn(final_rows, grad_logits).astype(low_type)
    upstream, gain_final, shift_final = norm_back(
        residual, vectors[-2], vectors[-1], matmul_nt(grad_logits, head_low))

    devices = chips * cores
    rows_list = [joined_rows] * 3 + [w_out.shape[2], w_up.shape[1], w_down.shape[1]]
    sums = [None] * layer_total
    vec_grads = [None] * layer_total
    squares = []
    big = None
    for at in reversed(range(layer_total)):
        first = CTX if at == layer_total - 1 else 0
        above = big

        def make_asides(turn, ready, earlier):
            if not direct or above is None:
                return None
            if turn == 0:
                blocks = as_blocks(
                    list(above) + [grad_head], BY_GRAD + (False,), rows_list + [w_head.shape[0] // devices],
                    ROUTES + (("zyx",),))
                plan, operands = reduce_plan(
                    blocks, BY_GRAD + ("group",), ROUTES + (("zyx",),), ((4, 5), (0, 1, 2, 3, 6)))
                return Aside(plan, operands, 3, BACK_PACE[0])
            blocks = as_blocks(ready, BY_GRAD[3:], rows_list[3:], ROUTES[3:])
            plan, operands = reduce_plan(blocks, BY_GRAD[3:], ROUTES[3:], ((1, 2), (0,)))
            head_sum = [earlier[6][0].astype(low_type)]
            return Aside(Both(plan, spread_plan(head_sum)), operands + head_sum, 7, BACK_PACE[1])

        upstream, extra, big, vec_grads[at] = layer_backward(
            upstream, kept_all[at], first, vectors[2 + 6 * at : 8 + 6 * at], weights[at], bias, make_asides)
        if not direct:
            sums[at] = whole_scatter(big, BY_GRAD, rows_list)
        elif extra[0] is not None:
            sums[at + 1] = list(extra[0][:6])
            sums[at] = list(extra[1][:3])
            squares += [extra[0][7], extra[1][3]]
            head_all = extra[1][4]
    grad_emb = matmul_tn(masked, upstream.astype(low_type))
    vec_list = [jnp.sum(upstream * leading, 0), jnp.sum(upstream, 0)]
    for at in range(layer_total):
        vec_list = vec_list + vec_grads[at]
    grad_vec = jnp.stack(vec_list + [gain_final, shift_final])

    scalars = [loss_part, jnp.sum(row_weight)]
    if direct:
        feats, vec_total = w_emb.shape[0], vectors.shape[0]
        n_small = -(-(feats + vec_total) // (8 * devices)) * 8
        small = jnp.concatenate([grad_emb, grad_vec], 0).astype(low_type)
        small = jnp.pad(small, ((0, n_small * devices - feats - vec_total), (0, 0)))
        kinds_last, routes = BY_GRAD[:3] + ("group",), ROUTES[:3] + (("zyx",),)
        blocks = as_blocks(list(big[:3]) + [small], BY_GRAD[:3] + (False,), rows_list[:3] + [n_small], routes)
        *joined_sums, small_sum, square = reduce_scatter_layer(blocks, kinds_last, routes, ((0, 1, 2, 3),), 4)
        sums[0] = joined_sums + sums[0]
        scalars = jnp.stack([jnp.sum(sum(squares + [square]))] + scalars)
        scalars = jnp.broadcast_to(jnp.pad(scalars, (0, 125))[None], (8, 128))
        last_parts = [small_sum[0].astype(low_type), scalars]
        small_all, totals = exchange(spread_plan(last_parts), last_parts, 5)
        small_all = small_all.reshape((devices * n_small, width)).astype(wide_type)
        totals = jnp.sum(totals[..., 0, :3].reshape((devices, 3)), 0)
        grad_emb, grad_vec = small_all[:feats], small_all[feats : feats + vec_total]
        grad_head = head_all.reshape(w_head.shape).astype(wide_type)
    else:
        names = ("dp", "head")
        square = sum(jnp.sum(p * p) for ps in sums for p in ps)
        totals = lax.psum(jnp.stack([square] + scalars), names)
        grad_head = lax.psum(grad_head.astype(wide_type), names)
        grad_emb, grad_vec = lax.psum(grad_emb, names), lax.psum(grad_vec, names)
        alike = sum(jnp.sum(g * g) for g in (grad_head, grad_emb, grad_vec))
        totals = jnp.stack([totals[0] + alike, totals[1], totals[2]])
    pooled = totals[2]
    loss = totals[1] / pooled
    grad_norm = jnp.sqrt(totals[0]) / pooled
    scale = jnp.minimum(1.0, clip_at / grad_norm) / pooled

    def joined_update(weight, moment_old, average):
        grad = jnp.stack([jnp.stack([p.reshape((joined_rows, -1)) for p in sums[at][:3]], 1) for at in range(layer_total)])
        flat = [a.reshape((-1, 128)) for a in (weight, moment_old, average, grad)]
        return [a.reshape(weight.shape) for a in update(*flat, scale)]

    def big_update(weight, moment_old, average, kind):
        grad = jnp.stack([sums[at][kind].reshape(weight.shape[1:]) for at in range(layer_total)])
        return update(weight, moment_old, average, grad, scale)

    e_w, e_m, e_a = update(w_emb, m_emb, a_emb, grad_emb, scale)
    v_w, v_m, v_a = update(vectors, m_vec, a_vec, grad_vec, scale)
    q_w, q_m, q_a = joined_update(w_qkv, m_qkv, a_qkv)
    o_w, o_m, o_a = big_update(w_out, m_out, a_out, 3)
    u_w, u_m, u_a = big_update(w_up, m_up, a_up, 4)
    d_w, d_m, d_a = big_update(w_down, m_down, a_down, 5)
    h_w, h_m, h_a = update(w_head, m_head, a_head, grad_head, scale)
    return (
        loss, grad_norm, e_w, e_m, e_a, v_w, v_m, v_a, q_w, q_m, q_a, o_w, o_m, o_a,
        u_w, u_m, u_a, d_w, d_m, d_a, h_w, h_m, h_a,
    )


def solution(mesh):
    tables = [P(("dp", "head"), None, None)] + [P(("dp", "head"), None)] + [P()] + [P(("dp", "head"), None)] * 3
    joined = P(None, "dp", None, "head", None)
    mixed = P(None, "head", "dp", None)
    wide = P(None, ("dp", "head"), None)
    state = [P()] * 6 + [joined] * 3 + [mixed] * 3 + [wide] * 6 + [P()] * 3
    return jax.shard_map(
        shards, mesh=mesh, in_specs=tuple(tables + state), out_specs=tuple([P(), P()] + state), check_vma=False)
```

```python
import functools
import jax
import jax.numpy as jnp
from jax import lax
from jax.sharding import PartitionSpec as P
from jax.experimental import pallas as pl
from jax.experimental.pallas import tpu as pltpu

MESH = pl.DeviceIdType.MESH


class Place:
    def __init__(self):
        self.chip = lax.axis_index("dp")
        self.core = lax.axis_index("head")
        self.x = self.chip % 2
        self.y = (self.chip // 2) % 2
        self.z = self.chip // 4
        z = self.z
        self.z_from = (z, 1 + z % 2, (12 - 2 * z) % 5, 3 - 3 * (z // 2))

    def peer(self, way):
        step = {
            "x": 1 - 2 * self.x,
            "y": 2 - 4 * self.y,
            "u": 4,
            "d": -4,
            "c": 0,
        }[way]
        core = 1 - self.core if way == "c" else self.core
        return (self.chip + step, core)

    def group(self, k):
        return (
            1 - self.y if k & 4 else self.y, 1 - self.x if k & 2 else self.x, 1 - self.core if k & 1 else self.core)

    def block(self, k, ax, ay):
        sx = self.x if ax == 0 else 1 - self.x
        sy = self.y if ay == 0 else 1 - self.y
        return self.z_from[k] * 4 + sy * 2 + sx


def meet(place, wide=False):
    barrier = pltpu.get_barrier_semaphore()
    to = [place.peer(way) for way in "xyc"]
    if wide:
        to = []
        for k in range(1, 8):
            y, x, core = place.group(k)
            to.append((place.z * 4 + y * 2 + x, core))
    to += [(place.chip + 4 * ((place.z + d) % 4 - place.z), place.core) for d in (1, 2, 3)]
    for device in to:
        pl.semaphore_signal(barrier, inc=1, device_id=device, device_id_type=MESH)
    pl.semaphore_wait(barrier, len(to))


def at_block(ref, chip, core, piece, by_core):
    return ref.at[core, chip, piece] if by_core else ref.at[chip, core, piece]


class Gather:
    def __init__(self, by_core, orders, shapes, dtype):
        self.by_core, self.orders, self.shapes, self.dtype = by_core, orders, shapes, dtype
        self.n, self.pieces = len(by_core), max(map(len, orders))

    def in_specs(self):
        return [pl.BlockSpec(memory_space=pl.ANY)] * self.n

    def out_specs(self):
        return [pl.BlockSpec(memory_space=pl.ANY)] * self.n

    def out_shape(self):
        return [
            jax.ShapeDtypeStruct(((2, 16) if bc else (16, 2)) + s, self.dtype)
            for s, bc in zip(self.shapes, self.by_core)]

    def scratch(self):
        n, pieces = self.n, self.pieces
        return [
            pltpu.SemaphoreType.DMA((n, pieces)),
            pltpu.SemaphoreType.DMA((n, pieces, 16)),
            pltpu.SemaphoreType.DMA((n,)),
            pltpu.SemaphoreType.DMA((n, pieces, 4)),
            pltpu.SemaphoreType.DMA((n,)),
        ]

    def steps(self, ins, outs, scratch, meeting=True):
        n, orders = self.n, self.orders
        local_sem, recv, core_recv, send, core_send = scratch
        place = Place()
        me = place.chip
        ways = {"x": 0, "y": 1, "u": 2, "d": 3}

        def slot(a, c, chip):
            return at_block(outs[a], chip, place.core, c, self.by_core[a])

        def copy(a, c, chip, way, src, sems):
            return pltpu.make_async_remote_copy(
                src_ref=src, dst_ref=slot(a, c, chip), send_sem=sems[0], recv_sem=sems[1],
                device_id=place.peer(way), device_id_type=MESH)

        def forward(a, c, order, k, ax, ay):
            chip = place.block(k, ax, ay)
            rel = {"x": ax, "y": ay, "z": k}
            last = max([i for i in range(3) if rel[order[i]] != 0], default=-1)
            src = ins[a].at[c] if last < 0 else slot(a, c, chip)
            for i in range(max(last, 0), 3):
                dim = order[i]
                if dim == "z":
                    sz = place.z_from[k]

                    @pl.when((sz <= place.z) & (place.z < 3))
                    def _():
                        copy(a, c, chip, "u", src, (send.at[a, c, 2], recv.at[a, c, chip])).start()

                    @pl.when((sz >= place.z) & (place.z > 0))
                    def _():
                        copy(a, c, chip, "d", src, (send.at[a, c, 3], recv.at[a, c, chip])).start()
                elif rel[dim] == 0:
                    copy(a, c, chip, dim, src, (send.at[a, c, ways[dim]], recv.at[a, c, chip])).start()
            copy(a, c, chip, "c", src, (core_send.at[a], core_recv.at[a])).start()

        def own(a, c):
            return pltpu.make_async_copy(ins[a].at[c], slot(a, c, me), local_sem.at[a, c])

        def entry(k, ax, ay):
            if (k, ax, ay) == (0, 0, 0):
                if meeting:
                    meet(place)
            for a in range(n):
                for c, order in enumerate(orders[a]):
                    chip = place.block(k, ax, ay)
                    if (k, ax, ay) != (0, 0, 0):
                        copy(a, c, chip, "x", slot(a, c, chip), (send.at[a, c, 0], recv.at[a, c, chip])).wait_recv()
                    forward(a, c, order, k, ax, ay)
                    if (k, ax, ay) == (0, 0, 0):
                        own(a, c).start()

        def finish():
            for a in range(n):
                for c in range(len(orders[a])):
                    own(a, c).wait()
            for a in range(n):
                whole = outs[a].at[0] if self.by_core[a] else outs[a].at[:, 0]
                pltpu.make_async_remote_copy(
                    src_ref=whole, dst_ref=whole, send_sem=core_send.at[a], recv_sem=core_recv.at[a],
                    device_id=place.peer("c"), device_id_type=MESH).wait()
                for c, order in enumerate(orders[a]):
                    def drain(way, count):
                        lead = outs[a].at[0] if self.by_core[a] else outs[a].at[:, 0]
                        part = lead.at[pl.ds(0, count), c]
                        pltpu.make_async_remote_copy(
                            src_ref=part, dst_ref=part, send_sem=send.at[a, c, ways[way]],
                            recv_sem=recv.at[a, c, 0],
                            device_id=place.peer("c"), device_id_type=MESH).wait_send()
                    before = 1
                    for dim in order:
                        if dim == "z":
                            for zz in range(4):
                                @pl.when(place.z == zz)
                                def _(zz=zz, before=before):
                                    if zz < 3:
                                        drain("u", before * (zz + 1))
                                    if zz > 0:
                                        drain("d", before * (4 - zz))
                            before *= 4
                        else:
                            drain(dim, before)
                            before *= 2

        entries = sorted(
            [(k, ax, ay) for k in range(4) for ax in range(2) for ay in range(2)], key=lambda e: e[0] + e[1] + e[2])
        return [functools.partial(entry, *e) for e in entries] + [finish]


QUARTERS = ((True, True), (True, False), (False, True), (False, False))


def as_grid(array, kind):
    lead = {True: (2, 4, 2, 2), False: (4, 2, 2, 2), "group": (2, 2, 2, 4)}[kind]
    return array.reshape(lead + array.shape[2:])


def quarter_of(ref, kind, core, y, x, c):
    if kind == "group":
        return ref.at[y, x, core, :, c]
    return ref.at[core, :, y, x, c] if kind else ref.at[:, y, x, core, c]


class Reduce:
    def __init__(self, kinds, orders, shapes, waves):
        self.kinds, self.orders, self.shapes, self.waves = kinds, orders, shapes, waves
        self.n, self.pieces = len(kinds), max(map(len, orders))

    def in_specs(self):
        return [pl.BlockSpec(memory_space=pl.ANY)] * self.n

    def out_specs(self):
        return [pl.BlockSpec(memory_space=pltpu.VMEM)] * (self.n + 1)

    def out_shape(self):
        return [jax.ShapeDtypeStruct(s, jnp.float32) for s in self.shapes + [(1, 128)]]

    def scratch(self):
        n, pieces = self.n, self.pieces
        buffers = []
        for lead in ((2, 2, 4), (2, 2, 4), (2, 4), (4,), (4,)):
            buffers += [pltpu.VMEM(lead + s, jnp.bfloat16) for s in self.shapes]
        return buffers + [
            pltpu.SemaphoreType.DMA((n, pieces, 4)),
            pltpu.SemaphoreType.DMA((2, n, pieces, 4)),
            pltpu.SemaphoreType.DMA((2, n, pieces, 2)),
            pltpu.SemaphoreType.DMA((2, n, pieces)),
            pltpu.SemaphoreType.DMA((2, n, pieces, 4)),
        ]

    def steps(self, ins, outs, scratch, meeting=True):
        n, kinds = self.n, self.kinds
        mine, other, first, second, line = [scratch[i * n : (i + 1) * n] for i in range(5)]
        load_sem, core_sem, first_sem, second_sem, line_sem = scratch[5 * n :]
        squares = outs[n]
        place = Place()
        items = [(a, c, order) for a in range(n) for c, order in enumerate(self.orders[a])]

        def at(order, far_first, far_second):
            far = {order[2]: far_first, order[1]: far_second}
            return (1 - place.y if far["y"] else place.y, 1 - place.x if far["x"] else place.x)

        def send(src, dst, sems, index, to, index_there=None):
            return pltpu.make_async_remote_copy(
                src_ref=src, dst_ref=dst, send_sem=sems.at[(0,) + index],
                recv_sem=sems.at[(1,) + (index if index_there is None else index_there)],
                device_id=to, device_id_type=MESH)

        def load(a, c, y, x):
            return pltpu.make_async_copy(
                quarter_of(ins[a], kinds[a], place.core, y, x, c), mine[a].at[y, x, :, c], load_sem.at[a, c, y * 2 + x])

        def to_core(a, c, y, x):
            return send(
                quarter_of(ins[a], kinds[a], 1 - place.core, y, x, c), other[a].at[y, x, :, c],
                core_sem, (a, c, y * 2 + x), place.peer("c"))

        def to_first(a, c, order, far):
            y, x = at(order, True, far)
            return send(
                mine[a].at[y, x, :, c], first[a].at[int(far), :, c], first_sem, (a, c, int(far)), place.peer(order[2]))

        def to_second(a, c, order):
            y, x = at(order, False, True)
            return send(mine[a].at[y, x, :, c], second[a].at[:, c], second_sem, (a, c), place.peer(order[1]))

        def to_owner(a, c, d):
            z = (place.z + d) % 4
            return send(
                mine[a].at[place.y, place.x, z, c], line[a].at[place.z, c], line_sem, (a, c, d),
                (place.chip + 4 * (z - place.z), place.core), (a, c, place.z))

        def from_line(a, c, d):
            z = (place.z + d) % 4
            return send(
                mine[a].at[place.y, place.x, z, c], line[a].at[z, c], line_sem, (a, c, d),
                (place.chip + 4 * (z - place.z), place.core), (a, c, z))

        def add(a, c, y, x, more):
            def one(z, carry):
                mine[a][y, x, z, c] = mine[a][y, x, z, c] + more(z)
                return carry
            lax.fori_loop(0, 4, one, 0)

        def begin():
            if meeting:
                meet(place)
            squares[...] = jnp.zeros_like(squares)
            for wave in self.waves:
                for quarter in QUARTERS:
                    for a, c, order in (items[i] for i in wave):
                        y, x = at(order, *quarter)
                        to_core(a, c, y, x).start()
                        load(a, c, y, x).start()

        def fold(item, quarter):
            a, c, order = item
            y, x = at(order, *quarter)
            load(a, c, y, x).wait()
            to_core(a, c, y, x).wait_recv()
            add(a, c, y, x, lambda z: other[a][y, x, z, c])
            if quarter[0]:
                to_first(a, c, order, quarter[1]).start()

        def take_first(item, far):
            a, c, order = item
            y, x = at(order, False, far)
            to_first(a, c, order, far).wait_recv()
            add(a, c, y, x, lambda z: first[a][int(far), z, c])
            if far:
                to_second(a, c, order).start()

        def take_second(item):
            a, c, order = item
            to_second(a, c, order).wait_recv()
            add(a, c, place.y, place.x, lambda z: second[a][z, c])
            for d in (1, 2, 3):
                to_owner(a, c, d).start()

        def last(item):
            a, c, order = item
            total = mine[a][place.y, place.x, place.z, c].astype(jnp.float32)
            for d in (1, 2, 3):
                from_line(a, c, d).wait_recv()
                total += line[a][(place.z + d) % 4, c].astype(jnp.float32)
            outs[a][c] = total
            by_lane = jnp.sum(total * total, 0, keepdims=True)
            for k in range(by_lane.shape[1] // 128):
                squares[...] += by_lane[:, k * 128 : (k + 1) * 128]

        def finish():
            for a, c, order in items:
                for quarter in QUARTERS:
                    to_core(a, c, *at(order, *quarter)).wait_send()
                to_first(a, c, order, True).wait_send()
                to_first(a, c, order, False).wait_send()
                to_second(a, c, order).wait_send()
                for d in (1, 2, 3):
                    to_owner(a, c, d).wait_send()

        def stage(turn, chosen):
            part = functools.partial
            if turn < 4:
                return [part(fold, items[i], QUARTERS[turn]) for i in chosen]
            if turn < 6:
                return [part(take_first, items[i], turn == 4) for i in chosen]
            return [part((take_second, last)[turn - 6], items[i]) for i in chosen]

        out = [begin]
        for w, chosen in enumerate(self.waves):
            out += stage(0, chosen) + stage(1, chosen)
            if w > 0:
                out += stage(5, self.waves[w - 1]) + stage(6, self.waves[w - 1])
            out += stage(2, chosen) + stage(3, chosen) + stage(4, chosen)
        out += stage(5, self.waves[-1]) + stage(6, self.waves[-1])
        for chosen in self.waves:
            out += stage(7, chosen)
        return out + [finish]


class Spread:
    wide = True

    def __init__(self, shapes, dtypes):
        self.shapes, self.dtypes, self.n = shapes, dtypes, len(shapes)

    def in_specs(self):
        return [pl.BlockSpec(memory_space=pl.ANY)] * self.n

    def out_specs(self):
        return [pl.BlockSpec(memory_space=pl.ANY)] * self.n

    def out_shape(self):
        return [jax.ShapeDtypeStruct((2, 2, 2, 4) + s, d) for s, d in zip(self.shapes, self.dtypes)]

    def scratch(self):
        n = self.n
        return [
            pltpu.SemaphoreType.DMA((n,)),
            pltpu.SemaphoreType.DMA((2, n, 4)),
            pltpu.SemaphoreType.DMA((2, n, 8)),
        ]

    def steps(self, ins, outs, scratch, meeting=True):
        local_sem, line_sem, group_sem = scratch
        place = Place()

        def own(a):
            return pltpu.make_async_copy(
                ins[a], outs[a].at[place.y, place.x, place.core, place.z], local_sem.at[a])

        def along(a, d, back):
            z = (place.z + d) % 4
            at = z if back else place.z
            return pltpu.make_async_remote_copy(
                src_ref=ins[a], dst_ref=outs[a].at[place.y, place.x, place.core, at],
                send_sem=line_sem.at[0, a, d], recv_sem=line_sem.at[1, a, at],
                device_id=(place.chip + 4 * (z - place.z), place.core), device_id_type=MESH)

        def across(a, k, back):
            to = place.group(k)
            y, x, core = to if back else (place.y, place.x, place.core)
            part = outs[a].at[y, x, core]
            return pltpu.make_async_remote_copy(
                src_ref=part, dst_ref=part, send_sem=group_sem.at[0, a, k], recv_sem=group_sem.at[1, a, k],
                device_id=(place.z * 4 + to[0] * 2 + to[1], to[2]), device_id_type=MESH)

        def begin():
            if meeting:
                meet(place, True)
            for a in range(self.n):
                for d in (1, 2, 3):
                    along(a, d, False).start()
                own(a).start()

        def middle():
            for a in range(self.n):
                own(a).wait()
                for d in (1, 2, 3):
                    along(a, d, True).wait_recv()
                for k in range(1, 8):
                    across(a, k, False).start()

        def end():
            for a in range(self.n):
                for k in range(1, 8):
                    across(a, k, True).wait_recv()
            for a in range(self.n):
                for d in (1, 2, 3):
                    along(a, d, False).wait_send()
                for k in range(1, 8):
                    across(a, k, False).wait_send()

        return [begin, middle, end]


class Both:
    wide = True

    def __init__(self, one, two):
        self.parts, self.n = (one, two), one.n + two.n

    def both(self, name):
        return getattr(self.parts[0], name)() + getattr(self.parts[1], name)()

    def in_specs(self):
        return self.both("in_specs")

    def out_specs(self):
        return self.both("out_specs")

    def out_shape(self):
        return self.both("out_shape")

    def scratch(self):
        return self.both("scratch")

    def steps(self, ins, outs, scratch, meeting=True):
        one, two = self.parts
        n_out, n_scratch = len(one.out_shape()), len(one.scratch())
        lists = (
            one.steps(ins[: one.n], outs[:n_out], scratch[:n_scratch], False),
            two.steps(ins[one.n :], outs[n_out:], scratch[n_scratch:], False))
        timed = [(i / (len(steps) - 1), step) for steps in lists for i, step in enumerate(steps)]
        return [lambda: meet(Place(), True)] + [step for _, step in sorted(timed, key=lambda t: t[0])]


VMEM_ALL = 64 * 1024 * 1024 - 65536


class Aside:
    def __init__(self, plan, arrays, collective_id, pace):
        self.plan, self.arrays, self.collective_id, self.pace = plan, arrays, collective_id, pace


def with_aside(
    body, aside, *, ticks, grid, in_specs, out_specs, out_shape, scratch_shapes=(), cost, operands):
    if aside is None:
        out = pl.pallas_call(
            functools.partial(body, tick=lambda i: None), grid=grid, in_specs=in_specs, out_specs=out_specs,
            out_shape=tuple(out_shape), scratch_shapes=scratch_shapes, cost_estimate=cost,
            compiler_params=pltpu.CompilerParams(vmem_limit_bytes=VMEM_ALL))(*operands)
        return out, None
    plan = aside.plan
    n_in, n_out, n_scr, n, n_plan = len(in_specs), len(out_specs), len(scratch_shapes), plan.n, len(plan.out_shape())
    cells = 1
    for extent in grid:
        cells *= extent

    def kernel(*refs):
        refs = list(refs)
        ins, refs = refs[:n_in], refs[n_in:]
        plan_ins, refs = refs[:n], refs[n:]
        outs, refs = refs[:n_out], refs[n_out:]
        plan_outs, refs = refs[:n_plan], refs[n_plan:]
        scratch, plan_scratch = refs[:n_scr], refs[n_scr:]
        steps = plan.steps(plan_ins, plan_outs, plan_scratch)
        cell = 0
        for axis, extent in enumerate(grid):
            cell = cell * extent + pl.program_id(axis)
        by_slot = {}
        for i, step in enumerate(steps[:-1]):
            at = (i / (len(steps) - 1)) ** aside.pace
            by_slot.setdefault(int(at * cells * ticks), []).append(step)

        def tick(i):
            for slot in sorted(by_slot):
                if slot % ticks == i:
                    @pl.when(cell == slot // ticks)
                    def _():
                        for step in by_slot[slot]:
                            step()

        body(*ins, *outs, *scratch, tick=tick)

        @pl.when(cell == cells - 1)
        def _():
            steps[-1]()

    out = pl.pallas_call(
        kernel, grid=grid,
        in_specs=list(in_specs) + plan.in_specs(), out_specs=list(out_specs) + plan.out_specs(),
        out_shape=tuple(out_shape) + tuple(plan.out_shape()),
        scratch_shapes=list(scratch_shapes) + plan.scratch(), cost_estimate=cost,
        compiler_params=pltpu.CompilerParams(
            collective_id=aside.collective_id, has_side_effects=True, vmem_limit_bytes=VMEM_ALL),
    )(*operands, *aside.arrays)
    return out[:n_out], out[n_out:]


def exchange(plan, arrays, collective_id):
    n = plan.n
    n_all = n + len(plan.out_shape())

    def kernel(*refs):
        for step in plan.steps(refs[:n], refs[n:n_all], refs[n_all:]):
            step()

    moved = sum(a.size for a in arrays) * 2
    return pl.pallas_call(
        kernel,
        out_shape=tuple(plan.out_shape()),
        in_specs=plan.in_specs(),
        out_specs=plan.out_specs(),
        scratch_shapes=plan.scratch(),
        compiler_params=pltpu.CompilerParams(
            collective_id=collective_id, has_side_effects=True, vmem_limit_bytes=VMEM_ALL),
        cost_estimate=pl.CostEstimate(flops=0, bytes_accessed=32 * moved, transcendentals=0),
    )(*arrays)


def gather_plan(arrays, by_core, orders):
    return Gather(by_core, orders, [a.shape for a in arrays], arrays[0].dtype)


def reduce_plan(arrays, kinds, orders, waves):
    plan = Reduce(kinds, orders, [a.shape[2:] for a in arrays], waves)
    return plan, [as_grid(a, kind) for a, kind in zip(arrays, kinds)]


def spread_plan(arrays):
    return Spread([a.shape for a in arrays], [a.dtype for a in arrays])


def all_gather_layer(arrays, by_core, orders, collective_id):
    return exchange(gather_plan(arrays, by_core, orders), arrays, collective_id)


def reduce_scatter_layer(arrays, kinds, orders, waves, collective_id):
    plan, operands = reduce_plan(arrays, kinds, orders, waves)
    return exchange(plan, operands, collective_id)


HD = 64
CTX = 768

eps_norm = 1e-05
clip_at = 0.01
rate = 3000.0
moment = 0.9
keep_avg = 0.9
decay_wd = 1e-05
low_type = jnp.bfloat16
wide_type = jnp.float32


def layer_norm(values, gain_row, shift_row):
    center = values - jnp.mean(values, -1, keepdims=True)
    spread = jnp.mean(center * center, -1, keepdims=True)
    return center * lax.rsqrt(spread + eps_norm) * gain_row + shift_row


def norm_back(values, gain_row, shift_row, upstream):
    _, pull = jax.vjp(layer_norm, values, gain_row, shift_row)
    return pull(upstream)


def gelu_back(values, upstream):
    _, pull = jax.vjp(jax.nn.gelu, values)
    return pull(upstream)[0]


def matmul(first_op, second_op):
    return jnp.dot(first_op, second_op, preferred_element_type=wide_type)


def contract(first_op, second_op, first_dim, second_dim):
    return lax.dot_general(
        first_op, second_op, (((first_dim,), (second_dim,)), ((), ())), preferred_element_type=wide_type
    )


def matmul_tn(first_op, second_op):
    return contract(first_op, second_op, 0, 0)


def matmul_nt(first_op, second_op):
    return contract(first_op, second_op, 1, 1)


def head_lanes(shape, head):
    lane = lax.broadcasted_iota(jnp.int32, shape, 1)
    mine = (lane < HD) if head == 0 else (lane >= HD)
    return mine, lane == (HD if head == 0 else 0)


def attend_kernel(q_ref, k_ref, v_ref, bias_ref, out_ref, lse_ref, *, tick):
    q_block = q_ref[0] * jnp.asarray(HD ** -0.5, low_type)
    k_block, v_block, bias = k_ref[0], v_ref[0], bias_ref[...]
    v_turned = v_block.T
    parts = []
    for head in range(2):
        tick(head)
        q_mine, q_one = head_lanes(q_block.shape, head)
        k_mine, _ = head_lanes(k_block.shape, head)
        one = jnp.where(q_one, jnp.ones_like(q_block), jnp.zeros_like(q_block))
        score = matmul_nt(jnp.where(k_mine, k_block, bias), jnp.where(q_mine, q_block, one))
        peak = jnp.max(score, 0, keepdims=True)
        lifted = jnp.exp(score - peak)
        total = jnp.sum(lifted, 0, keepdims=True)
        mixed = matmul(v_turned[head * HD : (head + 1) * HD], lifted.astype(low_type))
        parts.append(mixed / total)
        lse_ref[0, head : head + 1, :] = peak + jnp.log(total)
    out_ref[...] = jnp.concatenate(parts, 0).T.astype(low_type)


def attend(queries, keys_values, bias, aside):
    groups, rows, width = queries.shape
    pairs = width // 128
    block = min(256, rows)
    grid = (groups * pairs, rows // block)
    (mixed, lse), extra = with_aside(
        attend_kernel,
        aside,
        ticks=2,
        grid=grid,
        in_specs=[
            pl.BlockSpec((1, block, 128), lambda p, i: (p // pairs, i, p % pairs)),
            pl.BlockSpec((1, CTX, 128), lambda p, i: (p // pairs, 0, p % pairs)),
            pl.BlockSpec((1, CTX, 128), lambda p, i: (p // pairs, 0, pairs + p % pairs)),
            pl.BlockSpec((CTX, 128), lambda p, i: (0, 0)),
        ],
        out_specs=[
            pl.BlockSpec((block, 128), lambda p, i: (i, p)),
            pl.BlockSpec((1, 2, block), lambda p, i: (p, 0, i)),
        ],
        out_shape=(
            jax.ShapeDtypeStruct((rows, groups * width), low_type),
            jax.ShapeDtypeStruct((groups * pairs, 2, rows), wide_type),
        ),
        cost=pl.CostEstimate(
            flops=4 * rows * CTX * groups * width, bytes_accessed=8 * rows * groups * width,
            transcendentals=rows * CTX * groups * width // HD),
        operands=(queries, keys_values, keys_values, bias),
    )
    return mixed, lse, extra


def attend_back_kernel(q_ref, k_ref, v_ref, bias_ref, g_ref, o_ref, lse_ref, gq_ref, gk_ref, gv_ref, k_sum, v_sum, *, tick):
    step = pl.program_id(1)

    @pl.when(step == 0)
    def _():
        k_sum[...] = jnp.zeros_like(k_sum)
        v_sum[...] = jnp.zeros_like(v_sum)

    scale = HD ** -0.5
    q_block = q_ref[0] * jnp.asarray(scale, low_type)
    k_block, v_block, bias = k_ref[0], v_ref[0], bias_ref[...]
    g_block = g_ref[...]
    k_turned = k_block.T
    both = (g_block.astype(wide_type) * o_ref[...].astype(wide_type)).T
    parts = []
    for head in range(2):
        tick(head)
        q_mine, q_one = head_lanes(q_block.shape, head)
        k_mine, _ = head_lanes(k_block.shape, head)
        nothing = jnp.zeros_like(q_block)
        one = jnp.where(q_one, jnp.ones_like(q_block), nothing)
        score = matmul_nt(jnp.where(k_mine, k_block, bias), jnp.where(q_mine, q_block, one))
        prob = jnp.exp(score - lse_ref[0, head : head + 1, :])
        g_mine = jnp.where(q_mine, g_block, nothing)
        grad_prob = matmul_nt(v_block, g_mine)
        inner = jnp.sum(both[head * HD : (head + 1) * HD], 0, keepdims=True)
        grad_score = (prob * (grad_prob - inner)).astype(low_type)
        v_sum[...] += matmul(prob.astype(low_type), g_mine)
        k_sum[...] += matmul(grad_score, jnp.where(q_mine, q_block, nothing))
        parts.append(matmul(k_turned[head * HD : (head + 1) * HD], grad_score) * scale)
    gq_ref[0] = jnp.concatenate(parts, 0).T.astype(low_type)

    @pl.when(step == pl.num_programs(1) - 1)
    def _():
        gk_ref[0] = k_sum[...].astype(low_type)
        gv_ref[0] = v_sum[...].astype(low_type)


def attend_back(queries, keys_values, bias, grad_mixed, mixed, lse, aside):
    groups, rows, width = queries.shape
    pairs = width // 128
    block = min(256, rows)
    grid = (groups * pairs, rows // block)
    row_spec = pl.BlockSpec((block, 128), lambda p, i: (i, p))
    key_out = pl.BlockSpec((1, CTX, 128), lambda p, i: (p // pairs, 0, p % pairs))
    grads, extra = with_aside(
        attend_back_kernel,
        aside,
        ticks=2,
        grid=grid,
        in_specs=[
            pl.BlockSpec((1, block, 128), lambda p, i: (p // pairs, i, p % pairs)),
            pl.BlockSpec((1, CTX, 128), lambda p, i: (p // pairs, 0, p % pairs)),
            pl.BlockSpec((1, CTX, 128), lambda p, i: (p // pairs, 0, pairs + p % pairs)),
            pl.BlockSpec((CTX, 128), lambda p, i: (0, 0)),
            row_spec,
            row_spec,
            pl.BlockSpec((1, 2, block), lambda p, i: (p, 0, i)),
        ],
        out_specs=[
            pl.BlockSpec((1, block, 128), lambda p, i: (p // pairs, i, p % pairs)),
            key_out,
            key_out,
        ],
        out_shape=(
            jax.ShapeDtypeStruct(queries.shape, low_type),
            jax.ShapeDtypeStruct((groups, CTX, width), low_type),
            jax.ShapeDtypeStruct((groups, CTX, width), low_type),
        ),
        scratch_shapes=[pltpu.VMEM((CTX, 128), wide_type)] * 2,
        cost=pl.CostEstimate(
            flops=10 * rows * CTX * groups * width, bytes_accessed=16 * rows * groups * width,
            transcendentals=rows * CTX * groups * width // HD),
        operands=(queries, keys_values, keys_values, bias, grad_mixed, mixed, lse),
    )
    return tuple(grads) + (extra,)


def grouped(rows, weight):
    return jnp.einsum("rd,gdc->grc", rows, weight, preferred_element_type=wide_type)


GELU_K = 0.7978845608028654
GELU_C = 0.044715


def center_scale(values):
    center = values - jnp.mean(values, -1, keepdims=True)
    return center, lax.rsqrt(jnp.mean(center * center, -1, keepdims=True) + eps_norm)


def mlp_kernel(res_ref, mixed_ref, mix_ref, up_ref, down_ref, vec_ref, out_ref, middle_ref, hidden_ref, normed, total, *, tick):
    step, last = pl.program_id(1), pl.num_programs(1) - 1
    size = hidden_ref.shape[1]
    tick(0)

    @pl.when(step == 0)
    def _():
        middle = res_ref[...] + matmul(mixed_ref[...], mix_ref[...]) + vec_ref[4:5]
        middle_ref[...] = middle
        center, spread = center_scale(middle)
        normed[...] = (center * spread * vec_ref[2:3] + vec_ref[3:4]).astype(low_type)
        total[...] = middle + vec_ref[5:6]

    part = pl.ds(pl.multiple_of(step * size, size), size)
    hidden = matmul(normed[...], up_ref[:, part])
    hidden_ref[...] = hidden.astype(low_type)
    inner = jnp.tanh(GELU_K * (hidden + GELU_C * hidden * hidden * hidden))
    active = (0.5 * hidden * (1.0 + inner)).astype(low_type)
    tick(1)
    total[...] += matmul(active, down_ref[part, :])

    @pl.when(step == last)
    def _():
        out_ref[...] = total[...]


def mlp_forward(residual, first, mixed, weights, vec_rows, aside):
    _, w_mix, w_grow, w_shrink = weights
    rows, width = mixed.shape
    wide = w_grow.shape[1]
    block, chunk = 256, 512
    skip = first // block

    def whole(a):
        return pl.BlockSpec(a.shape, lambda i, j: (0, 0), pipeline_mode=pl.Buffered(1))

    row_spec = pl.BlockSpec((block, width), lambda i, j: (i, 0))
    outs, extra = with_aside(
        mlp_kernel,
        aside,
        ticks=2,
        grid=(rows // block, wide // chunk),
        in_specs=[
            pl.BlockSpec((block, width), lambda i, j: (i + skip, 0)), row_spec,
            whole(w_mix), whole(w_grow), whole(w_shrink), whole(vec_rows),
        ],
        out_specs=[row_spec, row_spec, pl.BlockSpec((block, chunk), lambda i, j: (i, j))],
        out_shape=(
            jax.ShapeDtypeStruct((rows, width), wide_type),
            jax.ShapeDtypeStruct((rows, width), wide_type),
            jax.ShapeDtypeStruct((rows, wide), low_type),
        ),
        scratch_shapes=[pltpu.VMEM((block, width), low_type), pltpu.VMEM((block, width), wide_type)],
        cost=pl.CostEstimate(
            flops=2 * rows * width * (2 * wide + width), bytes_accessed=rows * width * 24, transcendentals=rows * wide),
        operands=(residual, mixed, w_mix, w_grow, w_shrink, vec_rows),
    )
    return outs, extra


def mlp_back_kernel(
    u_ref, middle_ref, mixed_ref, mix_ref, up_ref, down_ref, vec_ref, hidden_ref,
    up_grad_ref, down_grad_ref, mix_grad_ref, mixed_grad_ref, mid_grad_ref, vec_grad_ref,
    u_low, normed_turned, normed_grad, *, tick,
):
    step, last = pl.program_id(0), pl.num_programs(0) - 1
    rows, width = u_ref.shape
    block = 256
    tick(0)

    @pl.when(step == 0)
    def _():
        @pl.loop(0, rows // block)
        def _(i):
            part = pl.ds(pl.multiple_of(i * block, block), block)
            center, spread = center_scale(middle_ref[part, :])
            normed = (center * spread * vec_ref[2:3] + vec_ref[3:4]).astype(low_type)
            normed_turned[:, part] = normed.T
            u_low[part, :] = u_ref[part, :].astype(low_type)
            normed_grad[part, :] = jnp.zeros((block, width), wide_type)

    hidden = hidden_ref[...].astype(wide_type)
    square = hidden * hidden
    inner = jnp.tanh(GELU_K * hidden * (1.0 + GELU_C * square))
    half = 0.5 * (1.0 + inner)
    active = (hidden * half).astype(low_type)
    slope = half + 0.5 * hidden * (1.0 - inner * inner) * (GELU_K * (1.0 + 3.0 * GELU_C * square))
    grad = (matmul_nt(u_low[...], down_ref[...]) * slope).astype(low_type)
    down_grad_ref[...] = matmul(active.T, u_low[...]).astype(low_type)
    tick(1)
    up_grad_ref[...] = matmul(normed_turned[...], grad).astype(low_type)
    tick(2)
    normed_grad[...] += matmul_nt(grad, up_ref[...])

    @pl.when(step == last)
    def _():
        vec_grad_ref[...] = jnp.zeros_like(vec_grad_ref)

        @pl.loop(0, rows // block)
        def _(i):
            part = pl.ds(pl.multiple_of(i * block, block), block)
            center, spread = center_scale(middle_ref[part, :])
            shape = center * spread
            grads = normed_grad[part, :]
            scaled = grads * vec_ref[2:3]
            from_norm = spread * (
                scaled - jnp.mean(scaled, -1, keepdims=True) - shape * jnp.mean(scaled * shape, -1, keepdims=True))
            u_part = u_ref[part, :]
            total = from_norm + u_part
            mid_grad_ref[part, :] = total
            vec_grad_ref[0:1] += jnp.sum(grads * shape, 0, keepdims=True)
            vec_grad_ref[1:2] += jnp.sum(grads, 0, keepdims=True)
            vec_grad_ref[2:3] += jnp.sum(total, 0, keepdims=True)
            vec_grad_ref[3:4] += jnp.sum(u_part, 0, keepdims=True)
            low = total.astype(low_type)
            u_low[part, :] = low
            mixed_grad_ref[part, :] = matmul_nt(low, mix_ref[...]).astype(low_type)
            normed_turned[:, part] = mixed_ref[part, :].T
        mix_grad_ref[...] = matmul(normed_turned[...], u_low[...]).astype(low_type)


def mlp_backward(upstream, middle, mixed, weights, vec_rows, hidden, aside):
    _, w_mix, w_grow, w_shrink = weights
    rows, width = upstream.shape
    wide = hidden.shape[1]
    chunk = 256

    def whole(shape):
        return pl.BlockSpec(shape, lambda j: (0, 0), pipeline_mode=pl.Buffered(1))

    square, row_shape = (width, width), (rows, width)
    up_spec = pl.BlockSpec((width, chunk), lambda j: (0, j))
    down_spec = pl.BlockSpec((chunk, width), lambda j: (j, 0))
    return with_aside(
        mlp_back_kernel,
        aside,
        ticks=3,
        grid=(wide // chunk,),
        in_specs=[
            whole(row_shape), whole(row_shape), whole(row_shape), whole(square), up_spec, down_spec,
            whole(vec_rows.shape), pl.BlockSpec((rows, chunk), lambda j: (0, j)),
        ],
        out_specs=[up_spec, down_spec] + [
            pl.BlockSpec(s, lambda j: (0, 0)) for s in (square, row_shape, row_shape, (8, width))],
        out_shape=(
            jax.ShapeDtypeStruct((width, wide), low_type),
            jax.ShapeDtypeStruct((wide, width), low_type),
            jax.ShapeDtypeStruct(square, low_type),
            jax.ShapeDtypeStruct(row_shape, low_type),
            jax.ShapeDtypeStruct(row_shape, wide_type),
            jax.ShapeDtypeStruct((8, width), wide_type),
        ),
        scratch_shapes=[
            pltpu.VMEM(row_shape, low_type), pltpu.VMEM((width, rows), low_type), pltpu.VMEM(row_shape, wide_type)],
        cost=pl.CostEstimate(
            flops=4 * rows * width * (2 * wide + width), bytes_accessed=rows * width * 40, transcendentals=rows * wide),
        operands=(upstream, middle, mixed, w_mix, w_grow, w_shrink, vec_rows, hidden),
    )


def joined_back_kernel(
    first, normed_ref, res_ref, mid_ref, vec_ref, w_ref, q_ref, k_ref, v_ref,
    wq_ref, wk_ref, wv_ref, out_ref, vec_grad_ref, turned, grads,
):
    group, last = pl.program_id(0), pl.num_programs(0) - 1
    rows, width = res_ref.shape
    part = w_ref.shape[2] // 3
    block = 256

    @pl.when(group == 0)
    def _():
        @pl.loop(0, rows // block)
        def _(i):
            at = pl.ds(pl.multiple_of(i * block, block), block)
            turned[:, at] = normed_ref[at, :].T

    wq_ref[0] = matmul(turned[:, first:], q_ref[0]).astype(low_type)
    wk_ref[0] = matmul(turned[:, :CTX], k_ref[0]).astype(low_type)
    wv_ref[0] = matmul(turned[:, :CTX], v_ref[0]).astype(low_type)
    for start in range(0, rows, block):
        total = jnp.zeros((block, width), wide_type)
        if start >= first:
            total += matmul_nt(q_ref[0, start - first : start - first + block], w_ref[0, :, :part])
        if start < CTX:
            total += matmul_nt(k_ref[0, start : start + block], w_ref[0, :, part : 2 * part])
            total += matmul_nt(v_ref[0, start : start + block], w_ref[0, :, 2 * part :])
        at = slice(start, start + block)

        @pl.when(group == 0)
        def _():
            grads[at] = total

        @pl.when(group > 0)
        def _():
            grads[at] += total

    @pl.when(group == last)
    def _():
        vec_grad_ref[...] = jnp.zeros_like(vec_grad_ref)
        for start in range(0, rows, block):
            at = slice(start, start + block)
            center, spread = center_scale(res_ref[at])
            shape = center * spread
            here = grads[at]
            scaled = here * vec_ref[0:1]
            total = spread * (
                scaled - jnp.mean(scaled, -1, keepdims=True) - shape * jnp.mean(scaled * shape, -1, keepdims=True))
            if start >= first:
                total += mid_ref[start - first : start - first + block]
            out_ref[at] = total
            vec_grad_ref[0:1] += jnp.sum(here * shape, 0, keepdims=True)
            vec_grad_ref[1:2] += jnp.sum(here, 0, keepdims=True)


def joined_backward(first, normed, residual, grad_middle, vec_rows, w_joined, grads):
    groups, width, kinds = w_joined.shape
    rows = residual.shape[0]

    def whole(a):
        return pl.BlockSpec(a.shape, lambda g: (0, 0), pipeline_mode=pl.Buffered(1))

    def of_group(shape):
        return pl.BlockSpec((1,) + shape[1:], lambda g: (g, 0, 0))

    weight_shape = (groups, width, kinds // 3)
    return pl.pallas_call(
        functools.partial(joined_back_kernel, first),
        grid=(groups,),
        in_specs=[whole(a) for a in (normed, residual, grad_middle, vec_rows)] + [
            of_group(a.shape) for a in (w_joined,) + grads],
        out_specs=[of_group(weight_shape)] * 3 + [
            pl.BlockSpec(shape, lambda g: (0, 0)) for shape in (residual.shape, (8, width))],
        out_shape=(jax.ShapeDtypeStruct(weight_shape, low_type),) * 3 + (
            jax.ShapeDtypeStruct(residual.shape, wide_type), jax.ShapeDtypeStruct((8, width), wide_type)),
        scratch_shapes=[pltpu.VMEM((width, rows), low_type), pltpu.VMEM((rows, width), wide_type)],
        cost_estimate=pl.CostEstimate(
            flops=4 * rows * width * kinds * groups, bytes_accessed=rows * width * 30, transcendentals=rows),
        compiler_params=pltpu.CompilerParams(vmem_limit_bytes=VMEM_ALL),
    )(normed, residual, grad_middle, vec_rows, w_joined, *grads)


def layer_forward(residual, first, vec_rows, weights, bias, asides, as_rest):
    w_joined = weights[0]
    width = w_joined.shape[2] // 3
    normed = layer_norm(residual, vec_rows[0], vec_rows[1]).astype(low_type)
    queries = grouped(normed[first:], w_joined[:, :, :width]).astype(low_type)
    keys_values = grouped(normed[:CTX], w_joined[:, :, width:]).astype(low_type)
    mixed, lse, extra = attend(queries, keys_values, bias, asides[0])
    if len(weights) == 1:
        weights = weights + as_rest(extra)
    (output, middle, hidden), more = mlp_forward(residual, first, mixed, weights, vec_rows, asides[1])
    return output, weights, more, (residual, normed, queries, keys_values, mixed, lse, middle, hidden)


def layer_backward(upstream, kept, first, vec_rows, weights, bias, make_asides):
    w_joined = weights[0]
    width = w_joined.shape[2] // 3
    residual, normed, queries, keys_values, mixed, lse, middle, hidden = kept
    outs, extra = mlp_backward(upstream, middle, mixed, weights, vec_rows, hidden, make_asides(0, None, None))
    grad_grow, grad_shrink, grad_mix, grad_mixed, grad_middle, mlp_vec = outs
    grad_q, grad_k, grad_v, more = attend_back(
        queries, keys_values, bias, grad_mixed, mixed, lse, make_asides(1, (grad_mix, grad_grow, grad_shrink), extra))

    if first > 0:
        *grads_joined, grad_out, norm_vec = joined_backward(
            first, normed, residual, grad_middle, vec_rows, w_joined, (grad_q, grad_k, grad_v))
        vec_grads = [norm_vec[0], norm_vec[1], mlp_vec[0], mlp_vec[1], mlp_vec[2], mlp_vec[3]]
        return grad_out, (extra, more), tuple(grads_joined) + (grad_mix, grad_grow, grad_shrink), vec_grads

    def weight_grad(rows, grads):
        return jnp.einsum("rd,grc->gdc", rows, grads, preferred_element_type=wide_type).astype(low_type)

    def row_grad(grads, part):
        return jnp.einsum(
            "grc,gdc->rd", grads, w_joined[:, :, part * width : (part + 1) * width], preferred_element_type=wide_type)

    grads_joined = (
        weight_grad(normed[first:], grad_q), weight_grad(normed[:CTX], grad_k), weight_grad(normed[:CTX], grad_v))
    from_q = row_grad(grad_q, 0)
    from_kv = row_grad(grad_k, 1) + row_grad(grad_v, 2)
    rows = residual.shape[0]
    below = jnp.zeros((first, from_q.shape[1]), wide_type)
    tail = jnp.zeros((rows - CTX, from_q.shape[1]), wide_type)
    grad_normed = jnp.concatenate([below, from_q], 0) + jnp.concatenate([from_kv, tail], 0)
    grad_input, gain_attn, shift_attn = norm_back(residual, vec_rows[0], vec_rows[1], grad_normed)
    vec_grads = [gain_attn, shift_attn, mlp_vec[0], mlp_vec[1], mlp_vec[2], mlp_vec[3]]
    grad_out = grad_input + jnp.concatenate([below, grad_middle], 0)
    return grad_out, (extra, more), grads_joined + (grad_mix, grad_grow, grad_shrink), vec_grads


def update(weight, moment_old, average, grad_in, scale):
    applied = grad_in * scale + decay_wd * weight
    moment_new = moment * moment_old + applied
    weight_new = weight - rate * (applied + moment * moment_new)
    return (weight_new, moment_new, keep_avg * average + (1.0 - keep_avg) * weight_new)


BY_CORE = (True, True, False, False)
GATHER_ROUTES = (("zxy",), ("zyx",), ("xzy",), ("yzx",))
FORE_PACE, BACK_PACE = (1.0, 1.0), (1.0, 1.0)
BY_GRAD = (True, True, True, True, False, False)
ROUTES = (("zxy",), ("zyx",), ("zxy",), ("zyx",), ("zyx",), ("zxy",))


def whole_gather(shard_list, by_core):
    return [
        lax.all_gather(lax.all_gather(shard, "dp", axis=0), "head", axis=0 if bc else 1)
        for shard, bc in zip(shard_list, by_core)]


def as_blocks(grads, by_core, rows_list, routes):
    chips, cores = lax.axis_size("dp"), lax.axis_size("head")
    return [
        grad.reshape(((cores, chips) if bc else (chips, cores)) + (len(route), rows // len(route), -1))
        for grad, bc, rows, route in zip(grads, by_core, rows_list, routes)]


def whole_scatter(grads, by_core, rows_list):
    outs = []
    for grad, bc in zip(as_blocks(grads, by_core, rows_list, ROUTES), by_core):
        half = lax.psum_scatter(grad.astype(wide_type), "head", scatter_dimension=0 if bc else 1)
        outs.append(lax.psum_scatter(half, "dp", scatter_dimension=0))
    return outs


def shards(
    rows_in, feat_mask, counts, ctx_vals, targets, query_mask,
    w_emb, m_emb, a_emb, vectors, m_vec, a_vec,
    w_qkv, m_qkv, a_qkv, w_out, m_out, a_out, w_up, m_up, a_up, w_down, m_down, a_down,
    w_head, m_head, a_head,
):
    chips, cores = lax.axis_size("dp"), lax.axis_size("head")
    direct = (chips, cores) == (16, 2)
    _, row_count, feat_count = rows_in.shape
    layer_total = w_qkv.shape[0]
    width = w_emb.shape[1]
    joined_rows = w_qkv.shape[1]
    kinds = w_qkv.shape[2] * w_qkv.shape[4]

    def own_weights(at):
        return [
            w_qkv[at].reshape((joined_rows, kinds)).astype(low_type)[None],
            w_out[at, 0].astype(low_type)[None],
            w_up[at].astype(low_type)[None],
            w_down[at].astype(low_type)[None],
        ]

    def as_joined(qkv):
        return (qkv.reshape((cores, width, kinds)),)

    def as_rest(gathered):
        out, up, down = gathered
        return (out.reshape((width, width)), up.reshape((width, -1)), down.reshape((-1, width)))

    own = [own_weights(at) for at in range(layer_total)]
    forward_asides = [[None, None] for _ in own]
    if direct:
        joined = own[0][0].reshape((2, joined_rows // 2, kinds))
        weights = [as_joined(all_gather_layer([joined], (True,), (("zxy", "zyx"),), 1)[0])]
        for at, layer in enumerate(own):
            if at == 0:
                forward_asides[at][0] = Aside(
                    gather_plan(layer[1:], BY_CORE[1:], (("zxy",), ("xzy",), ("yzx",))), layer[1:], 2, FORE_PACE[0])
            else:
                forward_asides[at - 1][1] = Aside(
                    gather_plan(layer, BY_CORE, GATHER_ROUTES), layer, 10 + at, FORE_PACE[1])
    else:
        gathered = [whole_gather(o, BY_CORE) for o in own]
        weights = [as_joined(g[0]) + as_rest(g[1:]) for g in gathered]

    table = lax.axis_index("dp") * cores + lax.axis_index("head")
    count = lax.dynamic_slice_in_dim(counts, table, 1, 0)
    bias = jnp.where(jnp.arange(CTX) < count, 0.0, -1e30).astype(low_type)
    bias = jnp.broadcast_to(bias[:, None], (CTX, 128))
    masked = rows_in[0] * feat_mask[0][None, :].astype(low_type)
    leading = jnp.concatenate([ctx_vals[0], jnp.zeros((row_count - CTX,), wide_type)])[:, None]
    residual = matmul(masked, w_emb.astype(low_type)) + vectors[1] + leading * vectors[0]
    kept_all = []
    for at in range(layer_total):
        first = CTX if at == layer_total - 1 else 0
        residual, weights[at], extra, kept = layer_forward(
            residual, first, vectors[2 + 6 * at : 8 + 6 * at], weights[at], bias, forward_asides[at], as_rest)
        if extra is not None:
            weights.append(as_joined(extra[0]) + as_rest(extra[1:]))
        kept_all.append(kept)

    head_low = w_head.astype(low_type)
    final_rows = layer_norm(residual, vectors[-2], vectors[-1]).astype(low_type)
    logits = matmul(final_rows, head_low)
    row_peak = jnp.max(logits, -1, keepdims=True)
    log_total = row_peak[:, 0] + jnp.log(jnp.sum(jnp.exp(logits - row_peak), -1))
    target_hit = (jnp.arange(logits.shape[1])[None, :] == targets[0][:, None]).astype(wide_type)
    picked = jnp.sum(logits * target_hit, -1)
    row_weight = query_mask[0].astype(wide_type)
    loss_part = jnp.sum((log_total - picked) * row_weight)
    grad_logits = ((jnp.exp(logits - log_total[:, None]) - target_hit) * row_weight[:, None]).astype(low_type)
    grad_head = matmul_tn(final_rows, grad_logits).astype(low_type)
    upstream, gain_final, shift_final = norm_back(
        residual, vectors[-2], vectors[-1], matmul_nt(grad_logits, head_low))

    devices = chips * cores
    rows_list = [joined_rows] * 3 + [w_out.shape[2], w_up.shape[1], w_down.shape[1]]
    sums = [None] * layer_total
    vec_grads = [None] * layer_total
    squares = []
    big = None
    for at in reversed(range(layer_total)):
        first = CTX if at == layer_total - 1 else 0
        above = big

        def make_asides(turn, ready, earlier):
            if not direct or above is None:
                return None
            if turn == 0:
                blocks = as_blocks(
                    list(above) + [grad_head], BY_GRAD + (False,), rows_list + [w_head.shape[0] // devices],
                    ROUTES + (("zyx",),))
                plan, operands = reduce_plan(
                    blocks, BY_GRAD + ("group",), ROUTES + (("zyx",),), ((4, 5), (0, 1, 2), (3, 6)))
                return Aside(plan, operands, 3, BACK_PACE[0])
            blocks = as_blocks(ready, BY_GRAD[3:], rows_list[3:], ROUTES[3:])
            plan, operands = reduce_plan(blocks, BY_GRAD[3:], ROUTES[3:], ((1, 2), (0,)))
            head_sum = [earlier[6][0].astype(low_type)]
            return Aside(Both(plan, spread_plan(head_sum)), operands + head_sum, 7, BACK_PACE[1])

        upstream, extra, big, vec_grads[at] = layer_backward(
            upstream, kept_all[at], first, vectors[2 + 6 * at : 8 + 6 * at], weights[at], bias, make_asides)
        if not direct:
            sums[at] = whole_scatter(big, BY_GRAD, rows_list)
        elif extra[0] is not None:
            sums[at + 1] = list(extra[0][:6])
            sums[at] = list(extra[1][:3])
            squares += [extra[0][7], extra[1][3]]
            head_all = extra[1][4]
    grad_emb = matmul_tn(masked, upstream.astype(low_type))
    vec_list = [jnp.sum(upstream * leading, 0), jnp.sum(upstream, 0)]
    for at in range(layer_total):
        vec_list = vec_list + vec_grads[at]
    grad_vec = jnp.stack(vec_list + [gain_final, shift_final])

    scalars = [loss_part, jnp.sum(row_weight)]
    if direct:
        feats, vec_total = w_emb.shape[0], vectors.shape[0]
        n_small = -(-(feats + vec_total) // (8 * devices)) * 8
        small = jnp.concatenate([grad_emb, grad_vec], 0).astype(low_type)
        small = jnp.pad(small, ((0, n_small * devices - feats - vec_total), (0, 0)))
        kinds_last, routes = BY_GRAD[:3] + ("group",), ROUTES[:3] + (("zyx",),)
        blocks = as_blocks(list(big[:3]) + [small], BY_GRAD[:3] + (False,), rows_list[:3] + [n_small], routes)
        *joined_sums, small_sum, square = reduce_scatter_layer(blocks, kinds_last, routes, ((0, 1), (2, 3)), 4)
        sums[0] = joined_sums + sums[0]
        scalars = jnp.stack([jnp.sum(sum(squares + [square]))] + scalars)
        scalars = jnp.broadcast_to(jnp.pad(scalars, (0, 125))[None], (8, 128))
        last_parts = [small_sum[0].astype(low_type), scalars]
        small_all, totals = exchange(spread_plan(last_parts), last_parts, 5)
        small_all = small_all.reshape((devices * n_small, width)).astype(wide_type)
        totals = jnp.sum(totals[..., 0, :3].reshape((devices, 3)), 0)
        grad_emb, grad_vec = small_all[:feats], small_all[feats : feats + vec_total]
        grad_head = head_all.reshape(w_head.shape).astype(wide_type)
    else:
        names = ("dp", "head")
        square = sum(jnp.sum(p * p) for ps in sums for p in ps)
        totals = lax.psum(jnp.stack([square] + scalars), names)
        grad_head = lax.psum(grad_head.astype(wide_type), names)
        grad_emb, grad_vec = lax.psum(grad_emb, names), lax.psum(grad_vec, names)
        alike = sum(jnp.sum(g * g) for g in (grad_head, grad_emb, grad_vec))
        totals = jnp.stack([totals[0] + alike, totals[1], totals[2]])
    pooled = totals[2]
    loss = totals[1] / pooled
    grad_norm = jnp.sqrt(totals[0]) / pooled
    scale = jnp.minimum(1.0, clip_at / grad_norm) / pooled

    def joined_update(weight, moment_old, average):
        grad = jnp.stack([jnp.stack([p.reshape((joined_rows, -1)) for p in sums[at][:3]], 1) for at in range(layer_total)])
        flat = [a.reshape((-1, 128)) for a in (weight, moment_old, average, grad)]
        return [a.reshape(weight.shape) for a in update(*flat, scale)]

    def big_update(weight, moment_old, average, kind):
        grad = jnp.stack([sums[at][kind].reshape(weight.shape[1:]) for at in range(layer_total)])
        return update(weight, moment_old, average, grad, scale)

    e_w, e_m, e_a = update(w_emb, m_emb, a_emb, grad_emb, scale)
    v_w, v_m, v_a = update(vectors, m_vec, a_vec, grad_vec, scale)
    q_w, q_m, q_a = joined_update(w_qkv, m_qkv, a_qkv)
    o_w, o_m, o_a = big_update(w_out, m_out, a_out, 3)
    u_w, u_m, u_a = big_update(w_up, m_up, a_up, 4)
    d_w, d_m, d_a = big_update(w_down, m_down, a_down, 5)
    h_w, h_m, h_a = update(w_head, m_head, a_head, grad_head, scale)
    return (
        loss, grad_norm, e_w, e_m, e_a, v_w, v_m, v_a, q_w, q_m, q_a, o_w, o_m, o_a,
        u_w, u_m, u_a, d_w, d_m, d_a, h_w, h_m, h_a,
    )


def solution(mesh):
    tables = [P(("dp", "head"), None, None)] + [P(("dp", "head"), None)] + [P()] + [P(("dp", "head"), None)] * 3
    joined = P(None, "dp", None, "head", None)
    mixed = P(None, "head", "dp", None)
    wide = P(None, ("dp", "head"), None)
    state = [P()] * 6 + [joined] * 3 + [mixed] * 3 + [wide] * 6 + [P()] * 3
    return jax.shard_map(
        shards, mesh=mesh, in_specs=tuple(tables + state), out_specs=tuple([P(), P()] + state), check_vma=False)
```
